256 devices in a mesh: sector: 4 (over x_lo, core), tile: 64 (over x_hi, z, y).
Axes of the slice: x: 4 (x_hi: 2, x_lo: 2; x = x_hi * 2 + x_lo), y: 4, z: 8, core: 2. Of those that a mesh axis runs over, the one named last changes fastest.
Arguments:
- snapshots: bfloat16 [4, 245760, 384], P(None, ('sector', 'tile')), may hold values from -6 to 6
- density: float32 [245760], P(('sector', 'tile')), may hold values from 0.5 to 2
- sound_speed: float32 [245760], P(('sector', 'tile')), may hold values from 0.5 to 2
- offsets: int32 [245760], P(('sector', 'tile')), may hold values from -32 to 32
- rotation: bfloat16 [384, 128], P('tile'), may hold values from -0.3125 to 0.3125
Outputs:
- projection: float32 [4, 384, 128], replicated
The draws below stay inside these ranges and needn't reach their ends.
All inputs are finite; a program needn't handle non-finite values.
Results may differ from the reference program's by a relative error of at most 0.0003.
Values may be sent and summed in bfloat16 or wider, within the bound.
No kernel may reach another device: no remote copies, remote signals or barrier semaphores. Data moves between devices by JAX's collectives and lax.ppermute only.
A program may use at most 64 MiB of HBM per device.

```python
import math
import jax
import jax.numpy as jnp
from jax import lax

K = 384
M = 128
CL = 960
HALO = 32
NC = 245760


def set_ends(values, own_key, smallest, top_value):
    index_at = [jax.random.randint(jax.random.fold_in(own_key, axis), (), 0, length) for axis, length in enumerate(values.shape)]
    longest = values.shape.index(max(values.shape))
    beside = index_at[:longest] + [(index_at[longest] + 1) % values.shape[longest]] + index_at[longest + 1:]
    return values.at[tuple(index_at)].set(smallest).at[tuple(beside)].set(top_value)


def level_of(rng, shape, cuts, smallest, top_value):
    def one(axis_at, shards_of):
        steps = jax.random.uniform(jax.random.fold_in(jax.random.fold_in(rng, 6), axis_at), (shards_of,), jnp.float32, smallest / len(cuts), top_value / len(cuts))
        return jnp.repeat(jnp.exp(steps), shape[axis_at] // shards_of).reshape((-1,) + (1,) * (len(shape) - axis_at - 1))

    factor_of = one(*cuts[0])
    for cut in cuts[1:]:
        factor_of = factor_of * one(*cut)
    return factor_of


def bell_draw(rng, extent, deviation, limit, split=(), held_as=jnp.bfloat16):
    level = level_of(rng, extent, split, -0.22, 0.18) if split else 1.0
    array = jax.random.normal(rng, extent, jnp.float32) * deviation * level
    return jnp.minimum(jnp.maximum(array, -limit), limit).astype(held_as)


def setup_inputs(seed: int = 0) -> dict:
    key_list = jax.random.split(jax.random.key(seed), 6)
    return {
        "snapshots": bell_draw(key_list[0], (4, NC, K), 1.0, 6.0, ((1, 256),)),
        "density": jnp.clip(jnp.exp(math.log(2.0) - 1.3862944 * jax.random.uniform(key_list[1], (NC,), jnp.float32) ** level_of(key_list[1], (NC,), ((0, 256),), -0.2, 0.2)), 0.5, 2.0),
        "sound_speed": jnp.clip(jnp.exp(math.log(2.0) - 1.3862944 * jax.random.uniform(key_list[2], (NC,), jnp.float32) ** level_of(key_list[2], (NC,), ((0, 256),), -0.2, 0.2)), 0.5, 2.0),
        "offsets": set_ends(jax.random.randint(key_list[3], (NC,), -HALO, HALO + 1), jax.random.fold_in(key_list[3], 1), -HALO, HALO).astype(jnp.int32),
        "rotation": bell_draw(key_list[4], (K, M), K ** -0.5, 0.3125, ((0, 64),)),
    }


def weighting(local_cells, near_press, near_sum, density, sound_speed):
    local_wide = local_cells.astype(jnp.float32)
    inverse = 1.0 / (density * sound_speed * sound_speed)
    vel_local = local_wide[1] + local_wide[2] + local_wide[3]
    potential = local_wide[0] * inverse + 0.5 * (near_sum - vel_local) / sound_speed
    kinetic = density[None] * local_wide[1:] + 0.5 * (near_press - local_wide[0])[None] / sound_speed[None]
    return jnp.concatenate([potential[None], kinetic], axis=0).astype(jnp.bfloat16)

def reference(snapshots, density, sound_speed, offsets, rotation):

    def block_terms(carry, first_cell):
        cell_rows = first_cell + jnp.arange(CL, dtype=jnp.int32)
        shift_rows = lax.dynamic_slice_in_dim(offsets, first_cell, CL)
        neighbor_rows = jnp.mod(cell_rows + shift_rows, NC).astype(jnp.int32)
        local_cells = lax.dynamic_slice_in_dim(snapshots, first_cell, CL, 1)
        neighbors = jnp.take(snapshots, neighbor_rows, axis=1).astype(jnp.float32)
        near_press = neighbors[0]
        near_sum = neighbors[1] + neighbors[2] + neighbors[3]
        dens_rows = lax.dynamic_slice_in_dim(density, first_cell, CL)[:, None]
        speed_rows = lax.dynamic_slice_in_dim(sound_speed, first_cell, CL)[:, None]
        weighted = weighting(local_cells, near_press, near_sum, dens_rows, speed_rows)
        mode_fields = jnp.dot(local_cells.reshape(4 * CL, K), rotation, preferred_element_type=jnp.float32)
        mode_fields = mode_fields.astype(jnp.bfloat16).reshape(4, CL, M)
        parts = [jnp.dot(weighted[component].T, mode_fields[component], preferred_element_type=jnp.float32) for component in range(4)]
        return (carry + jnp.stack(parts, axis=0), None)
    starts = jnp.arange(NC // CL, dtype=jnp.int32) * CL
    initial = jnp.zeros((4, K, M), jnp.float32)
    summed, _ = lax.scan(block_terms, initial, starts)
    return summed / math.sqrt(NC)
```

```python
import math

import jax
import jax.numpy as jnp
from jax import lax
from jax.experimental import pallas as pl
from jax.experimental.pallas import tpu as pltpu
from jax.sharding import Mesh, PartitionSpec as P

HALO = 32
COMPONENTS = 4
BLOCK = 192
TILE_AXES = ("x_hi", "z", "y")
PLANE_AXES = ("x_lo", "core", "x_hi", "y")
CELL_AXES = ("x_lo", "core", "x_hi", "z", "y")


def project_kernel(snap, low, high, dens, speed, offs, rot, out, rows_ref, weighted):
    cells = snap.shape[1]
    density = dens[...]
    sound = speed[...]
    rows_ref[...] = jnp.zeros_like(rows_ref)
    rows_ref[0:1, 0:cells] = density
    rows_ref[1:2, 0:cells] = 1.0 / (density * sound * sound)
    rows_ref[2:3, 0:cells] = 0.5 / sound
    rows_ref[3:4, 0:cells] = offs[...].astype(jnp.float32)
    columns = rows_ref[...].T
    rotation_t = rot[...].T
    window = BLOCK + 2 * HALO
    row_at = lax.broadcasted_iota(jnp.int32, (BLOCK, window), 0) + HALO
    col_at = lax.broadcasted_iota(jnp.int32, (BLOCK, window), 1)
    here = (col_at == row_at).astype(jnp.float32)
    modes = [[] for _ in range(COMPONENTS)]
    for start in range(0, cells, BLOCK):
        stop = start + BLOCK
        scale = columns[start:stop]
        rho, inverse, half = scale[:, 0:1], scale[:, 1:2], scale[:, 2:3]
        shift = scale[:, 3:4].astype(jnp.int32)
        there = (col_at == row_at + shift).astype(jnp.float32)
        stencil = (there - here).astype(jnp.bfloat16)

        def around(component):
            parts = []
            if start == 0:
                parts.append(low[component])
            parts.append(snap[component, max(start - HALO, 0) : min(stop + HALO, cells)])
            if stop == cells:
                parts.append(high[component])
            return parts[0] if len(parts) == 1 else jnp.concatenate(parts, axis=0)

        def difference(component):
            return jnp.dot(stencil, around(component), preferred_element_type=jnp.float32)

        press_part = half * difference(0)
        sum_part = half * ((difference(1) + difference(2)) + difference(3))
        for component in range(COMPONENTS):
            block = snap[component, start:stop]
            wide = block.astype(jnp.float32)
            if component == 0:
                value = wide * inverse + sum_part
            else:
                value = rho * wide + press_part
            weighted[component, start:stop] = value.astype(jnp.bfloat16)
            mode = lax.dot_general(
                rotation_t, block, (((1,), (1,)), ((), ())), preferred_element_type=jnp.float32
            )
            modes[component].append(mode.astype(jnp.bfloat16))
    for component in range(COMPONENTS):
        mode_t = jnp.concatenate(modes[component], axis=1)
        total = jnp.dot(mode_t, weighted[component], preferred_element_type=jnp.float32)
        out[component] = total.T


def local_projection(snapshots, low, high, density, sound_speed, offsets, rotation):
    components, cells, width = snapshots.shape
    modes = rotation.shape[1]
    return pl.pallas_call(
        project_kernel,
        out_shape=jax.ShapeDtypeStruct((components, width, modes), jnp.float32),
        in_specs=[pl.BlockSpec(memory_space=pltpu.VMEM)] * 7,
        out_specs=pl.BlockSpec(memory_space=pltpu.VMEM),
        scratch_shapes=[
            pltpu.VMEM((8, 1024), jnp.float32),
            pltpu.VMEM((components, cells, width), jnp.bfloat16),
        ],
        compiler_params=pltpu.CompilerParams(vmem_limit_bytes=40 << 20),
        cost_estimate=pl.CostEstimate(flops=2_000_000_000, bytes_accessed=6_000_000, transcendentals=0),
    )(
        snapshots,
        low,
        high,
        density.reshape(1, cells),
        sound_speed.reshape(1, cells),
        offsets.reshape(1, cells),
        rotation,
    )


def spread(block, axes):
    count = lax.axis_size(axes)
    return lax.all_to_all(jnp.broadcast_to(block[None], (count,) + block.shape), axes, 0, 0)


def on_device(snapshots, density, sound_speed, offsets, rotation):
    components, cells, width = snapshots.shape
    count = lax.axis_size(CELL_AXES)
    forward = [(i, (i + 1) % count) for i in range(count)]
    backward = [(i, (i - 1) % count) for i in range(count)]
    with jax.named_scope("halo"):
        low = lax.ppermute(snapshots[:, cells - HALO :], CELL_AXES, forward)
        high = lax.ppermute(snapshots[:, :HALO], CELL_AXES, backward)
    with jax.named_scope("rotation_rows"):
        full_rotation = spread(rotation, TILE_AXES).reshape(width, rotation.shape[1])
    with jax.named_scope("local_projection"):
        partial = local_projection(
            snapshots, low, high, density, sound_speed, offsets, full_rotation
        )
    modes = partial.shape[2]
    members = lax.axis_size(PLANE_AXES)
    with jax.named_scope("sum_plane"):
        pieces = partial.reshape(members, components * width // members, modes)
        piece = jnp.sum(lax.all_to_all(pieces, PLANE_AXES, 0, 0), axis=0)
    with jax.named_scope("sum_z"):
        piece = jnp.sum(spread(piece, ("z",)), axis=0)
        piece = piece * (1.0 / math.sqrt(cells * count))
    with jax.named_scope("share_plane"):
        whole = spread(piece, PLANE_AXES)
    return whole.reshape(components, width, modes)


def solution(mesh):
    fine = Mesh(mesh.devices.reshape(2, 2, 2, 8, 4), CELL_AXES)
    return jax.shard_map(
        on_device,
        mesh=fine,
        in_specs=(
            P(None, CELL_AXES, None),
            P(CELL_AXES),
            P(CELL_AXES),
            P(CELL_AXES),
            P(TILE_AXES, None),
        ),
        out_specs=P(),
        check_vma=False,
    )
```

```python
import math

import jax
import jax.numpy as jnp
from jax import lax
from jax.experimental import pallas as pl
from jax.experimental.pallas import tpu as pltpu
from jax.sharding import Mesh, PartitionSpec as P

HALO = 32
COMPONENTS = 4
BLOCK = 192
TILE_AXES = ("x_hi", "z", "y")
PLANE_AXES = ("x_lo", "x_hi", "y")
CELL_AXES = ("x_lo", "core", "x_hi", "z", "y")
VMEM = pl.BlockSpec(memory_space=pltpu.VMEM)
HBM = pl.BlockSpec(memory_space=pltpu.HBM)
PARAMS = pltpu.CompilerParams(vmem_limit_bytes=12 << 20)


def in_hbm(array):
    return pltpu.with_memory_space_constraint(array, pltpu.HBM)


def weighting_kernel(
    snap_hbm, low, high, dens_hbm, speed_hbm, offs_hbm, weighted, snap, dens, speed, offs, rows_ref, sems
):
    cells = snap.shape[1]
    vectors = ((dens_hbm, dens), (speed_hbm, speed), (offs_hbm, offs))
    small = [
        pltpu.make_async_copy(source, target, sems.at[COMPONENTS + i])
        for i, (source, target) in enumerate(vectors)
    ]
    copies = [
        pltpu.make_async_copy(snap_hbm.at[component], snap.at[component], sems.at[component])
        for component in range(COMPONENTS)
    ]
    for copy in small + copies:
        copy.start()
    for copy in small:
        copy.wait()
    density = dens[...]
    sound = speed[...]
    rows_ref[...] = jnp.zeros_like(rows_ref)
    rows_ref[0:1, 0:cells] = density
    rows_ref[1:2, 0:cells] = 1.0 / (density * sound * sound)
    rows_ref[2:3, 0:cells] = 0.5 / sound
    rows_ref[3:4, 0:cells] = offs[...].astype(jnp.float32)
    columns = rows_ref[...].T
    window = BLOCK + 2 * HALO
    row_at = lax.broadcasted_iota(jnp.int32, (BLOCK, window), 0) + HALO
    col_at = lax.broadcasted_iota(jnp.int32, (BLOCK, window), 1)
    here = (col_at == row_at).astype(jnp.float32)
    for copy in copies:
        copy.wait()
    for start in range(0, cells, BLOCK):
        stop = start + BLOCK
        scale = columns[start:stop]
        rho, inverse, half = scale[:, 0:1], scale[:, 1:2], scale[:, 2:3]
        shift = scale[:, 3:4].astype(jnp.int32)
        there = (col_at == row_at + shift).astype(jnp.float32)
        stencil = (there - here).astype(jnp.bfloat16)

        def around(component):
            parts = []
            if start == 0:
                parts.append(low[component])
            parts.append(snap[component, max(start - HALO, 0) : min(stop + HALO, cells)])
            if stop == cells:
                parts.append(high[component])
            return parts[0] if len(parts) == 1 else jnp.concatenate(parts, axis=0)

        def difference(component):
            return jnp.dot(stencil, around(component), preferred_element_type=jnp.float32)

        press_part = half * difference(0)
        sum_part = half * ((difference(1) + difference(2)) + difference(3))
        for component in range(COMPONENTS):
            wide = snap[component, start:stop].astype(jnp.float32)
            if component == 0:
                value = wide * inverse + sum_part
            else:
                value = rho * wide + press_part
            weighted[component, start:stop] = value.astype(jnp.bfloat16)


def weigh(snapshots, low, high, density, sound_speed, offsets):
    components, cells, width = snapshots.shape
    return pl.pallas_call(
        weighting_kernel,
        out_shape=jax.ShapeDtypeStruct(snapshots.shape, jnp.bfloat16),
        in_specs=[HBM, VMEM, VMEM, HBM, HBM, HBM],
        out_specs=VMEM,
        scratch_shapes=[
            pltpu.VMEM(snapshots.shape, jnp.bfloat16),
            pltpu.VMEM((1, cells), jnp.float32),
            pltpu.VMEM((1, cells), jnp.float32),
            pltpu.VMEM((1, cells), jnp.int32),
            pltpu.VMEM((8, 1024), jnp.float32),
            pltpu.SemaphoreType.DMA((components + 3,)),
        ],
        compiler_params=PARAMS,
        cost_estimate=pl.CostEstimate(flops=800_000_000, bytes_accessed=6_000_000, transcendentals=0),
    )(
        snapshots,
        low,
        high,
        in_hbm(density.reshape(1, cells)),
        in_hbm(sound_speed.reshape(1, cells)),
        in_hbm(offsets.reshape(1, cells)),
    )


def projection_kernel(snap_hbm, weighted, rot, keep, send, snap, sems):
    copies = [
        pltpu.make_async_copy(snap_hbm.at[component], snap.at[component], sems.at[component])
        for component in range(COMPONENTS)
    ]
    for copy in copies:
        copy.start()
    rotation_t = rot[...].T
    core = lax.axis_index("core")
    for component in range(COMPONENTS):
        copies[component].wait()
        mode = lax.dot_general(
            rotation_t,
            snap[component],
            (((1,), (1,)), ((), ())),
            preferred_element_type=jnp.float32,
        ).astype(jnp.bfloat16)
        total = jnp.dot(mode, weighted[component], preferred_element_type=jnp.float32).T
        owner, place = divmod(component, 2)

        @pl.when(core == owner)
        def _():
            keep[place] = total

        @pl.when(core != owner)
        def _():
            send[place] = total


def project(snapshots, weighted, rotation):
    components, cells, width = snapshots.shape
    modes = rotation.shape[1]
    half = jax.ShapeDtypeStruct((components // 2, width, modes), jnp.float32)
    return pl.pallas_call(
        projection_kernel,
        out_shape=(half, half),
        in_specs=[HBM, VMEM, VMEM],
        out_specs=(VMEM, VMEM),
        scratch_shapes=[
            pltpu.VMEM(snapshots.shape, jnp.bfloat16),
            pltpu.SemaphoreType.DMA((components,)),
        ],
        compiler_params=PARAMS,
        cost_estimate=pl.CostEstimate(flops=800_000_000, bytes_accessed=6_000_000, transcendentals=0),
    )(snapshots, weighted, rotation)


def place_kernel(mine, other, out, sems):
    core = lax.axis_index("core")
    half = mine.shape[0]
    copies = [
        pltpu.make_async_copy(mine, out.at[pl.ds(core * half, half)], sems.at[0]),
        pltpu.make_async_copy(other, out.at[pl.ds((1 - core) * half, half)], sems.at[1]),
    ]
    for copy in copies:
        copy.start()
    for copy in copies:
        copy.wait()


def place(mine, other):
    half, width, modes = mine.shape
    return pl.pallas_call(
        place_kernel,
        out_shape=jax.ShapeDtypeStruct((2 * half, width, modes), mine.dtype),
        in_specs=[VMEM, VMEM],
        out_specs=HBM,
        scratch_shapes=[pltpu.SemaphoreType.DMA((2,))],
        compiler_params=PARAMS,
    )(mine, other)


def spread(block, axes):
    count = lax.axis_size(axes)
    return lax.all_to_all(jnp.broadcast_to(block[None], (count,) + block.shape), axes, 0, 0)


def on_device(snapshots, density, sound_speed, offsets, rotation):
    components, cells, width = snapshots.shape
    count = lax.axis_size(CELL_AXES)
    resident = in_hbm(snapshots)
    forward = [(i, (i + 1) % count) for i in range(count)]
    backward = [(i, (i - 1) % count) for i in range(count)]
    swap = [(0, 1), (1, 0)]
    with jax.named_scope("halo"):
        ends = snapshots[:, cells - HALO :], snapshots[:, :HALO]
        last, first, rotation = lax.optimization_barrier((*ends, rotation))
        low = lax.ppermute(last, CELL_AXES, forward)
        high = lax.ppermute(first, CELL_AXES, backward)
    with jax.named_scope("rotation_rows"):
        full_rotation = spread(rotation, TILE_AXES).reshape(width, rotation.shape[1])
    with jax.named_scope("weighting"):
        weighted = weigh(resident, low, high, density, sound_speed, offsets)
    with jax.named_scope("projections"):
        keep, send = project(resident, weighted, full_rotation)
    modes = keep.shape[2]
    members = lax.axis_size(PLANE_AXES)
    with jax.named_scope("sum_core"):
        mine = keep + lax.ppermute(send, "core", swap)
    with jax.named_scope("sum_plane"):
        pieces = mine.reshape(members, components * width // (2 * members), modes)
        piece = jnp.sum(lax.all_to_all(pieces, PLANE_AXES, 0, 0), axis=0)
    with jax.named_scope("sum_z"):
        piece = jnp.sum(spread(piece, ("z",)), axis=0)
        piece = piece * (1.0 / math.sqrt(cells * count))
    with jax.named_scope("share_plane"):
        mine = spread(piece, PLANE_AXES).reshape(components // 2, width, modes)
    with jax.named_scope("share_core"):
        return place(mine, lax.ppermute(mine, "core", swap))


def solution(mesh):
    fine = Mesh(mesh.devices.reshape(2, 2, 2, 8, 4), CELL_AXES)
    return jax.shard_map(
        on_device,
        mesh=fine,
        in_specs=(
            P(None, CELL_AXES, None),
            P(CELL_AXES),
            P(CELL_AXES),
            P(CELL_AXES),
            P(TILE_AXES, None),
        ),
        out_specs=P(),
        check_vma=False,
    )
```

```python
import math

import jax
import jax.numpy as jnp
from jax import lax
from jax.experimental import pallas as pl
from jax.experimental.pallas import tpu as pltpu
from jax.sharding import Mesh, PartitionSpec as P

HALO = 32
COMPONENTS = 4
BLOCK = 192
PADDED = 8
WEIGHT_FLOPS = 1_000_000_000
EDGE_FLOPS = 10_000_000_000
TILE_AXES = ("x_hi", "z", "y")
PLANE_AXES = ("x_lo", "x_hi", "y")
CELL_AXES = ("x_lo", "core", "x_hi", "z", "y")
VMEM = pl.BlockSpec(memory_space=pltpu.VMEM)
HBM = pl.BlockSpec(memory_space=pltpu.HBM)
PARAMS = pltpu.CompilerParams(vmem_limit_bytes=12 << 20)


def in_hbm(array):
    return pltpu.with_memory_space_constraint(array, pltpu.HBM)


def start_kernel(snap, rot_hbm, first, last, spread_rot, rot, sems):
    cells = snap.shape[1]
    copies = [
        pltpu.make_async_copy(rot_hbm, rot, sems.at[0]),
        pltpu.make_async_copy(snap.at[:, pl.ds(0, HALO)], first, sems.at[1]),
        pltpu.make_async_copy(snap.at[:, pl.ds(cells - HALO, HALO)], last, sems.at[2]),
    ]
    for copy in copies:
        copy.start()
    copies[0].wait()
    rows = rot.shape[0]
    padding = jnp.zeros((PADDED - rows, rot.shape[1]), jnp.float32)
    block = jnp.concatenate([rot[...].astype(jnp.float32), padding], axis=0).astype(jnp.bfloat16)
    for tile in range(spread_rot.shape[0]):
        spread_rot[tile] = block
    for copy in copies[1:]:
        copy.wait()


def start(snapshots, rotation, tiles):
    components, _, width = snapshots.shape
    rows, modes = rotation.shape
    edge = jax.ShapeDtypeStruct((components, HALO, width), jnp.bfloat16)
    return pl.pallas_call(
        start_kernel,
        out_shape=(edge, edge, jax.ShapeDtypeStruct((tiles, PADDED, modes), jnp.bfloat16)),
        in_specs=[HBM, HBM],
        out_specs=(VMEM, VMEM, VMEM),
        scratch_shapes=[pltpu.VMEM((rows, modes), jnp.bfloat16), pltpu.SemaphoreType.DMA((3,))],
        compiler_params=PARAMS,
    )(snapshots, in_hbm(rotation))


def stencil_of(shift, window, offset):
    shape = (shift.shape[0], window)
    row_at = lax.broadcasted_iota(jnp.int32, shape, 0) + offset
    col_at = lax.broadcasted_iota(jnp.int32, shape, 1)
    here = (col_at == row_at).astype(jnp.float32)
    there = (col_at == row_at + shift).astype(jnp.float32)
    return (there - here).astype(jnp.bfloat16)


def weigh_rows(scale, offset, around, block):
    rho, inverse, half = scale[:, 0:1], scale[:, 1:2], scale[:, 2:3]
    stencil = stencil_of(scale[:, 3:4].astype(jnp.int32), around(0).shape[0], offset)

    def difference(component):
        return jnp.dot(stencil, around(component), preferred_element_type=jnp.float32)

    press_part = half * difference(0)
    sum_part = half * ((difference(1) + difference(2)) + difference(3))
    values = []
    for component in range(COMPONENTS):
        wide = block(component).astype(jnp.float32)
        value = wide * inverse + sum_part if component == 0 else rho * wide + press_part
        values.append(value.astype(jnp.bfloat16))
    return values


def weighting_kernel(
    snap_hbm, dens_hbm, speed_hbm, offs_hbm, weighted, edge_scale, snap, dens, speed, offs, rows_ref, sems
):
    cells = snap.shape[1]
    vectors = ((dens_hbm, dens), (speed_hbm, speed), (offs_hbm, offs))
    small = [
        pltpu.make_async_copy(source, target, sems.at[COMPONENTS + i])
        for i, (source, target) in enumerate(vectors)
    ]
    copies = [
        pltpu.make_async_copy(snap_hbm.at[component], snap.at[component], sems.at[component])
        for component in range(COMPONENTS)
    ]
    for copy in small + copies:
        copy.start()
    for copy in small:
        copy.wait()
    density = dens[...]
    sound = speed[...]
    rows_ref[...] = jnp.zeros_like(rows_ref)
    rows_ref[0:1, 0:cells] = density
    rows_ref[1:2, 0:cells] = 1.0 / (density * sound * sound)
    rows_ref[2:3, 0:cells] = 0.5 / sound
    rows_ref[3:4, 0:cells] = offs[...].astype(jnp.float32)
    columns = rows_ref[...].T
    edge_scale[0:HALO] = columns[0:HALO]
    edge_scale[HALO:] = columns[cells - HALO : cells]
    for copy in copies:
        copy.wait()
    for begin in range(0, cells, BLOCK):
        stop = begin + BLOCK
        low, high = max(begin - HALO, 0), min(stop + HALO, cells)
        values = weigh_rows(
            columns[begin:stop],
            begin - low,
            lambda component: snap[component, low:high],
            lambda component: snap[component, begin:stop],
        )
        for component in range(COMPONENTS):
            weighted[component, begin:stop] = values[component]


def weigh(snapshots, density, sound_speed, offsets):
    components, cells, width = snapshots.shape
    field = jax.ShapeDtypeStruct(snapshots.shape, jnp.bfloat16)
    return pl.pallas_call(
        weighting_kernel,
        out_shape=(field, jax.ShapeDtypeStruct((2 * HALO, 8), jnp.float32)),
        in_specs=[HBM] * 4,
        out_specs=(VMEM, VMEM),
        scratch_shapes=[
            pltpu.VMEM(snapshots.shape, jnp.bfloat16),
            pltpu.VMEM((1, cells), jnp.float32),
            pltpu.VMEM((1, cells), jnp.float32),
            pltpu.VMEM((1, cells), jnp.int32),
            pltpu.VMEM((8, 1024), jnp.float32),
            pltpu.SemaphoreType.DMA((components + 3,)),
        ],
        compiler_params=PARAMS,
        cost_estimate=pl.CostEstimate(
            flops=WEIGHT_FLOPS, bytes_accessed=6_000_000, transcendentals=0
        ),
    )(
        snapshots,
        in_hbm(density.reshape(1, cells)),
        in_hbm(sound_speed.reshape(1, cells)),
        in_hbm(offsets.reshape(1, cells)),
    )


def edge_kernel(snap_hbm, edge_scale, low, high, edges, begin, end, sems):
    cells = snap_hbm.shape[1]
    copies = [
        pltpu.make_async_copy(snap_hbm.at[:, pl.ds(0, 2 * HALO)], begin, sems.at[0]),
        pltpu.make_async_copy(snap_hbm.at[:, pl.ds(cells - 2 * HALO, 2 * HALO)], end, sems.at[1]),
    ]
    for copy in copies:
        copy.start()
    for copy in copies:
        copy.wait()
    first = weigh_rows(
        edge_scale[0:HALO],
        HALO,
        lambda component: jnp.concatenate([low[component], begin[component]], axis=0),
        lambda component: begin[component, 0:HALO],
    )
    last = weigh_rows(
        edge_scale[HALO:],
        HALO,
        lambda component: jnp.concatenate([end[component], high[component]], axis=0),
        lambda component: end[component, HALO:],
    )
    for component in range(COMPONENTS):
        edges[component, 0:HALO] = first[component]
        edges[component, HALO:] = last[component]


def weigh_edges(snapshots, edge_scale, low, high):
    components, _, width = snapshots.shape
    rim = (components, 2 * HALO, width)
    return pl.pallas_call(
        edge_kernel,
        out_shape=jax.ShapeDtypeStruct(rim, jnp.bfloat16),
        in_specs=[HBM, VMEM, VMEM, VMEM],
        out_specs=VMEM,
        scratch_shapes=[
            pltpu.VMEM(rim, jnp.bfloat16),
            pltpu.VMEM(rim, jnp.bfloat16),
            pltpu.SemaphoreType.DMA((2,)),
        ],
        compiler_params=PARAMS,
        cost_estimate=pl.CostEstimate(flops=EDGE_FLOPS, bytes_accessed=600_000, transcendentals=0),
    )(snapshots, edge_scale, low, high)


def projection_kernel(snap_hbm, weighted, edges, rot, keep, send, snap, sems):
    cells, width = snap.shape[1:]
    copies = [
        pltpu.make_async_copy(snap_hbm.at[component], snap.at[component], sems.at[component])
        for component in range(COMPONENTS)
    ]
    for copy in copies[:2]:
        copy.start()
    tiles, padded, modes = rot.shape
    rows = width // tiles
    shape = (width, tiles * padded)
    target = lax.broadcasted_iota(jnp.int32, shape, 0)
    source = lax.broadcasted_iota(jnp.int32, shape, 1)
    within = source & (padded - 1)
    tile = (source - within) // padded
    chosen = jnp.logical_and(target == tile * rows + within, within < rows)
    compact = jnp.dot(
        chosen.astype(jnp.float32).astype(jnp.bfloat16),
        rot[...].reshape(tiles * padded, modes),
        preferred_element_type=jnp.float32,
    )
    rotation_t = compact.T.astype(jnp.bfloat16)
    core = lax.axis_index("core")
    for component in range(COMPONENTS):
        copies[component].wait()
        if component + 2 < COMPONENTS:
            copies[component + 2].start()
        mode = lax.dot_general(
            rotation_t,
            snap[component],
            (((1,), (1,)), ((), ())),
            preferred_element_type=jnp.float32,
        ).astype(jnp.bfloat16)
        parts = [
            edges[component, 0:HALO],
            weighted[component, HALO : cells - HALO],
            edges[component, HALO:],
        ]
        total = jnp.dot(mode, jnp.concatenate(parts, axis=0), preferred_element_type=jnp.float32).T
        owner, place = divmod(component, 2)

        @pl.when(core == owner)
        def _():
            keep[place] = total

        @pl.when(core != owner)
        def _():
            send[place] = total


def project(snapshots, weighted, edges, rotation):
    components, _, width = snapshots.shape
    half = jax.ShapeDtypeStruct((components // 2, width, rotation.shape[2]), jnp.float32)
    return pl.pallas_call(
        projection_kernel,
        out_shape=(half, half),
        in_specs=[HBM] + [VMEM] * 3,
        out_specs=(VMEM, VMEM),
        scratch_shapes=[
            pltpu.VMEM(snapshots.shape, jnp.bfloat16),
            pltpu.SemaphoreType.DMA((components,)),
        ],
        compiler_params=PARAMS,
        cost_estimate=pl.CostEstimate(flops=800_000_000, bytes_accessed=6_000_000, transcendentals=0),
    )(snapshots, weighted, edges, rotation)


def place_kernel(mine, other, out, sems):
    core = lax.axis_index("core")
    half = mine.shape[0]
    copies = [
        pltpu.make_async_copy(mine, out.at[pl.ds(core * half, half)], sems.at[0]),
        pltpu.make_async_copy(other, out.at[pl.ds((1 - core) * half, half)], sems.at[1]),
    ]
    for copy in copies:
        copy.start()
    for copy in copies:
        copy.wait()


def place(mine, other):
    half, width, modes = mine.shape
    return pl.pallas_call(
        place_kernel,
        out_shape=jax.ShapeDtypeStruct((2 * half, width, modes), mine.dtype),
        in_specs=[VMEM, VMEM],
        out_specs=HBM,
        scratch_shapes=[pltpu.SemaphoreType.DMA((2,))],
        compiler_params=PARAMS,
    )(mine, other)


def spread(block, axes):
    count = lax.axis_size(axes)
    return lax.all_to_all(jnp.broadcast_to(block[None], (count,) + block.shape), axes, 0, 0)


def on_device(snapshots, density, sound_speed, offsets, rotation):
    components, cells, width = snapshots.shape
    count = lax.axis_size(CELL_AXES)
    resident = in_hbm(snapshots)
    forward = [(i, (i + 1) % count) for i in range(count)]
    backward = [(i, (i - 1) % count) for i in range(count)]
    swap = [(0, 1), (1, 0)]
    with jax.named_scope("start"):
        first, last, rows = start(resident, rotation, lax.axis_size(TILE_AXES))
    with jax.named_scope("halo"):
        low = lax.ppermute(last, CELL_AXES, forward)
        high = lax.ppermute(first, CELL_AXES, backward)
    with jax.named_scope("rotation_rows"):
        full_rotation = lax.all_to_all(rows, TILE_AXES, 0, 0)
    with jax.named_scope("weighting"):
        weighted, edge_scale = weigh(resident, density, sound_speed, offsets)
        edges = weigh_edges(resident, edge_scale, low, high)
    with jax.named_scope("projections"):
        keep, send = project(resident, weighted, edges, full_rotation)
    modes = keep.shape[2]
    members = lax.axis_size(PLANE_AXES)
    with jax.named_scope("sum_core"):
        mine = keep + lax.ppermute(send, "core", swap)
    with jax.named_scope("sum_plane"):
        pieces = mine.reshape(members, components * width // (2 * members), modes)
        piece = jnp.sum(lax.all_to_all(pieces, PLANE_AXES, 0, 0), axis=0)
    with jax.named_scope("sum_z"):
        piece = jnp.sum(spread(piece, ("z",)), axis=0)
        piece = piece * (1.0 / math.sqrt(cells * count))
    with jax.named_scope("share_plane"):
        mine = spread(piece, PLANE_AXES).reshape(components // 2, width, modes)
    with jax.named_scope("share_core"):
        return place(mine, lax.ppermute(mine, "core", swap))


def solution(mesh):
    fine = Mesh(mesh.devices.reshape(2, 2, 2, 8, 4), CELL_AXES)
    return jax.shard_map(
        on_device,
        mesh=fine,
        in_specs=(
            P(None, CELL_AXES, None),
            P(CELL_AXES),
            P(CELL_AXES),
            P(CELL_AXES),
            P(TILE_AXES, None),
        ),
        out_specs=P(),
        check_vma=False,
    )
```

```python
import math

import jax
import jax.numpy as jnp
from jax import lax
from jax.experimental import pallas as pl
from jax.experimental.pallas import tpu as pltpu
from jax.sharding import Mesh, PartitionSpec as P

HALO = 32
COMPONENTS = 4
BLOCK = 192
PADDED = 8
WEIGHT_FLOPS = 1_000_000_000
EDGE_FLOPS = 1_000_000_000
TILE_AXES = ("x_hi", "z", "y")
PLANE_AXES = ("x_lo", "x_hi", "y")
CELL_AXES = ("x_lo", "core", "x_hi", "z", "y")
VMEM = pl.BlockSpec(memory_space=pltpu.VMEM)
HBM = pl.BlockSpec(memory_space=pltpu.HBM)
PARAMS = pltpu.CompilerParams(vmem_limit_bytes=16 << 20)


def in_hbm(array):
    return pltpu.with_memory_space_constraint(array, pltpu.HBM)


def start_kernel(snap, rot, first, last, spread_rot, sems):
    cells = snap.shape[1]
    rows = rot.shape[0]
    copies = [
        pltpu.make_async_copy(rot, spread_rot.at[tile, pl.ds(0, rows)], sems.at[tile])
        for tile in range(spread_rot.shape[0])
    ]
    copies.append(pltpu.make_async_copy(snap.at[:, pl.ds(0, HALO)], first, sems.at[len(copies)]))
    copies.append(pltpu.make_async_copy(snap.at[:, pl.ds(cells - HALO, HALO)], last, sems.at[len(copies)]))
    for copy in copies:
        copy.start()
    for copy in copies:
        copy.wait()


def start(snapshots, rotation, tiles):
    components, _, width = snapshots.shape
    modes = rotation.shape[1]
    edge = jax.ShapeDtypeStruct((components, HALO, width), jnp.bfloat16)
    return pl.pallas_call(
        start_kernel,
        out_shape=(edge, edge, jax.ShapeDtypeStruct((tiles, PADDED, modes), jnp.bfloat16)),
        in_specs=[HBM, HBM],
        out_specs=(VMEM, VMEM, HBM),
        scratch_shapes=[pltpu.SemaphoreType.DMA((tiles + 2,))],
        compiler_params=PARAMS,
    )(snapshots, in_hbm(rotation))


def stencil_of(shift, window, offset):
    shape = (shift.shape[0], window)
    row_at = lax.broadcasted_iota(jnp.int32, shape, 0) + offset
    col_at = lax.broadcasted_iota(jnp.int32, shape, 1)
    here = (col_at == row_at).astype(jnp.float32)
    there = (col_at == row_at + shift).astype(jnp.float32)
    return (there - here).astype(jnp.bfloat16)


def weigh_rows(scale, offset, around, block):
    rho, inverse, half = scale[:, 0:1], scale[:, 1:2], scale[:, 2:3]
    stencil = stencil_of(scale[:, 3:4].astype(jnp.int32), around(0).shape[0], offset)

    def difference(component):
        return jnp.dot(stencil, around(component), preferred_element_type=jnp.float32)

    press_part = half * difference(0)
    sum_part = half * ((difference(1) + difference(2)) + difference(3))
    values = []
    for component in range(COMPONENTS):
        wide = block(component).astype(jnp.float32)
        value = wide * inverse + sum_part if component == 0 else rho * wide + press_part
        values.append(value.astype(jnp.bfloat16))
    return values


def weighting_kernel(
    snap_hbm, dens_hbm, speed_hbm, offs_hbm,
    weighted_send, snap_send, weighted_keep, edge_scale,
    snap, weighted, dens, speed, offs, rows_ref, sems,
):
    cells = snap.shape[1]
    half = COMPONENTS // 2
    sent = (1 - lax.axis_index("core")) * half
    vectors = ((dens_hbm, dens), (speed_hbm, speed), (offs_hbm, offs))
    small = [
        pltpu.make_async_copy(source, target, sems.at[COMPONENTS + i])
        for i, (source, target) in enumerate(vectors)
    ]
    copies = [
        pltpu.make_async_copy(snap_hbm.at[component], snap.at[component], sems.at[component])
        for component in range(COMPONENTS)
    ]
    for copy in small + copies:
        copy.start()
    for copy in small:
        copy.wait()
    density = dens[...]
    sound = speed[...]
    rows_ref[...] = jnp.zeros_like(rows_ref)
    rows_ref[0:1, 0:cells] = density
    rows_ref[1:2, 0:cells] = 1.0 / (density * sound * sound)
    rows_ref[2:3, 0:cells] = 0.5 / sound
    rows_ref[3:4, 0:cells] = offs[...].astype(jnp.float32)
    columns = rows_ref[...].T
    edge_scale[0:HALO] = columns[0:HALO]
    edge_scale[HALO:] = columns[cells - HALO : cells]
    for copy in copies:
        copy.wait()
    for begin in range(0, cells, BLOCK):
        stop = begin + BLOCK
        low, high = max(begin - HALO, 0), min(stop + HALO, cells)
        values = weigh_rows(
            columns[begin:stop],
            begin - low,
            lambda component: snap[component, low:high],
            lambda component: snap[component, begin:stop],
        )
        for component in range(COMPONENTS):
            weighted[component, begin:stop] = values[component]
    keep = pltpu.make_async_copy(weighted.at[pl.ds(half - sent, half)], weighted_keep, sems.at[0])
    keep.start()
    for place in range(half):
        weighted_send[place] = weighted[sent + place]
        snap_send[place] = snap[sent + place]
    keep.wait()


def weigh(snapshots, density, sound_speed, offsets):
    components, cells, width = snapshots.shape
    half = (components // 2, cells, width)
    field = jax.ShapeDtypeStruct(half, jnp.bfloat16)
    return pl.pallas_call(
        weighting_kernel,
        out_shape=(field, field, pltpu.HBM(half, jnp.bfloat16), jax.ShapeDtypeStruct((2 * HALO, 8), jnp.float32)),
        in_specs=[HBM] * 4,
        out_specs=(VMEM, VMEM, HBM, VMEM),
        scratch_shapes=[
            pltpu.VMEM(snapshots.shape, jnp.bfloat16),
            pltpu.VMEM(snapshots.shape, jnp.bfloat16),
            pltpu.VMEM((1, cells), jnp.float32),
            pltpu.VMEM((1, cells), jnp.float32),
            pltpu.VMEM((1, cells), jnp.int32),
            pltpu.VMEM((8, 1024), jnp.float32),
            pltpu.SemaphoreType.DMA((components + 3,)),
        ],
        compiler_params=PARAMS,
        cost_estimate=pl.CostEstimate(flops=WEIGHT_FLOPS, bytes_accessed=6_000_000, transcendentals=0),
    )(
        snapshots,
        in_hbm(density.reshape(1, cells)),
        in_hbm(sound_speed.reshape(1, cells)),
        in_hbm(offsets.reshape(1, cells)),
    )


def edge_kernel(snap_hbm, edge_scale, low, high, edges, begin, end, sems):
    cells = snap_hbm.shape[1]
    copies = [
        pltpu.make_async_copy(snap_hbm.at[:, pl.ds(0, 2 * HALO)], begin, sems.at[0]),
        pltpu.make_async_copy(snap_hbm.at[:, pl.ds(cells - 2 * HALO, 2 * HALO)], end, sems.at[1]),
    ]
    for copy in copies:
        copy.start()
    for copy in copies:
        copy.wait()
    first = weigh_rows(
        edge_scale[0:HALO],
        HALO,
        lambda component: jnp.concatenate([low[component], begin[component]], axis=0),
        lambda component: begin[component, 0:HALO],
    )
    last = weigh_rows(
        edge_scale[HALO:],
        HALO,
        lambda component: jnp.concatenate([end[component], high[component]], axis=0),
        lambda component: end[component, HALO:],
    )
    for component in range(COMPONENTS):
        edges[component, 0:HALO] = first[component]
        edges[component, HALO:] = last[component]


def weigh_edges(snapshots, edge_scale, low, high):
    components, _, width = snapshots.shape
    rim = (components, 2 * HALO, width)
    return pl.pallas_call(
        edge_kernel,
        out_shape=jax.ShapeDtypeStruct(rim, jnp.bfloat16),
        in_specs=[HBM, VMEM, VMEM, VMEM],
        out_specs=VMEM,
        scratch_shapes=[
            pltpu.VMEM(rim, jnp.bfloat16),
            pltpu.VMEM(rim, jnp.bfloat16),
            pltpu.SemaphoreType.DMA((2,)),
        ],
        compiler_params=PARAMS,
        cost_estimate=pl.CostEstimate(flops=EDGE_FLOPS, bytes_accessed=600_000, transcendentals=0),
    )(snapshots, edge_scale, low, high)


def totals_of(rotation_t, snap, weighted, edges):
    cells = snap.shape[0]
    mode = lax.dot_general(
        rotation_t, snap, (((1,), (1,)), ((), ())), preferred_element_type=jnp.float32
    ).astype(jnp.bfloat16)
    parts = [edges[0:HALO], weighted[HALO : cells - HALO], edges[HALO:]]
    return jnp.dot(mode, jnp.concatenate(parts, axis=0), preferred_element_type=jnp.float32).T


def sent_kernel(snap, weighted, edges, rot, send, rotation_t):
    half, _, width = snap.shape
    tiles, padded, modes = rot.shape
    rows = width // tiles
    shape = (width, tiles * padded)
    target = lax.broadcasted_iota(jnp.int32, shape, 0)
    source = lax.broadcasted_iota(jnp.int32, shape, 1)
    within = source & (padded - 1)
    tile = (source - within) // padded
    chosen = jnp.logical_and(target == tile * rows + within, within < rows)
    loaded = rot[...].reshape(tiles * padded, modes).astype(jnp.float32)
    held = lax.broadcasted_iota(jnp.int32, loaded.shape, 0) & (padded - 1)
    loaded = jnp.where(held < rows, loaded, 0.0).astype(jnp.bfloat16)
    compact = jnp.dot(
        chosen.astype(jnp.float32).astype(jnp.bfloat16), loaded, preferred_element_type=jnp.float32
    )
    turned = compact.T.astype(jnp.bfloat16)
    rotation_t[...] = turned
    sent = (1 - lax.axis_index("core")) * half
    for place in range(half):
        send[place] = totals_of(turned, snap[place], weighted[place], edges[sent + place])


def project_sent(snap, weighted, edges, rotation):
    half, _, width = snap.shape
    modes = rotation.shape[2]
    return pl.pallas_call(
        sent_kernel,
        out_shape=(
            jax.ShapeDtypeStruct((half, width, modes), jnp.float32),
            jax.ShapeDtypeStruct((modes, width), jnp.bfloat16),
        ),
        in_specs=[VMEM] * 4,
        out_specs=(VMEM, VMEM),
        compiler_params=PARAMS,
        cost_estimate=pl.CostEstimate(flops=400_000_000, bytes_accessed=3_000_000, transcendentals=0),
    )(snap, weighted, edges, rotation)


def kept_kernel(snap_hbm, weighted, edges, rotation_t, keep, snap, sems):
    half = snap.shape[0]
    kept = lax.axis_index("core") * half
    copies = [
        pltpu.make_async_copy(snap_hbm.at[kept + place], snap.at[place], sems.at[place])
        for place in range(half)
    ]
    for copy in copies:
        copy.start()
    for place in range(half):
        copies[place].wait()
        keep[place] = totals_of(rotation_t[...], snap[place], weighted[place], edges[kept + place])


def project_kept(snapshots, weighted, edges, rotation_t):
    half, cells, width = weighted.shape
    modes = rotation_t.shape[0]
    return pl.pallas_call(
        kept_kernel,
        out_shape=jax.ShapeDtypeStruct((half, width, modes), jnp.float32),
        in_specs=[HBM, VMEM, VMEM, VMEM],
        out_specs=VMEM,
        scratch_shapes=[
            pltpu.VMEM(weighted.shape, jnp.bfloat16),
            pltpu.SemaphoreType.DMA((half,)),
        ],
        compiler_params=PARAMS,
        cost_estimate=pl.CostEstimate(flops=400_000_000, bytes_accessed=6_000_000, transcendentals=0),
    )(snapshots, weighted, edges, rotation_t)


def place_own_kernel(mine, out, sem):
    half = mine.shape[0]
    copy = pltpu.make_async_copy(mine, out.at[pl.ds(lax.axis_index("core") * half, half)], sem)
    copy.start()
    copy.wait()


def place_other_kernel(begun, other, out, sem):
    half = other.shape[0]
    copy = pltpu.make_async_copy(other, out.at[pl.ds((1 - lax.axis_index("core")) * half, half)], sem)
    copy.start()
    copy.wait()


def place_own(mine):
    half, width, modes = mine.shape
    return pl.pallas_call(
        place_own_kernel,
        out_shape=jax.ShapeDtypeStruct((2 * half, width, modes), mine.dtype),
        in_specs=[VMEM],
        out_specs=HBM,
        scratch_shapes=[pltpu.SemaphoreType.DMA],
        compiler_params=PARAMS,
        cost_estimate=pl.CostEstimate(flops=0, bytes_accessed=1_000_000, transcendentals=0),
    )(mine)


def place_other(begun, other):
    return pl.pallas_call(
        place_other_kernel,
        out_shape=jax.ShapeDtypeStruct(begun.shape, begun.dtype),
        in_specs=[HBM, VMEM],
        out_specs=HBM,
        scratch_shapes=[pltpu.SemaphoreType.DMA],
        input_output_aliases={0: 0},
        compiler_params=PARAMS,
        cost_estimate=pl.CostEstimate(flops=0, bytes_accessed=1_000_000, transcendentals=0),
    )(begun, other)


def spread(block, axes):
    count = lax.axis_size(axes)
    return lax.all_to_all(jnp.broadcast_to(block[None], (count,) + block.shape), axes, 0, 0)


def on_device(snapshots, density, sound_speed, offsets, rotation):
    components, cells, width = snapshots.shape
    count = lax.axis_size(CELL_AXES)
    resident = in_hbm(snapshots)
    forward = [(i, (i + 1) % count) for i in range(count)]
    backward = [(i, (i - 1) % count) for i in range(count)]
    swap = [(0, 1), (1, 0)]
    with jax.named_scope("start"):
        first, last, rows = start(resident, rotation, lax.axis_size(TILE_AXES))
    with jax.named_scope("halo"):
        low = lax.ppermute(last, CELL_AXES, forward)
        high = lax.ppermute(first, CELL_AXES, backward)
    with jax.named_scope("rotation_rows"):
        full_rotation = lax.all_to_all(rows, TILE_AXES, 0, 0)
    with jax.named_scope("weighting"):
        weighted_send, snap_send, weighted_keep, edge_scale = weigh(
            resident, density, sound_speed, offsets
        )
        edges = weigh_edges(resident, edge_scale, low, high)
    with jax.named_scope("projections"):
        send, rotation_t = project_sent(snap_send, weighted_send, edges, full_rotation)
        received = lax.ppermute(send, "core", swap)
        keep = project_kept(resident, weighted_keep, edges, rotation_t)
        mine = keep + received
    modes = mine.shape[2]
    members = lax.axis_size(PLANE_AXES)
    with jax.named_scope("sum_plane"):
        pieces = mine.reshape(members, components * width // (2 * members), modes)
        piece = jnp.sum(lax.all_to_all(pieces, PLANE_AXES, 0, 0), axis=0)
    with jax.named_scope("sum_z"):
        piece = jnp.sum(spread(piece, ("z",)), axis=0)
        piece = piece * (1.0 / math.sqrt(cells * count))
    with jax.named_scope("share_plane"):
        mine = spread(piece, PLANE_AXES).reshape(components // 2, width, modes)
    with jax.named_scope("share_core"):
        other = lax.ppermute(mine, "core", swap)
        return place_other(place_own(mine), other)


def solution(mesh):
    fine = Mesh(mesh.devices.reshape(2, 2, 2, 8, 4), CELL_AXES)
    return jax.shard_map(
        on_device,
        mesh=fine,
        in_specs=(
            P(None, CELL_AXES, None),
            P(CELL_AXES),
            P(CELL_AXES),
            P(CELL_AXES),
            P(TILE_AXES, None),
        ),
        out_specs=P(),
        check_vma=False,
    )
```

```python
import math

import jax
import jax.numpy as jnp
from jax import lax
from jax.experimental import pallas as pl
from jax.experimental.pallas import tpu as pltpu
from jax.sharding import Mesh, PartitionSpec as P

HALO = 32
COMPONENTS = 4
BLOCK = 192
PADDED = 8
WEIGHT_FLOPS = 1_000_000_000
EDGE_FLOPS = 1_000_000_000
TILE_AXES = ("x_hi", "z", "y")
PLANE_AXES = ("x_lo", "x_hi", "y")
CELL_AXES = ("x_lo", "core", "x_hi", "z", "y")
VMEM = pl.BlockSpec(memory_space=pltpu.VMEM)
HBM = pl.BlockSpec(memory_space=pltpu.HBM)
PARAMS = pltpu.CompilerParams(vmem_limit_bytes=16 << 20)


def in_hbm(array):
    return pltpu.with_memory_space_constraint(array, pltpu.HBM)


def start_kernel(snap, rot_hbm, first, last, spread_rot, rot, sems):
    cells = snap.shape[1]
    copies = [
        pltpu.make_async_copy(rot_hbm, rot, sems.at[0]),
        pltpu.make_async_copy(snap.at[:, pl.ds(0, HALO)], first, sems.at[1]),
        pltpu.make_async_copy(snap.at[:, pl.ds(cells - HALO, HALO)], last, sems.at[2]),
    ]
    for copy in copies:
        copy.start()
    copies[0].wait()
    rows = rot.shape[0]
    padding = jnp.zeros((PADDED - rows, rot.shape[1]), jnp.float32)
    block = jnp.concatenate([rot[...].astype(jnp.float32), padding], axis=0).astype(jnp.bfloat16)
    for tile in range(spread_rot.shape[0]):
        spread_rot[tile] = block
    for copy in copies[1:]:
        copy.wait()


def start(snapshots, rotation, tiles):
    components, _, width = snapshots.shape
    rows, modes = rotation.shape
    edge = jax.ShapeDtypeStruct((components, HALO, width), jnp.bfloat16)
    return pl.pallas_call(
        start_kernel,
        out_shape=(edge, edge, jax.ShapeDtypeStruct((tiles, PADDED, modes), jnp.bfloat16)),
        in_specs=[HBM, HBM],
        out_specs=(VMEM, VMEM, VMEM),
        scratch_shapes=[pltpu.VMEM((rows, modes), jnp.bfloat16), pltpu.SemaphoreType.DMA((3,))],
        compiler_params=PARAMS,
    )(snapshots, in_hbm(rotation))


def stencil_of(shift, window, offset):
    shape = (shift.shape[0], window)
    row_at = lax.broadcasted_iota(jnp.int32, shape, 0) + offset
    col_at = lax.broadcasted_iota(jnp.int32, shape, 1)
    here = (col_at == row_at).astype(jnp.float32)
    there = (col_at == row_at + shift).astype(jnp.float32)
    return (there - here).astype(jnp.bfloat16)


def weigh_rows(scale, offset, around, block):
    rho, inverse, half = scale[:, 0:1], scale[:, 1:2], scale[:, 2:3]
    stencil = stencil_of(scale[:, 3:4].astype(jnp.int32), around(0).shape[0], offset)

    def difference(component):
        return jnp.dot(stencil, around(component), preferred_element_type=jnp.float32)

    press_part = half * difference(0)
    sum_part = half * ((difference(1) + difference(2)) + difference(3))
    values = []
    for component in range(COMPONENTS):
        wide = block(component).astype(jnp.float32)
        value = wide * inverse + sum_part if component == 0 else rho * wide + press_part
        values.append(value.astype(jnp.bfloat16))
    return values


def weighting_kernel(
    snap_hbm, dens_hbm, speed_hbm, offs_hbm,
    weighted, edge_scale, begin_rim, end_rim,
    snap, dens, speed, offs, rows_ref, sems,
):
    cells = snap.shape[1]
    starts = list(range(0, cells, BLOCK))
    bounds = [0] + [start + HALO for start in starts[1:]] + [cells]
    vectors = ((dens_hbm, dens), (speed_hbm, speed), (offs_hbm, offs))
    small = [
        pltpu.make_async_copy(source, target, sems.at[len(starts) + i])
        for i, (source, target) in enumerate(vectors)
    ]
    copies = []
    for i in range(len(starts)):
        rows = pl.ds(bounds[i], bounds[i + 1] - bounds[i])
        copies.append(pltpu.make_async_copy(snap_hbm.at[:, rows], snap.at[:, rows], sems.at[i]))
    for copy in small + copies:
        copy.start()
    for copy in small:
        copy.wait()
    density = dens[...]
    sound = speed[...]
    rows_ref[...] = jnp.zeros_like(rows_ref)
    rows_ref[0:1, 0:cells] = density
    rows_ref[1:2, 0:cells] = 1.0 / (density * sound * sound)
    rows_ref[2:3, 0:cells] = 0.5 / sound
    rows_ref[3:4, 0:cells] = offs[...].astype(jnp.float32)
    columns = rows_ref[...].T
    edge_scale[0:HALO] = columns[0:HALO]
    edge_scale[HALO:] = columns[cells - HALO : cells]
    for i, begin in enumerate(starts):
        copies[i].wait()
        stop = begin + BLOCK
        low, high = max(begin - HALO, 0), min(stop + HALO, bounds[i + 1])
        values = weigh_rows(
            columns[begin:stop],
            begin - low,
            lambda component: snap[component, low:high],
            lambda component: snap[component, begin:stop],
        )
        for component in range(COMPONENTS):
            weighted[component, begin:stop] = values[component]
    begin_rim[...] = snap[:, 0 : 2 * HALO]
    end_rim[...] = snap[:, cells - 2 * HALO :]


def weigh(snapshots, density, sound_speed, offsets):
    components, cells, width = snapshots.shape
    rim = jax.ShapeDtypeStruct((components, 2 * HALO, width), jnp.bfloat16)
    return pl.pallas_call(
        weighting_kernel,
        out_shape=(
            jax.ShapeDtypeStruct(snapshots.shape, jnp.bfloat16),
            jax.ShapeDtypeStruct((2 * HALO, 8), jnp.float32),
            rim,
            rim,
        ),
        in_specs=[HBM] * 4,
        out_specs=(VMEM,) * 4,
        scratch_shapes=[
            pltpu.VMEM(snapshots.shape, jnp.bfloat16),
            pltpu.VMEM((1, cells), jnp.float32),
            pltpu.VMEM((1, cells), jnp.float32),
            pltpu.VMEM((1, cells), jnp.int32),
            pltpu.VMEM((8, 1024), jnp.float32),
            pltpu.SemaphoreType.DMA((cells // BLOCK + 3,)),
        ],
        compiler_params=PARAMS,
        cost_estimate=pl.CostEstimate(flops=WEIGHT_FLOPS, bytes_accessed=6_000_000, transcendentals=0),
    )(
        snapshots,
        in_hbm(density.reshape(1, cells)),
        in_hbm(sound_speed.reshape(1, cells)),
        in_hbm(offsets.reshape(1, cells)),
    )


def edge_kernel(begin, end, edge_scale, low, high, edges):
    first = weigh_rows(
        edge_scale[0:HALO],
        HALO,
        lambda component: jnp.concatenate([low[component], begin[component]], axis=0),
        lambda component: begin[component, 0:HALO],
    )
    last = weigh_rows(
        edge_scale[HALO:],
        HALO,
        lambda component: jnp.concatenate([end[component], high[component]], axis=0),
        lambda component: end[component, HALO:],
    )
    for component in range(COMPONENTS):
        edges[component, 0:HALO] = first[component]
        edges[component, HALO:] = last[component]


def weigh_edges(begin, end, edge_scale, low, high):
    return pl.pallas_call(
        edge_kernel,
        out_shape=jax.ShapeDtypeStruct(begin.shape, jnp.bfloat16),
        in_specs=[VMEM] * 5,
        out_specs=VMEM,
        compiler_params=PARAMS,
        cost_estimate=pl.CostEstimate(flops=EDGE_FLOPS, bytes_accessed=600_000, transcendentals=0),
    )(begin, end, edge_scale, low, high)


def totals_of(rotation_t, snap, weighted, edges):
    cells = snap.shape[0]
    mode = lax.dot_general(
        rotation_t, snap, (((1,), (1,)), ((), ())), preferred_element_type=jnp.float32
    ).astype(jnp.bfloat16)
    parts = [edges[0:HALO], weighted[HALO : cells - HALO], edges[HALO:]]
    return jnp.dot(mode, jnp.concatenate(parts, axis=0), preferred_element_type=jnp.float32).T


def sent_kernel(snap_hbm, weighted, edges, rot, send, rotation_t, snap_keep, snap, sems):
    half, _, width = snap.shape
    kept = lax.axis_index("core") * half
    sent = half - kept
    copies = [
        pltpu.make_async_copy(snap_hbm.at[sent + place], snap.at[place], sems.at[place])
        for place in range(half)
    ]
    copies.append(pltpu.make_async_copy(snap_hbm.at[pl.ds(kept, half)], snap_keep, sems.at[half]))
    for copy in copies:
        copy.start()
    tiles, padded, modes = rot.shape
    rows = width // tiles
    shape = (width, tiles * padded)
    target = lax.broadcasted_iota(jnp.int32, shape, 0)
    source = lax.broadcasted_iota(jnp.int32, shape, 1)
    within = source & (padded - 1)
    tile = (source - within) // padded
    chosen = jnp.logical_and(target == tile * rows + within, within < rows)
    compact = jnp.dot(
        chosen.astype(jnp.float32).astype(jnp.bfloat16),
        rot[...].reshape(tiles * padded, modes),
        preferred_element_type=jnp.float32,
    )
    turned = compact.T.astype(jnp.bfloat16)
    rotation_t[...] = turned
    for place in range(half):
        copies[place].wait()
        send[place] = totals_of(turned, snap[place], weighted.at[sent + place], edges.at[sent + place])
    copies[half].wait()


def project_sent(snapshots, weighted, edges, rotation):
    components, cells, width = snapshots.shape
    half = (components // 2, cells, width)
    modes = rotation.shape[2]
    return pl.pallas_call(
        sent_kernel,
        out_shape=(
            jax.ShapeDtypeStruct((components // 2, width, modes), jnp.float32),
            jax.ShapeDtypeStruct((modes, width), jnp.bfloat16),
            jax.ShapeDtypeStruct(half, jnp.bfloat16),
        ),
        in_specs=[HBM, VMEM, VMEM, VMEM],
        out_specs=(VMEM, VMEM, VMEM),
        scratch_shapes=[
            pltpu.VMEM(half, jnp.bfloat16),
            pltpu.SemaphoreType.DMA((components // 2 + 1,)),
        ],
        compiler_params=PARAMS,
        cost_estimate=pl.CostEstimate(flops=400_000_000, bytes_accessed=3_000_000, transcendentals=0),
    )(snapshots, weighted, edges, rotation)


def kept_kernel(snap, weighted, edges, rotation_t, keep):
    half = snap.shape[0]
    kept = lax.axis_index("core") * half
    for place in range(half):
        keep[place] = totals_of(
            rotation_t[...], snap[place], weighted.at[kept + place], edges.at[kept + place]
        )


def project_kept(snap, weighted, edges, rotation_t):
    half, _, width = snap.shape
    modes = rotation_t.shape[0]
    return pl.pallas_call(
        kept_kernel,
        out_shape=jax.ShapeDtypeStruct((half, width, modes), jnp.float32),
        in_specs=[VMEM] * 4,
        out_specs=VMEM,
        compiler_params=PARAMS,
        cost_estimate=pl.CostEstimate(flops=400_000_000, bytes_accessed=3_000_000, transcendentals=0),
    )(snap, weighted, edges, rotation_t)


def place_own_kernel(mine, out, sem):
    half = mine.shape[0]
    copy = pltpu.make_async_copy(mine, out.at[pl.ds(lax.axis_index("core") * half, half)], sem)
    copy.start()
    copy.wait()


def place_other_kernel(begun, other, out, sem):
    half = other.shape[0]
    copy = pltpu.make_async_copy(other, out.at[pl.ds((1 - lax.axis_index("core")) * half, half)], sem)
    copy.start()
    copy.wait()


def place_own(mine):
    half, width, modes = mine.shape
    return pl.pallas_call(
        place_own_kernel,
        out_shape=jax.ShapeDtypeStruct((2 * half, width, modes), mine.dtype),
        in_specs=[VMEM],
        out_specs=HBM,
        scratch_shapes=[pltpu.SemaphoreType.DMA],
        compiler_params=PARAMS,
        cost_estimate=pl.CostEstimate(flops=0, bytes_accessed=1_000_000, transcendentals=0),
    )(mine)


def place_other(begun, other):
    return pl.pallas_call(
        place_other_kernel,
        out_shape=jax.ShapeDtypeStruct(begun.shape, begun.dtype),
        in_specs=[HBM, VMEM],
        out_specs=HBM,
        scratch_shapes=[pltpu.SemaphoreType.DMA],
        input_output_aliases={0: 0},
        compiler_params=PARAMS,
        cost_estimate=pl.CostEstimate(flops=0, bytes_accessed=1_000_000, transcendentals=0),
    )(begun, other)


def spread(block, axes):
    count = lax.axis_size(axes)
    return lax.all_to_all(jnp.broadcast_to(block[None], (count,) + block.shape), axes, 0, 0)


def on_device(snapshots, density, sound_speed, offsets, rotation):
    components, cells, width = snapshots.shape
    count = lax.axis_size(CELL_AXES)
    resident = in_hbm(snapshots)
    forward = [(i, (i + 1) % count) for i in range(count)]
    backward = [(i, (i - 1) % count) for i in range(count)]
    swap = [(0, 1), (1, 0)]
    with jax.named_scope("start"):
        first, last, rows = start(resident, rotation, lax.axis_size(TILE_AXES))
    with jax.named_scope("halo"):
        low = lax.ppermute(last, CELL_AXES, forward)
        high = lax.ppermute(first, CELL_AXES, backward)
    with jax.named_scope("rotation_rows"):
        full_rotation = lax.all_to_all(rows, TILE_AXES, 0, 0)
    with jax.named_scope("weighting"):
        weighted, edge_scale, begin, end = weigh(resident, density, sound_speed, offsets)
        edges = weigh_edges(begin, end, edge_scale, low, high)
    with jax.named_scope("projections"):
        send, rotation_t, snap_keep = project_sent(resident, weighted, edges, full_rotation)
        received = lax.ppermute(send, "core", swap)
        keep = project_kept(snap_keep, weighted, edges, rotation_t)
        mine = keep + received
    modes = mine.shape[2]
    members = lax.axis_size(PLANE_AXES)
    with jax.named_scope("sum_plane"):
        pieces = mine.reshape(members, components * width // (2 * members), modes)
        piece = jnp.sum(lax.all_to_all(pieces, PLANE_AXES, 0, 0), axis=0)
    with jax.named_scope("sum_z"):
        piece = jnp.sum(spread(piece, ("z",)), axis=0)
        piece = piece * (1.0 / math.sqrt(cells * count))
    with jax.named_scope("share_plane"):
        mine = spread(piece, PLANE_AXES).reshape(components // 2, width, modes)
    with jax.named_scope("share_core"):
        other = lax.ppermute(mine, "core", swap)
        return place_other(place_own(mine), other)


def solution(mesh):
    fine = Mesh(mesh.devices.reshape(2, 2, 2, 8, 4), CELL_AXES)
    return jax.shard_map(
        on_device,
        mesh=fine,
        in_specs=(
            P(None, CELL_AXES, None),
            P(CELL_AXES),
            P(CELL_AXES),
            P(CELL_AXES),
            P(TILE_AXES, None),
        ),
        out_specs=P(),
        check_vma=False,
    )
```

```python
import math

import jax
import jax.numpy as jnp
from jax import lax
from jax.experimental import pallas as pl
from jax.experimental.pallas import tpu as pltpu
from jax.sharding import Mesh, PartitionSpec as P

HALO = 32
COMPONENTS = 4
BLOCK = 192
PADDED = 8
WEIGHT_FLOPS = 1_000_000_000
EDGE_FLOPS = 1_000_000_000
TILE_AXES = ("x_hi", "z", "y")
PLANE_AXES = ("x_lo", "x_hi", "y")
CELL_AXES = ("x_lo", "core", "x_hi", "z", "y")
VMEM = pl.BlockSpec(memory_space=pltpu.VMEM)
HBM = pl.BlockSpec(memory_space=pltpu.HBM)
PARAMS = pltpu.CompilerParams(vmem_limit_bytes=16 << 20)


def in_hbm(array):
    return pltpu.with_memory_space_constraint(array, pltpu.HBM)


def start_kernel(snap, rot_hbm, first, last, spread_hbm, begin, end, rot, spread_rot, sems):
    cells = snap.shape[1]
    copies = [
        pltpu.make_async_copy(rot_hbm, rot, sems.at[0]),
        pltpu.make_async_copy(snap.at[:, pl.ds(0, HALO)], begin, sems.at[1]),
        pltpu.make_async_copy(snap.at[:, pl.ds(cells - HALO, HALO)], end, sems.at[2]),
    ]
    for copy in copies:
        copy.start()
    copies[0].wait()
    rows = rot.shape[0]
    padding = jnp.zeros((PADDED - rows, rot.shape[1]), jnp.float32)
    block = jnp.concatenate([rot[...].astype(jnp.float32), padding], axis=0).astype(jnp.bfloat16)
    for tile in range(spread_rot.shape[0]):
        spread_rot[tile] = block
    written = pltpu.make_async_copy(spread_rot, spread_hbm, sems.at[0])
    written.start()
    for copy, rim, target in ((copies[1], begin, first), (copies[2], end, last)):
        copy.wait()
        speed = [rim[component].astype(jnp.float32) for component in range(1, COMPONENTS)]
        target[0] = rim[0]
        target[1] = ((speed[0] + speed[1]) + speed[2]).astype(jnp.bfloat16)
    written.wait()


def start(snapshots, rotation, tiles):
    components, _, width = snapshots.shape
    rows, modes = rotation.shape
    edge = jax.ShapeDtypeStruct((2, HALO, width), jnp.bfloat16)
    rim = pltpu.VMEM((components, HALO, width), jnp.bfloat16)
    return pl.pallas_call(
        start_kernel,
        out_shape=(edge, edge, jax.ShapeDtypeStruct((tiles, PADDED, modes), jnp.bfloat16)),
        in_specs=[HBM, HBM],
        out_specs=(VMEM, VMEM, HBM),
        scratch_shapes=[
            rim,
            rim,
            pltpu.VMEM((rows, modes), jnp.bfloat16),
            pltpu.VMEM((tiles, PADDED, modes), jnp.bfloat16),
            pltpu.SemaphoreType.DMA((3,)),
        ],
        compiler_params=PARAMS,
    )(snapshots, in_hbm(rotation))


def stencil_of(shift, window, offset):
    shape = (shift.shape[0], window)
    row_at = lax.broadcasted_iota(jnp.int32, shape, 0) + offset
    col_at = lax.broadcasted_iota(jnp.int32, shape, 1)
    here = (col_at == row_at).astype(jnp.float32)
    there = (col_at == row_at + shift).astype(jnp.float32)
    return (there - here).astype(jnp.bfloat16)


def weigh_rows(scale, offset, around, block):
    rho, inverse, half = scale[:, 0:1], scale[:, 1:2], scale[:, 2:3]
    stencil = stencil_of(scale[:, 3:4].astype(jnp.int32), around(0).shape[0], offset)

    def difference(component):
        return jnp.dot(stencil, around(component), preferred_element_type=jnp.float32)

    press_part = half * difference(0)
    sum_part = half * ((difference(1) + difference(2)) + difference(3))
    values = []
    for component in range(COMPONENTS):
        wide = block(component).astype(jnp.float32)
        value = wide * inverse + sum_part if component == 0 else rho * wide + press_part
        values.append(value.astype(jnp.bfloat16))
    return values


def weighting_kernel(
    snap_hbm, dens_hbm, speed_hbm, offs_hbm,
    weighted, edge_scale, begin_rim, end_rim,
    snap, dens, speed, offs, rows_ref, sems,
):
    cells = snap.shape[1]
    starts = list(range(0, cells, BLOCK))
    bounds = [0] + [start + HALO for start in starts[1:]] + [cells]
    vectors = ((dens_hbm, dens), (speed_hbm, speed), (offs_hbm, offs))
    small = [
        pltpu.make_async_copy(source, target, sems.at[len(starts) + i])
        for i, (source, target) in enumerate(vectors)
    ]
    copies = []
    for i in range(len(starts)):
        rows = pl.ds(bounds[i], bounds[i + 1] - bounds[i])
        copies.append(pltpu.make_async_copy(snap_hbm.at[:, rows], snap.at[:, rows], sems.at[i]))
    for copy in small + copies:
        copy.start()
    for copy in small:
        copy.wait()
    density = dens[...]
    sound = speed[...]
    rows_ref[...] = jnp.zeros_like(rows_ref)
    rows_ref[0:1, 0:cells] = density
    rows_ref[1:2, 0:cells] = 1.0 / (density * sound * sound)
    rows_ref[2:3, 0:cells] = 0.5 / sound
    rows_ref[3:4, 0:cells] = offs[...].astype(jnp.float32)
    columns = rows_ref[...].T
    edge_scale[0:HALO] = columns[0:HALO]
    edge_scale[HALO:] = columns[cells - HALO : cells]
    for i, begin in enumerate(starts):
        copies[i].wait()
        stop = begin + BLOCK
        low, high = max(begin - HALO, 0), min(stop + HALO, bounds[i + 1])
        values = weigh_rows(
            columns[begin:stop],
            begin - low,
            lambda component: snap[component, low:high],
            lambda component: snap[component, begin:stop],
        )
        for component in range(COMPONENTS):
            weighted[component, begin:stop] = values[component]
    begin_rim[...] = snap[:, 0 : 2 * HALO]
    end_rim[...] = snap[:, cells - 2 * HALO :]


def weigh(snapshots, density, sound_speed, offsets):
    components, cells, width = snapshots.shape
    rim = jax.ShapeDtypeStruct((components, 2 * HALO, width), jnp.bfloat16)
    return pl.pallas_call(
        weighting_kernel,
        out_shape=(
            jax.ShapeDtypeStruct(snapshots.shape, jnp.bfloat16),
            jax.ShapeDtypeStruct((2 * HALO, 8), jnp.float32),
            rim,
            rim,
        ),
        in_specs=[HBM] * 4,
        out_specs=(VMEM,) * 4,
        scratch_shapes=[
            pltpu.VMEM(snapshots.shape, jnp.bfloat16),
            pltpu.VMEM((1, cells), jnp.float32),
            pltpu.VMEM((1, cells), jnp.float32),
            pltpu.VMEM((1, cells), jnp.int32),
            pltpu.VMEM((8, 1024), jnp.float32),
            pltpu.SemaphoreType.DMA((cells // BLOCK + 3,)),
        ],
        compiler_params=PARAMS,
        cost_estimate=pl.CostEstimate(flops=WEIGHT_FLOPS, bytes_accessed=6_000_000, transcendentals=0),
    )(
        snapshots,
        in_hbm(density.reshape(1, cells)),
        in_hbm(sound_speed.reshape(1, cells)),
        in_hbm(offsets.reshape(1, cells)),
    )


def edge_kernel(begin, end, edge_scale, high, low, edges):
    blank = jnp.zeros(low.shape[1:], low.dtype)

    def beyond(halo, component):
        return halo[component] if component < 2 else blank

    first = weigh_rows(
        edge_scale[0:HALO],
        HALO,
        lambda component: jnp.concatenate([beyond(low, component), begin[component]], axis=0),
        lambda component: begin[component, 0:HALO],
    )
    last = weigh_rows(
        edge_scale[HALO:],
        HALO,
        lambda component: jnp.concatenate([end[component], beyond(high, component)], axis=0),
        lambda component: end[component, HALO:],
    )
    for component in range(COMPONENTS):
        edges[component, 0:HALO] = first[component]
        edges[component, HALO:] = last[component]


def weigh_edges(begin, end, edge_scale, low, high):
    return pl.pallas_call(
        edge_kernel,
        out_shape=jax.ShapeDtypeStruct(begin.shape, jnp.bfloat16),
        in_specs=[VMEM] * 5,
        out_specs=VMEM,
        compiler_params=PARAMS,
        cost_estimate=pl.CostEstimate(flops=EDGE_FLOPS, bytes_accessed=600_000, transcendentals=0),
    )(begin, end, edge_scale, high, low)


def totals_of(rotation_t, snap, weighted, edges):
    cells = snap.shape[0]
    mode = lax.dot_general(
        rotation_t, snap, (((1,), (1,)), ((), ())), preferred_element_type=jnp.float32
    ).astype(jnp.bfloat16)
    parts = [edges[0:HALO], weighted[HALO : cells - HALO], edges[HALO:]]
    return jnp.dot(mode, jnp.concatenate(parts, axis=0), preferred_element_type=jnp.float32).T


def sent_kernel(snap_hbm, weighted, edges, rot, send, rotation_t, snap_keep, snap, sems):
    half, _, width = snap.shape
    kept = lax.axis_index("core") * half
    sent = half - kept
    copies = [
        pltpu.make_async_copy(snap_hbm.at[sent + place], snap.at[place], sems.at[place])
        for place in range(half)
    ]
    copies.append(pltpu.make_async_copy(snap_hbm.at[pl.ds(kept, half)], snap_keep, sems.at[half]))
    for copy in copies:
        copy.start()
    tiles, padded, modes = rot.shape
    rows = width // tiles
    shape = (width, tiles * padded)
    target = lax.broadcasted_iota(jnp.int32, shape, 0)
    source = lax.broadcasted_iota(jnp.int32, shape, 1)
    within = source & (padded - 1)
    tile = (source - within) // padded
    chosen = jnp.logical_and(target == tile * rows + within, within < rows)
    compact = jnp.dot(
        chosen.astype(jnp.float32).astype(jnp.bfloat16),
        rot[...].reshape(tiles * padded, modes),
        preferred_element_type=jnp.float32,
    )
    turned = compact.T.astype(jnp.bfloat16)
    rotation_t[...] = turned
    for place in range(half):
        copies[place].wait()
        send[place] = totals_of(turned, snap[place], weighted.at[sent + place], edges.at[sent + place])
    copies[half].wait()


def project_sent(snapshots, weighted, edges, rotation):
    components, cells, width = snapshots.shape
    half = (components // 2, cells, width)
    modes = rotation.shape[2]
    return pl.pallas_call(
        sent_kernel,
        out_shape=(
            jax.ShapeDtypeStruct((components // 2, width, modes), jnp.float32),
            jax.ShapeDtypeStruct((modes, width), jnp.bfloat16),
            jax.ShapeDtypeStruct(half, jnp.bfloat16),
        ),
        in_specs=[HBM, VMEM, VMEM, VMEM],
        out_specs=(VMEM, VMEM, VMEM),
        scratch_shapes=[
            pltpu.VMEM(half, jnp.bfloat16),
            pltpu.SemaphoreType.DMA((components // 2 + 1,)),
        ],
        compiler_params=PARAMS,
        cost_estimate=pl.CostEstimate(flops=400_000_000, bytes_accessed=3_000_000, transcendentals=0),
    )(snapshots, weighted, edges, rotation)


def kept_kernel(snap, weighted, edges, rotation_t, keep):
    half = snap.shape[0]
    kept = lax.axis_index("core") * half
    for place in range(half):
        keep[place] = totals_of(
            rotation_t[...], snap[place], weighted.at[kept + place], edges.at[kept + place]
        )


def project_kept(snap, weighted, edges, rotation_t):
    half, _, width = snap.shape
    modes = rotation_t.shape[0]
    return pl.pallas_call(
        kept_kernel,
        out_shape=jax.ShapeDtypeStruct((half, width, modes), jnp.float32),
        in_specs=[VMEM] * 4,
        out_specs=VMEM,
        compiler_params=PARAMS,
        cost_estimate=pl.CostEstimate(flops=400_000_000, bytes_accessed=3_000_000, transcendentals=0),
    )(snap, weighted, edges, rotation_t)


def place_own_kernel(mine, out, sem):
    half = mine.shape[0]
    copy = pltpu.make_async_copy(mine, out.at[pl.ds(lax.axis_index("core") * half, half)], sem)
    copy.start()
    copy.wait()


def place_other_kernel(begun, other, out, sem):
    half = other.shape[0]
    copy = pltpu.make_async_copy(other, out.at[pl.ds((1 - lax.axis_index("core")) * half, half)], sem)
    copy.start()
    copy.wait()


def place_own(mine):
    half, width, modes = mine.shape
    return pl.pallas_call(
        place_own_kernel,
        out_shape=jax.ShapeDtypeStruct((2 * half, width, modes), mine.dtype),
        in_specs=[VMEM],
        out_specs=HBM,
        scratch_shapes=[pltpu.SemaphoreType.DMA],
        compiler_params=PARAMS,
        cost_estimate=pl.CostEstimate(flops=0, bytes_accessed=1_000_000, transcendentals=0),
    )(mine)


def place_other(begun, other):
    return pl.pallas_call(
        place_other_kernel,
        out_shape=jax.ShapeDtypeStruct(begun.shape, begun.dtype),
        in_specs=[HBM, VMEM],
        out_specs=HBM,
        scratch_shapes=[pltpu.SemaphoreType.DMA],
        input_output_aliases={0: 0},
        compiler_params=PARAMS,
        cost_estimate=pl.CostEstimate(flops=0, bytes_accessed=1_000_000, transcendentals=0),
    )(begun, other)


def spread(block, axes):
    count = lax.axis_size(axes)
    return lax.all_to_all(jnp.broadcast_to(block[None], (count,) + block.shape), axes, 0, 0)


def on_device(snapshots, density, sound_speed, offsets, rotation):
    components, cells, width = snapshots.shape
    count = lax.axis_size(CELL_AXES)
    resident = in_hbm(snapshots)
    forward = [(i, (i + 1) % count) for i in range(count)]
    backward = [(i, (i - 1) % count) for i in range(count)]
    swap = [(0, 1), (1, 0)]
    with jax.named_scope("start"):
        first, last, rows = start(resident, rotation, lax.axis_size(TILE_AXES))
    with jax.named_scope("halo"):
        high = lax.ppermute(first, CELL_AXES, backward)
        low = lax.ppermute(last, CELL_AXES, forward)
    with jax.named_scope("rotation_rows"):
        full_rotation = lax.all_to_all(rows, TILE_AXES, 0, 0)
    with jax.named_scope("weighting"):
        weighted, edge_scale, begin, end = weigh(resident, density, sound_speed, offsets)
        edges = weigh_edges(begin, end, edge_scale, low, high)
    with jax.named_scope("projections"):
        send, rotation_t, snap_keep = project_sent(resident, weighted, edges, full_rotation)
        received = lax.ppermute(send, "core", swap)
        keep = project_kept(snap_keep, weighted, edges, rotation_t)
        mine = keep + received
    modes = mine.shape[2]
    members = lax.axis_size(PLANE_AXES)
    with jax.named_scope("sum_plane"):
        pieces = mine.reshape(members, components * width // (2 * members), modes)
        piece = jnp.sum(lax.all_to_all(pieces, PLANE_AXES, 0, 0), axis=0)
    with jax.named_scope("sum_z"):
        piece = jnp.sum(spread(piece, ("z",)), axis=0)
        piece = piece * (1.0 / math.sqrt(cells * count))
    with jax.named_scope("share_plane"):
        mine = spread(piece, PLANE_AXES).reshape(components // 2, width, modes)
    with jax.named_scope("share_core"):
        other = lax.ppermute(mine, "core", swap)
        return place_other(place_own(mine), other)


def solution(mesh):
    fine = Mesh(mesh.devices.reshape(2, 2, 2, 8, 4), CELL_AXES)
    return jax.shard_map(
        on_device,
        mesh=fine,
        in_specs=(
            P(None, CELL_AXES, None),
            P(CELL_AXES),
            P(CELL_AXES),
            P(CELL_AXES),
            P(TILE_AXES, None),
        ),
        out_specs=P(),
        check_vma=False,
    )
```

```python
import math

import jax
import jax.numpy as jnp
from jax import lax
from jax.experimental import pallas as pl
from jax.experimental.pallas import tpu as pltpu
from jax.sharding import Mesh, PartitionSpec as P

HALO = 32
COMPONENTS = 4
BLOCK = 192
PADDED = 8
WEIGHT_FLOPS = 1_000_000_000
EDGE_FLOPS = 1_000_000_000
TILE_AXES = ("x_hi", "z", "y")
PLANE_AXES = ("x_lo", "x_hi", "y")
CELL_AXES = ("x_lo", "core", "x_hi", "z", "y")
VMEM = pl.BlockSpec(memory_space=pltpu.VMEM)
HBM = pl.BlockSpec(memory_space=pltpu.HBM)
PARAMS = pltpu.CompilerParams(vmem_limit_bytes=16 << 20)


def in_hbm(array):
    return pltpu.with_memory_space_constraint(array, pltpu.HBM)


def start_kernel(snap, rot_hbm, inner, outer, spread_hbm, begin, end, rot, spread_rot, sems):
    cells = snap.shape[1]
    odd = lax.axis_index("y") % 2
    inner_at = pl.multiple_of((1 - odd) * (cells - HALO), HALO)
    outer_at = pl.multiple_of(odd * (cells - HALO), HALO)
    copies = [
        pltpu.make_async_copy(rot_hbm, rot, sems.at[0]),
        pltpu.make_async_copy(snap.at[:, pl.ds(outer_at, HALO)], begin, sems.at[1]),
        pltpu.make_async_copy(snap.at[:, pl.ds(inner_at, HALO)], end, sems.at[2]),
    ]
    for copy in copies:
        copy.start()
    copies[0].wait()
    rows = rot.shape[0]
    padding = jnp.zeros((PADDED - rows, rot.shape[1]), jnp.float32)
    block = jnp.concatenate([rot[...].astype(jnp.float32), padding], axis=0).astype(jnp.bfloat16)
    for tile in range(spread_rot.shape[0]):
        spread_rot[tile] = block
    written = pltpu.make_async_copy(spread_rot, spread_hbm, sems.at[0])
    written.start()
    for copy, rim, target in ((copies[1], begin, outer), (copies[2], end, inner)):
        copy.wait()
        speed = [rim[component].astype(jnp.float32) for component in range(1, COMPONENTS)]
        target[0] = rim[0]
        target[1] = ((speed[0] + speed[1]) + speed[2]).astype(jnp.bfloat16)
    written.wait()


def start(snapshots, rotation, tiles):
    components, _, width = snapshots.shape
    rows, modes = rotation.shape
    edge = jax.ShapeDtypeStruct((2, HALO, width), jnp.bfloat16)
    rim = pltpu.VMEM((components, HALO, width), jnp.bfloat16)
    return pl.pallas_call(
        start_kernel,
        out_shape=(edge, edge, jax.ShapeDtypeStruct((tiles, PADDED, modes), jnp.bfloat16)),
        in_specs=[HBM, HBM],
        out_specs=(VMEM, VMEM, HBM),
        scratch_shapes=[
            rim,
            rim,
            pltpu.VMEM((rows, modes), jnp.bfloat16),
            pltpu.VMEM((tiles, PADDED, modes), jnp.bfloat16),
            pltpu.SemaphoreType.DMA((3,)),
        ],
        compiler_params=PARAMS,
    )(snapshots, in_hbm(rotation))


def stencil_of(shift, window, offset):
    shape = (shift.shape[0], window)
    row_at = lax.broadcasted_iota(jnp.int32, shape, 0) + offset
    col_at = lax.broadcasted_iota(jnp.int32, shape, 1)
    here = (col_at == row_at).astype(jnp.float32)
    there = (col_at == row_at + shift).astype(jnp.float32)
    return (there - here).astype(jnp.bfloat16)


def weigh_rows(scale, offset, around, block):
    rho, inverse, half = scale[:, 0:1], scale[:, 1:2], scale[:, 2:3]
    stencil = stencil_of(scale[:, 3:4].astype(jnp.int32), around(0).shape[0], offset)

    def difference(component):
        return jnp.dot(stencil, around(component), preferred_element_type=jnp.float32)

    press_part = half * difference(0)
    sum_part = half * ((difference(1) + difference(2)) + difference(3))
    values = []
    for component in range(COMPONENTS):
        wide = block(component).astype(jnp.float32)
        value = wide * inverse + sum_part if component == 0 else rho * wide + press_part
        values.append(value.astype(jnp.bfloat16))
    return values


def weighting_kernel(
    snap_hbm, dens_hbm, speed_hbm, offs_hbm,
    weighted, edge_scale, begin_rim, end_rim,
    snap, dens, speed, offs, rows_ref, sems,
):
    cells = snap.shape[1]
    starts = list(range(0, cells, BLOCK))
    bounds = [0] + [start + HALO for start in starts[1:]] + [cells]
    vectors = ((dens_hbm, dens), (speed_hbm, speed), (offs_hbm, offs))
    small = [
        pltpu.make_async_copy(source, target, sems.at[len(starts) + i])
        for i, (source, target) in enumerate(vectors)
    ]
    copies = []
    for i in range(len(starts)):
        rows = pl.ds(bounds[i], bounds[i + 1] - bounds[i])
        copies.append(pltpu.make_async_copy(snap_hbm.at[:, rows], snap.at[:, rows], sems.at[i]))
    for copy in small + copies:
        copy.start()
    for copy in small:
        copy.wait()
    density = dens[...]
    sound = speed[...]
    rows_ref[...] = jnp.zeros_like(rows_ref)
    rows_ref[0:1, 0:cells] = density
    rows_ref[1:2, 0:cells] = 1.0 / (density * sound * sound)
    rows_ref[2:3, 0:cells] = 0.5 / sound
    rows_ref[3:4, 0:cells] = offs[...].astype(jnp.float32)
    columns = rows_ref[...].T
    edge_scale[0:HALO] = columns[0:HALO]
    edge_scale[HALO:] = columns[cells - HALO : cells]
    for i, begin in enumerate(starts):
        copies[i].wait()
        stop = begin + BLOCK
        low, high = max(begin - HALO, 0), min(stop + HALO, bounds[i + 1])
        values = weigh_rows(
            columns[begin:stop],
            begin - low,
            lambda component: snap[component, low:high],
            lambda component: snap[component, begin:stop],
        )
        for component in range(COMPONENTS):
            weighted[component, begin:stop] = values[component]
    begin_rim[...] = snap[:, 0 : 2 * HALO]
    end_rim[...] = snap[:, cells - 2 * HALO :]


def weigh(snapshots, density, sound_speed, offsets):
    components, cells, width = snapshots.shape
    rim = jax.ShapeDtypeStruct((components, 2 * HALO, width), jnp.bfloat16)
    return pl.pallas_call(
        weighting_kernel,
        out_shape=(
            jax.ShapeDtypeStruct(snapshots.shape, jnp.bfloat16),
            jax.ShapeDtypeStruct((2 * HALO, 8), jnp.float32),
            rim,
            rim,
        ),
        in_specs=[HBM] * 4,
        out_specs=(VMEM,) * 4,
        scratch_shapes=[
            pltpu.VMEM(snapshots.shape, jnp.bfloat16),
            pltpu.VMEM((1, cells), jnp.float32),
            pltpu.VMEM((1, cells), jnp.float32),
            pltpu.VMEM((1, cells), jnp.int32),
            pltpu.VMEM((8, 1024), jnp.float32),
            pltpu.SemaphoreType.DMA((cells // BLOCK + 3,)),
        ],
        compiler_params=PARAMS,
        cost_estimate=pl.CostEstimate(flops=WEIGHT_FLOPS, bytes_accessed=6_000_000, transcendentals=0),
    )(
        snapshots,
        in_hbm(density.reshape(1, cells)),
        in_hbm(sound_speed.reshape(1, cells)),
        in_hbm(offsets.reshape(1, cells)),
    )


def edge_kernel(begin, end, edge_scale, outer, inner, edges):
    odd = lax.axis_index("y") % 2
    blank = jnp.zeros(outer.shape[1:], outer.dtype)
    mask = lax.broadcast_in_dim(odd, outer.shape, ()) == 1
    low = jnp.where(mask, inner[...], outer[...])
    high = jnp.where(mask, outer[...], inner[...])

    def beyond(halo, component):
        return halo[component] if component < 2 else blank

    first = weigh_rows(
        edge_scale[0:HALO],
        HALO,
        lambda component: jnp.concatenate([beyond(low, component), begin[component]], axis=0),
        lambda component: begin[component, 0:HALO],
    )
    last = weigh_rows(
        edge_scale[HALO:],
        HALO,
        lambda component: jnp.concatenate([end[component], beyond(high, component)], axis=0),
        lambda component: end[component, HALO:],
    )
    for component in range(COMPONENTS):
        edges[component, 0:HALO] = first[component]
        edges[component, HALO:] = last[component]


def weigh_edges(begin, end, edge_scale, outer, inner):
    return pl.pallas_call(
        edge_kernel,
        out_shape=jax.ShapeDtypeStruct(begin.shape, jnp.bfloat16),
        in_specs=[VMEM] * 5,
        out_specs=VMEM,
        compiler_params=PARAMS,
        cost_estimate=pl.CostEstimate(flops=EDGE_FLOPS, bytes_accessed=600_000, transcendentals=0),
    )(begin, end, edge_scale, outer, inner)


def totals_of(rotation_t, snap, weighted, edges):
    cells = snap.shape[0]
    mode = lax.dot_general(
        rotation_t, snap, (((1,), (1,)), ((), ())), preferred_element_type=jnp.float32
    ).astype(jnp.bfloat16)
    parts = [edges[0:HALO], weighted[HALO : cells - HALO], edges[HALO:]]
    return jnp.dot(mode, jnp.concatenate(parts, axis=0), preferred_element_type=jnp.float32).T


def sent_kernel(snap_hbm, weighted, edges, rot, send, rotation_t, snap_keep, snap, sems):
    half, _, width = snap.shape
    kept = lax.axis_index("core") * half
    sent = half - kept
    copies = [
        pltpu.make_async_copy(snap_hbm.at[sent + place], snap.at[place], sems.at[place])
        for place in range(half)
    ]
    copies.append(pltpu.make_async_copy(snap_hbm.at[pl.ds(kept, half)], snap_keep, sems.at[half]))
    for copy in copies:
        copy.start()
    tiles, padded, modes = rot.shape
    rows = width // tiles
    shape = (width, tiles * padded)
    target = lax.broadcasted_iota(jnp.int32, shape, 0)
    source = lax.broadcasted_iota(jnp.int32, shape, 1)
    within = source & (padded - 1)
    tile = (source - within) // padded
    chosen = jnp.logical_and(target == tile * rows + within, within < rows)
    compact = jnp.dot(
        chosen.astype(jnp.float32).astype(jnp.bfloat16),
        rot[...].reshape(tiles * padded, modes),
        preferred_element_type=jnp.float32,
    )
    turned = compact.T.astype(jnp.bfloat16)
    rotation_t[...] = turned
    for place in range(half):
        copies[place].wait()
        send[place] = totals_of(turned, snap[place], weighted.at[sent + place], edges.at[sent + place])
    copies[half].wait()


def project_sent(snapshots, weighted, edges, rotation):
    components, cells, width = snapshots.shape
    half = (components // 2, cells, width)
    modes = rotation.shape[2]
    return pl.pallas_call(
        sent_kernel,
        out_shape=(
            jax.ShapeDtypeStruct((components // 2, width, modes), jnp.float32),
            jax.ShapeDtypeStruct((modes, width), jnp.bfloat16),
            jax.ShapeDtypeStruct(half, jnp.bfloat16),
        ),
        in_specs=[HBM, VMEM, VMEM, VMEM],
        out_specs=(VMEM, VMEM, VMEM),
        scratch_shapes=[
            pltpu.VMEM(half, jnp.bfloat16),
            pltpu.SemaphoreType.DMA((components // 2 + 1,)),
        ],
        compiler_params=PARAMS,
        cost_estimate=pl.CostEstimate(flops=400_000_000, bytes_accessed=3_000_000, transcendentals=0),
    )(snapshots, weighted, edges, rotation)


def kept_kernel(snap, weighted, edges, rotation_t, keep):
    half = snap.shape[0]
    kept = lax.axis_index("core") * half
    for place in range(half):
        keep[place] = totals_of(
            rotation_t[...], snap[place], weighted.at[kept + place], edges.at[kept + place]
        )


def project_kept(snap, weighted, edges, rotation_t):
    half, _, width = snap.shape
    modes = rotation_t.shape[0]
    return pl.pallas_call(
        kept_kernel,
        out_shape=jax.ShapeDtypeStruct((half, width, modes), jnp.float32),
        in_specs=[VMEM] * 4,
        out_specs=VMEM,
        compiler_params=PARAMS,
        cost_estimate=pl.CostEstimate(flops=400_000_000, bytes_accessed=3_000_000, transcendentals=0),
    )(snap, weighted, edges, rotation_t)


def place_own_kernel(mine, out, sem):
    half = mine.shape[0]
    copy = pltpu.make_async_copy(mine, out.at[pl.ds(lax.axis_index("core") * half, half)], sem)
    copy.start()
    copy.wait()


def place_other_kernel(begun, other, out, sem):
    half = other.shape[0]
    copy = pltpu.make_async_copy(other, out.at[pl.ds((1 - lax.axis_index("core")) * half, half)], sem)
    copy.start()
    copy.wait()


def place_own(mine):
    half, width, modes = mine.shape
    return pl.pallas_call(
        place_own_kernel,
        out_shape=jax.ShapeDtypeStruct((2 * half, width, modes), mine.dtype),
        in_specs=[VMEM],
        out_specs=HBM,
        scratch_shapes=[pltpu.SemaphoreType.DMA],
        compiler_params=PARAMS,
        cost_estimate=pl.CostEstimate(flops=0, bytes_accessed=1_000_000, transcendentals=0),
    )(mine)


def place_other(begun, other):
    return pl.pallas_call(
        place_other_kernel,
        out_shape=jax.ShapeDtypeStruct(begun.shape, begun.dtype),
        in_specs=[HBM, VMEM],
        out_specs=HBM,
        scratch_shapes=[pltpu.SemaphoreType.DMA],
        input_output_aliases={0: 0},
        compiler_params=PARAMS,
        cost_estimate=pl.CostEstimate(flops=0, bytes_accessed=1_000_000, transcendentals=0),
    )(begun, other)


def spread(block, axes):
    count = lax.axis_size(axes)
    return lax.all_to_all(jnp.broadcast_to(block[None], (count,) + block.shape), axes, 0, 0)


def on_device(snapshots, density, sound_speed, offsets, rotation):
    components, cells, width = snapshots.shape
    count = lax.axis_size(CELL_AXES)
    resident = in_hbm(snapshots)
    inside = [(i, i ^ 1) for i in range(count)]
    across = [(i, (i + 1 if i % 2 else i - 1) % count) for i in range(count)]
    swap = [(0, 1), (1, 0)]
    with jax.named_scope("start"):
        inner, outer, rows = start(resident, rotation, lax.axis_size(TILE_AXES))
    with jax.named_scope("halo"):
        outer = lax.ppermute(outer, CELL_AXES, across)
        inner = lax.ppermute(inner, CELL_AXES, inside)
    with jax.named_scope("rotation_rows"):
        full_rotation = lax.all_to_all(rows, TILE_AXES, 0, 0)
    with jax.named_scope("weighting"):
        weighted, edge_scale, begin, end = weigh(resident, density, sound_speed, offsets)
        edges = weigh_edges(begin, end, edge_scale, outer, inner)
    with jax.named_scope("projections"):
        send, rotation_t, snap_keep = project_sent(resident, weighted, edges, full_rotation)
        received = lax.ppermute(send, "core", swap)
        keep = project_kept(snap_keep, weighted, edges, rotation_t)
        mine = keep + received
    modes = mine.shape[2]
    members = lax.axis_size(PLANE_AXES)
    with jax.named_scope("sum_plane"):
        pieces = mine.reshape(members, components * width // (2 * members), modes)
        piece = jnp.sum(lax.all_to_all(pieces, PLANE_AXES, 0, 0), axis=0)
    with jax.named_scope("sum_z"):
        piece = jnp.sum(spread(piece, ("z",)), axis=0)
        piece = piece * (1.0 / math.sqrt(cells * count))
    with jax.named_scope("share_plane"):
        mine = spread(piece, PLANE_AXES).reshape(components // 2, width, modes)
    with jax.named_scope("share_core"):
        other = lax.ppermute(mine, "core", swap)
        return place_other(place_own(mine), other)


def solution(mesh):
    fine = Mesh(mesh.devices.reshape(2, 2, 2, 8, 4), CELL_AXES)
    return jax.shard_map(
        on_device,
        mesh=fine,
        in_specs=(
            P(None, CELL_AXES, None),
            P(CELL_AXES),
            P(CELL_AXES),
            P(CELL_AXES),
            P(TILE_AXES, None),
        ),
        out_specs=P(),
        check_vma=False,
    )
```

```python
import math

import jax
import jax.numpy as jnp
from jax import lax
from jax.experimental import pallas as pl
from jax.experimental.pallas import tpu as pltpu
from jax.sharding import Mesh, PartitionSpec as P

HALO = 32
COMPONENTS = 4
BLOCK = 192
PADDED = 8
WEIGHT_FLOPS = 1_000_000_000
EDGE_FLOPS = 1_000_000_000
TILE_AXES = ("x_hi", "z", "y")
SPREAD_AXES = ("z", "y", "x_hi")
PLANE_AXES = ("y", "x_lo", "x_hi")
CELL_AXES = ("x_lo", "core", "x_hi", "z", "y")
VMEM = pl.BlockSpec(memory_space=pltpu.VMEM)
HBM = pl.BlockSpec(memory_space=pltpu.HBM)
PARAMS = pltpu.CompilerParams(vmem_limit_bytes=16 << 20)


def in_hbm(array):
    return pltpu.with_memory_space_constraint(array, pltpu.HBM)


def start_kernel(snap, rot_hbm, inner, outer, spread_hbm, begin, end, rot, spread_rot, sems):
    cells = snap.shape[1]
    odd = lax.axis_index("y") % 2
    inner_at = pl.multiple_of((1 - odd) * (cells - HALO), HALO)
    outer_at = pl.multiple_of(odd * (cells - HALO), HALO)
    copies = [
        pltpu.make_async_copy(rot_hbm, rot, sems.at[0]),
        pltpu.make_async_copy(snap.at[:, pl.ds(outer_at, HALO)], begin, sems.at[1]),
        pltpu.make_async_copy(snap.at[:, pl.ds(inner_at, HALO)], end, sems.at[2]),
    ]
    for copy in copies:
        copy.start()
    copies[0].wait()
    rows = rot.shape[0]
    padding = jnp.zeros((PADDED - rows, rot.shape[1]), jnp.float32)
    block = jnp.concatenate([rot[...].astype(jnp.float32), padding], axis=0).astype(jnp.bfloat16)
    for tile in range(spread_rot.shape[0]):
        spread_rot[tile] = block
    written = pltpu.make_async_copy(spread_rot, spread_hbm, sems.at[0])
    written.start()
    for copy, rim, target in ((copies[1], begin, outer), (copies[2], end, inner)):
        copy.wait()
        speed = [rim[component].astype(jnp.float32) for component in range(1, COMPONENTS)]
        target[0] = rim[0]
        target[1] = ((speed[0] + speed[1]) + speed[2]).astype(jnp.bfloat16)
    written.wait()


def start(snapshots, rotation, tiles):
    components, _, width = snapshots.shape
    rows, modes = rotation.shape
    edge = jax.ShapeDtypeStruct((2, HALO, width), jnp.bfloat16)
    rim = pltpu.VMEM((components, HALO, width), jnp.bfloat16)
    return pl.pallas_call(
        start_kernel,
        out_shape=(edge, edge, jax.ShapeDtypeStruct((tiles, PADDED, modes), jnp.bfloat16)),
        in_specs=[HBM, HBM],
        out_specs=(VMEM, VMEM, HBM),
        scratch_shapes=[
            rim,
            rim,
            pltpu.VMEM((rows, modes), jnp.bfloat16),
            pltpu.VMEM((tiles, PADDED, modes), jnp.bfloat16),
            pltpu.SemaphoreType.DMA((3,)),
        ],
        compiler_params=PARAMS,
    )(snapshots, in_hbm(rotation))


def stencil_of(shift, window, offset):
    shape = (shift.shape[0], window)
    row_at = lax.broadcasted_iota(jnp.int32, shape, 0) + offset
    col_at = lax.broadcasted_iota(jnp.int32, shape, 1)
    here = (col_at == row_at).astype(jnp.float32)
    there = (col_at == row_at + shift).astype(jnp.float32)
    return (there - here).astype(jnp.bfloat16)


def weigh_rows(scale, offset, around, block):
    rho, inverse, half = scale[:, 0:1], scale[:, 1:2], scale[:, 2:3]
    stencil = stencil_of(scale[:, 3:4].astype(jnp.int32), around(0).shape[0], offset)

    def difference(component):
        return jnp.dot(stencil, around(component), preferred_element_type=jnp.float32)

    press_part = half * difference(0)
    sum_part = half * ((difference(1) + difference(2)) + difference(3))
    values = []
    for component in range(COMPONENTS):
        wide = block(component).astype(jnp.float32)
        value = wide * inverse + sum_part if component == 0 else rho * wide + press_part
        values.append(value.astype(jnp.bfloat16))
    return values


def weighting_kernel(
    snap_hbm, dens_hbm, speed_hbm, offs_hbm,
    weighted_send, snap_send, weighted_keep, edge_scale, begin_rim, end_rim,
    snap, weighted, dens, speed, offs, rows_ref, sems, out_sems,
):
    cells = snap.shape[1]
    half = COMPONENTS // 2
    kept = lax.axis_index("core") * half
    sent = half - kept
    starts = list(range(0, cells, BLOCK))
    bounds = [0] + [start + HALO for start in starts[1:]] + [cells]
    vectors = ((dens_hbm, dens), (speed_hbm, speed), (offs_hbm, offs))
    small = [
        pltpu.make_async_copy(source, target, sems.at[len(starts) + i])
        for i, (source, target) in enumerate(vectors)
    ]
    copies = []
    for i in range(len(starts)):
        rows = pl.ds(bounds[i], bounds[i + 1] - bounds[i])
        copies.append(pltpu.make_async_copy(snap_hbm.at[:, rows], snap.at[:, rows], sems.at[i]))
    for copy in small + copies:
        copy.start()
    for copy in small:
        copy.wait()
    density = dens[...]
    sound = speed[...]
    rows_ref[...] = jnp.zeros_like(rows_ref)
    rows_ref[0:1, 0:cells] = density
    rows_ref[1:2, 0:cells] = 1.0 / (density * sound * sound)
    rows_ref[2:3, 0:cells] = 0.5 / sound
    rows_ref[3:4, 0:cells] = offs[...].astype(jnp.float32)
    columns = rows_ref[...].T
    edge_scale[0:HALO] = columns[0:HALO]
    edge_scale[HALO:] = columns[cells - HALO : cells]
    leaving = []
    for i, begin in enumerate(starts):
        copies[i].wait()
        if i == 1:
            leaving.append(
                pltpu.make_async_copy(snap_hbm.at[pl.ds(sent, half)], snap_send, out_sems.at[2 * len(starts)])
            )
            leaving[-1].start()
        stop = begin + BLOCK
        low, high = max(begin - HALO, 0), min(stop + HALO, bounds[i + 1])
        values = weigh_rows(
            columns[begin:stop],
            begin - low,
            lambda component: snap[component, low:high],
            lambda component: snap[component, begin:stop],
        )
        for component in range(COMPONENTS):
            weighted[component, begin:stop] = values[component]
        for first, target in ((sent, weighted_send), (kept, weighted_keep)):
            rows = pl.ds(begin, BLOCK)
            leaving.append(
                pltpu.make_async_copy(
                    weighted.at[pl.ds(first, half), rows],
                    target.at[:, rows],
                    out_sems.at[2 * i + int(target is weighted_keep)],
                )
            )
            leaving[-1].start()
    begin_rim[...] = snap[:, 0 : 2 * HALO]
    end_rim[...] = snap[:, cells - 2 * HALO :]
    for copy in leaving:
        copy.wait()


def weigh(snapshots, density, sound_speed, offsets):
    components, cells, width = snapshots.shape
    half = (components // 2, cells, width)
    field = jax.ShapeDtypeStruct(half, jnp.bfloat16)
    rim = jax.ShapeDtypeStruct((components, 2 * HALO, width), jnp.bfloat16)
    return pl.pallas_call(
        weighting_kernel,
        out_shape=(
            field,
            field,
            pltpu.HBM(half, jnp.bfloat16),
            jax.ShapeDtypeStruct((2 * HALO, 8), jnp.float32),
            rim,
            rim,
        ),
        in_specs=[HBM] * 4,
        out_specs=(VMEM, VMEM, HBM, VMEM, VMEM, VMEM),
        scratch_shapes=[
            pltpu.VMEM(snapshots.shape, jnp.bfloat16),
            pltpu.VMEM(snapshots.shape, jnp.bfloat16),
            pltpu.VMEM((1, cells), jnp.float32),
            pltpu.VMEM((1, cells), jnp.float32),
            pltpu.VMEM((1, cells), jnp.int32),
            pltpu.VMEM((8, 1024), jnp.float32),
            pltpu.SemaphoreType.DMA((cells // BLOCK + 3,)),
            pltpu.SemaphoreType.DMA((2 * (cells // BLOCK) + 1,)),
        ],
        compiler_params=PARAMS,
        cost_estimate=pl.CostEstimate(flops=WEIGHT_FLOPS, bytes_accessed=6_000_000, transcendentals=0),
    )(
        snapshots,
        in_hbm(density.reshape(1, cells)),
        in_hbm(sound_speed.reshape(1, cells)),
        in_hbm(offsets.reshape(1, cells)),
    )


def edge_kernel(begin, end, edge_scale, outer, inner, edges):
    odd = lax.axis_index("y") % 2
    blank = jnp.zeros(outer.shape[1:], outer.dtype)
    mask = lax.broadcast_in_dim(odd, outer.shape, ()) == 1
    low = jnp.where(mask, inner[...], outer[...])
    high = jnp.where(mask, outer[...], inner[...])

    def beyond(halo, component):
        return halo[component] if component < 2 else blank

    first = weigh_rows(
        edge_scale[0:HALO],
        HALO,
        lambda component: jnp.concatenate([beyond(low, component), begin[component]], axis=0),
        lambda component: begin[component, 0:HALO],
    )
    last = weigh_rows(
        edge_scale[HALO:],
        HALO,
        lambda component: jnp.concatenate([end[component], beyond(high, component)], axis=0),
        lambda component: end[component, HALO:],
    )
    for component in range(COMPONENTS):
        edges[component, 0:HALO] = first[component]
        edges[component, HALO:] = last[component]


def weigh_edges(begin, end, edge_scale, outer, inner):
    return pl.pallas_call(
        edge_kernel,
        out_shape=jax.ShapeDtypeStruct(begin.shape, jnp.bfloat16),
        in_specs=[VMEM] * 5,
        out_specs=VMEM,
        compiler_params=PARAMS,
        cost_estimate=pl.CostEstimate(flops=EDGE_FLOPS, bytes_accessed=600_000, transcendentals=0),
    )(begin, end, edge_scale, outer, inner)


def totals_of(rotation_t, snap, weighted, edges):
    cells = snap.shape[0]
    mode = lax.dot_general(
        rotation_t, snap, (((1,), (1,)), ((), ())), preferred_element_type=jnp.float32
    ).astype(jnp.bfloat16)
    parts = [edges[0:HALO], weighted[HALO : cells - HALO], edges[HALO:]]
    return jnp.dot(mode, jnp.concatenate(parts, axis=0), preferred_element_type=jnp.float32).T


def sent_kernel(snap_hbm, snap, weighted, edges, rot, send, rotation_t, snap_keep, sem):
    half, _, width = snap.shape
    kept = lax.axis_index("core") * half
    sent = half - kept
    load = pltpu.make_async_copy(snap_hbm.at[pl.ds(kept, half)], snap_keep, sem)
    load.start()
    tiles, padded, modes = rot.shape
    rows = width // tiles
    shape = (width, tiles * padded)
    target = lax.broadcasted_iota(jnp.int32, shape, 0)
    source = lax.broadcasted_iota(jnp.int32, shape, 1)
    within = source & (padded - 1)
    slot = (source - within) // padded
    tile = (slot & 1) * (tiles // 2) + (slot >> 1)
    chosen = jnp.logical_and(target == tile * rows + within, within < rows)
    compact = jnp.dot(
        chosen.astype(jnp.float32).astype(jnp.bfloat16),
        rot[...].reshape(tiles * padded, modes),
        preferred_element_type=jnp.float32,
    )
    turned = compact.T.astype(jnp.bfloat16)
    rotation_t[...] = turned
    for place in range(half):
        send[place] = totals_of(turned, snap[place], weighted.at[place], edges.at[sent + place])
    load.wait()


def project_sent(snapshots, snap_send, weighted_send, edges, rotation):
    half, _, width = snap_send.shape
    modes = rotation.shape[2]
    return pl.pallas_call(
        sent_kernel,
        out_shape=(
            jax.ShapeDtypeStruct((half, width, modes), jnp.float32),
            jax.ShapeDtypeStruct((modes, width), jnp.bfloat16),
            jax.ShapeDtypeStruct(snap_send.shape, jnp.bfloat16),
        ),
        in_specs=[HBM, VMEM, VMEM, VMEM, VMEM],
        out_specs=(VMEM, VMEM, VMEM),
        scratch_shapes=[pltpu.SemaphoreType.DMA],
        compiler_params=PARAMS,
        cost_estimate=pl.CostEstimate(flops=400_000_000, bytes_accessed=3_000_000, transcendentals=0),
    )(snapshots, snap_send, weighted_send, edges, rotation)


def kept_kernel(snap, weighted, edges, rotation_t, keep):
    half = snap.shape[0]
    kept = lax.axis_index("core") * half
    for place in range(half):
        keep[place] = totals_of(
            rotation_t[...], snap[place], weighted.at[place], edges.at[kept + place]
        )


def project_kept(snap, weighted, edges, rotation_t):
    half, _, width = snap.shape
    modes = rotation_t.shape[0]
    return pl.pallas_call(
        kept_kernel,
        out_shape=jax.ShapeDtypeStruct((half, width, modes), jnp.float32),
        in_specs=[VMEM] * 4,
        out_specs=VMEM,
        compiler_params=PARAMS,
        cost_estimate=pl.CostEstimate(flops=400_000_000, bytes_accessed=3_000_000, transcendentals=0),
    )(snap, weighted, edges, rotation_t)


def place_own_kernel(mine, out, sem):
    half = mine.shape[0]
    copy = pltpu.make_async_copy(mine, out.at[pl.ds(lax.axis_index("core") * half, half)], sem)
    copy.start()
    copy.wait()


def place_other_kernel(begun, other, out, sem):
    half = other.shape[0]
    copy = pltpu.make_async_copy(other, out.at[pl.ds((1 - lax.axis_index("core")) * half, half)], sem)
    copy.start()
    copy.wait()


def place_own(mine):
    half, width, modes = mine.shape
    return pl.pallas_call(
        place_own_kernel,
        out_shape=jax.ShapeDtypeStruct((2 * half, width, modes), mine.dtype),
        in_specs=[VMEM],
        out_specs=HBM,
        scratch_shapes=[pltpu.SemaphoreType.DMA],
        compiler_params=PARAMS,
        cost_estimate=pl.CostEstimate(flops=0, bytes_accessed=1_000_000, transcendentals=0),
    )(mine)


def place_other(begun, other):
    return pl.pallas_call(
        place_other_kernel,
        out_shape=jax.ShapeDtypeStruct(begun.shape, begun.dtype),
        in_specs=[HBM, VMEM],
        out_specs=HBM,
        scratch_shapes=[pltpu.SemaphoreType.DMA],
        input_output_aliases={0: 0},
        compiler_params=PARAMS,
        cost_estimate=pl.CostEstimate(flops=0, bytes_accessed=1_000_000, transcendentals=0),
    )(begun, other)


def spread(block, axes):
    count = lax.axis_size(axes)
    return lax.all_to_all(jnp.broadcast_to(block[None], (count,) + block.shape), axes, 0, 0)


def on_device(snapshots, density, sound_speed, offsets, rotation):
    components, cells, width = snapshots.shape
    count = lax.axis_size(CELL_AXES)
    resident = in_hbm(snapshots)
    inside = [(i, i ^ 1) for i in range(count)]
    across = [(i, (i + 1 if i % 2 else i - 1) % count) for i in range(count)]
    swap = [(0, 1), (1, 0)]
    with jax.named_scope("start"):
        inner, outer, rows = start(resident, rotation, lax.axis_size(TILE_AXES))
    with jax.named_scope("halo"):
        outer = lax.ppermute(outer, CELL_AXES, across)
        inner = lax.ppermute(inner, CELL_AXES, inside)
    with jax.named_scope("rotation_rows"):
        full_rotation = lax.all_to_all(rows, SPREAD_AXES, 0, 0)
    with jax.named_scope("weighting"):
        weighted_send, snap_send, weighted_keep, edge_scale, begin, end = weigh(
            resident, density, sound_speed, offsets
        )
        edges = weigh_edges(begin, end, edge_scale, outer, inner)
    with jax.named_scope("projections"):
        send, rotation_t, snap_keep = project_sent(
            resident, snap_send, weighted_send, edges, full_rotation
        )
        received = lax.ppermute(send, "core", swap)
        keep = project_kept(snap_keep, weighted_keep, edges, rotation_t)
        mine = keep + received
    modes = mine.shape[2]
    members = lax.axis_size(PLANE_AXES)
    with jax.named_scope("sum_plane"):
        pieces = mine.reshape(members, components * width // (2 * members), modes)
        piece = jnp.sum(lax.all_to_all(pieces, PLANE_AXES, 0, 0), axis=0)
    with jax.named_scope("sum_z"):
        piece = jnp.sum(spread(piece, ("z",)), axis=0)
        piece = piece * (1.0 / math.sqrt(cells * count))
    with jax.named_scope("share_plane"):
        mine = spread(piece, PLANE_AXES).reshape(components // 2, width, modes)
    with jax.named_scope("share_core"):
        other = lax.ppermute(mine, "core", swap)
        return place_other(place_own(mine), other)


def solution(mesh):
    fine = Mesh(mesh.devices.reshape(2, 2, 2, 8, 4), CELL_AXES)
    return jax.shard_map(
        on_device,
        mesh=fine,
        in_specs=(
            P(None, CELL_AXES, None),
            P(CELL_AXES),
            P(CELL_AXES),
            P(CELL_AXES),
            P(TILE_AXES, None),
        ),
        out_specs=P(),
        check_vma=False,
    )
```

```python
import math

import jax
import jax.numpy as jnp
from jax import lax
from jax.experimental import pallas as pl
from jax.experimental.pallas import tpu as pltpu
from jax.sharding import Mesh, PartitionSpec as P

HALO = 32
COMPONENTS = 4
BLOCK = 192
PADDED = 8
WEIGHT_FLOPS = 1_000_000_000
EDGE_FLOPS = 1_000_000_000
START_BYTES = 100_000_000
TILE_AXES = ("x_hi", "z", "y")
SPREAD_AXES = ("z", "y", "x_hi")
PLANE_AXES = ("y", "x_lo", "x_hi")
CELL_AXES = ("x_lo", "core", "x_hi", "z", "y")
VMEM = pl.BlockSpec(memory_space=pltpu.VMEM)
HBM = pl.BlockSpec(memory_space=pltpu.HBM)
PARAMS = pltpu.CompilerParams(vmem_limit_bytes=16 << 20)


def in_hbm(array):
    return pltpu.with_memory_space_constraint(array, pltpu.HBM)


def start_kernel(snap, rot_hbm, inner, outer, spread_hbm, begin, end, rot, spread_rot, sems):
    cells = snap.shape[1]
    odd = lax.axis_index("y") % 2
    inner_at = pl.multiple_of((1 - odd) * (cells - HALO), HALO)
    outer_at = pl.multiple_of(odd * (cells - HALO), HALO)
    copies = [
        pltpu.make_async_copy(rot_hbm, rot, sems.at[0]),
        pltpu.make_async_copy(snap.at[:, pl.ds(outer_at, HALO)], begin, sems.at[1]),
        pltpu.make_async_copy(snap.at[:, pl.ds(inner_at, HALO)], end, sems.at[2]),
    ]
    for copy in copies:
        copy.start()
    copies[0].wait()
    rows = rot.shape[0]
    padding = jnp.zeros((PADDED - rows, rot.shape[1]), jnp.float32)
    block = jnp.concatenate([rot[...].astype(jnp.float32), padding], axis=0).astype(jnp.bfloat16)
    for tile in range(spread_rot.shape[0]):
        spread_rot[tile] = block
    written = pltpu.make_async_copy(spread_rot, spread_hbm, sems.at[0])
    written.start()
    for copy, rim, target in ((copies[1], begin, outer), (copies[2], end, inner)):
        copy.wait()
        speed = [rim[component].astype(jnp.float32) for component in range(1, COMPONENTS)]
        target[0] = rim[0]
        target[1] = ((speed[0] + speed[1]) + speed[2]).astype(jnp.bfloat16)
    written.wait()


def start(snapshots, rotation, tiles):
    components, _, width = snapshots.shape
    rows, modes = rotation.shape
    edge = jax.ShapeDtypeStruct((2, HALO, width), jnp.bfloat16)
    rim = pltpu.VMEM((components, HALO, width), jnp.bfloat16)
    return pl.pallas_call(
        start_kernel,
        out_shape=(edge, edge, jax.ShapeDtypeStruct((tiles, PADDED, modes), jnp.bfloat16)),
        in_specs=[HBM, HBM],
        out_specs=(VMEM, VMEM, HBM),
        scratch_shapes=[
            rim,
            rim,
            pltpu.VMEM((rows, modes), jnp.bfloat16),
            pltpu.VMEM((tiles, PADDED, modes), jnp.bfloat16),
            pltpu.SemaphoreType.DMA((3,)),
        ],
        compiler_params=PARAMS,
        cost_estimate=pl.CostEstimate(flops=0, bytes_accessed=START_BYTES, transcendentals=0),
    )(snapshots, in_hbm(rotation))


def stencil_of(shift, window, offset):
    shape = (shift.shape[0], window)
    row_at = lax.broadcasted_iota(jnp.int32, shape, 0) + offset
    col_at = lax.broadcasted_iota(jnp.int32, shape, 1)
    here = (col_at == row_at).astype(jnp.float32)
    there = (col_at == row_at + shift).astype(jnp.float32)
    return (there - here).astype(jnp.bfloat16)


def weigh_rows(scale, offset, around, block):
    rho, inverse, half = scale[:, 0:1], scale[:, 1:2], scale[:, 2:3]
    stencil = stencil_of(scale[:, 3:4].astype(jnp.int32), around(0).shape[0], offset)

    def difference(component):
        return jnp.dot(stencil, around(component), preferred_element_type=jnp.float32)

    press_part = half * difference(0)
    sum_part = half * ((difference(1) + difference(2)) + difference(3))
    values = []
    for component in range(COMPONENTS):
        wide = block(component).astype(jnp.float32)
        value = wide * inverse + sum_part if component == 0 else rho * wide + press_part
        values.append(value.astype(jnp.bfloat16))
    return values


def weighting_kernel(
    snap, dens, speed, offs, weighted_hbm, edge_scale, begin_rim, end_rim, weighted, rows_ref, sems
):
    cells = snap.shape[1]
    begin_rim[...] = snap[:, 0 : 2 * HALO]
    end_rim[...] = snap[:, cells - 2 * HALO :]
    density = dens[...]
    sound = speed[...]
    rows_ref[...] = jnp.zeros_like(rows_ref)
    rows_ref[0:1, 0:cells] = density
    rows_ref[1:2, 0:cells] = 1.0 / (density * sound * sound)
    rows_ref[2:3, 0:cells] = 0.5 / sound
    rows_ref[3:4, 0:cells] = offs[...].astype(jnp.float32)
    columns = rows_ref[...].T
    edge_scale[0:HALO] = columns[0:HALO]
    edge_scale[HALO:] = columns[cells - HALO : cells]
    copies = []
    for begin in range(0, cells, BLOCK):
        stop = begin + BLOCK
        low, high = max(begin - HALO, 0), min(stop + HALO, cells)
        values = weigh_rows(
            columns[begin:stop],
            begin - low,
            lambda component: snap[component, low:high],
            lambda component: snap[component, begin:stop],
        )
        for component in range(COMPONENTS):
            weighted[component, begin:stop] = values[component]
        rows = pl.ds(begin, BLOCK)
        copies.append(
            pltpu.make_async_copy(weighted.at[:, rows], weighted_hbm.at[:, rows], sems.at[len(copies)])
        )
        copies[-1].start()
    for copy in copies:
        copy.wait()


def weigh(snapshots, density, sound_speed, offsets):
    components, cells, width = snapshots.shape
    rim = jax.ShapeDtypeStruct((components, 2 * HALO, width), jnp.bfloat16)
    return pl.pallas_call(
        weighting_kernel,
        out_shape=(
            pltpu.HBM(snapshots.shape, jnp.bfloat16),
            jax.ShapeDtypeStruct((2 * HALO, 8), jnp.float32),
            rim,
            rim,
        ),
        in_specs=[VMEM] * 4,
        out_specs=(HBM, VMEM, VMEM, VMEM),
        scratch_shapes=[
            pltpu.VMEM(snapshots.shape, jnp.bfloat16),
            pltpu.VMEM((8, 1024), jnp.float32),
            pltpu.SemaphoreType.DMA((cells // BLOCK,)),
        ],
        compiler_params=PARAMS,
        cost_estimate=pl.CostEstimate(flops=WEIGHT_FLOPS, bytes_accessed=6_000_000, transcendentals=0),
    )(
        snapshots,
        density.reshape(1, cells),
        sound_speed.reshape(1, cells),
        offsets.reshape(1, cells),
    )


def edge_kernel(begin, end, edge_scale, outer, inner, edges):
    odd = lax.axis_index("y") % 2
    blank = jnp.zeros(outer.shape[1:], outer.dtype)
    mask = lax.broadcast_in_dim(odd, outer.shape, ()) == 1
    low = jnp.where(mask, inner[...], outer[...])
    high = jnp.where(mask, outer[...], inner[...])

    def beyond(halo, component):
        return halo[component] if component < 2 else blank

    first = weigh_rows(
        edge_scale[0:HALO],
        HALO,
        lambda component: jnp.concatenate([beyond(low, component), begin[component]], axis=0),
        lambda component: begin[component, 0:HALO],
    )
    last = weigh_rows(
        edge_scale[HALO:],
        HALO,
        lambda component: jnp.concatenate([end[component], beyond(high, component)], axis=0),
        lambda component: end[component, HALO:],
    )
    for component in range(COMPONENTS):
        edges[component, 0:HALO] = first[component]
        edges[component, HALO:] = last[component]


def weigh_edges(begin, end, edge_scale, outer, inner):
    return pl.pallas_call(
        edge_kernel,
        out_shape=jax.ShapeDtypeStruct(begin.shape, jnp.bfloat16),
        in_specs=[VMEM] * 5,
        out_specs=VMEM,
        compiler_params=PARAMS,
        cost_estimate=pl.CostEstimate(flops=EDGE_FLOPS, bytes_accessed=600_000, transcendentals=0),
    )(begin, end, edge_scale, outer, inner)


def modes_of(rotation_t, snap):
    return lax.dot_general(
        rotation_t, snap, (((1,), (1,)), ((), ())), preferred_element_type=jnp.float32
    ).astype(jnp.bfloat16)


def totals_of(mode, weighted, edges):
    cells = weighted.shape[0]
    parts = [edges[0:HALO], weighted[HALO : cells - HALO], edges[HALO:]]
    return jnp.dot(mode, jnp.concatenate(parts, axis=0), preferred_element_type=jnp.float32).T


def sent_kernel(
    weighted_hbm, snap, edges, rot, send, rotation_t, weighted_keep, weighted, sems
):
    half, _, width = weighted.shape
    kept = lax.axis_index("core") * half
    sent = half - kept
    copies = [
        pltpu.make_async_copy(weighted_hbm.at[sent + place], weighted.at[place], sems.at[place])
        for place in range(half)
    ]
    copies.append(
        pltpu.make_async_copy(weighted_hbm.at[pl.ds(kept, half)], weighted_keep, sems.at[half])
    )
    for copy in copies:
        copy.start()
    tiles, padded, modes = rot.shape
    rows = width // tiles
    shape = (width, tiles * padded)
    target = lax.broadcasted_iota(jnp.int32, shape, 0)
    source = lax.broadcasted_iota(jnp.int32, shape, 1)
    within = source & (padded - 1)
    slot = (source - within) // padded
    tile = (slot & 1) * (tiles // 2) + (slot >> 1)
    chosen = jnp.logical_and(target == tile * rows + within, within < rows)
    compact = jnp.dot(
        chosen.astype(jnp.float32).astype(jnp.bfloat16),
        rot[...].reshape(tiles * padded, modes),
        preferred_element_type=jnp.float32,
    )
    turned = compact.T.astype(jnp.bfloat16)
    rotation_t[...] = turned
    mode = [modes_of(turned, snap[sent + place]) for place in range(half)]
    for place in range(half):
        copies[place].wait()
        send[place] = totals_of(mode[place], weighted.at[place], edges.at[sent + place])
    copies[half].wait()


def project_sent(weighted, snapshots, edges, rotation):
    components, cells, width = snapshots.shape
    half = components // 2
    modes = rotation.shape[2]
    return pl.pallas_call(
        sent_kernel,
        out_shape=(
            jax.ShapeDtypeStruct((half, width, modes), jnp.float32),
            jax.ShapeDtypeStruct((modes, width), jnp.bfloat16),
            jax.ShapeDtypeStruct((half, cells, width), jnp.bfloat16),
        ),
        in_specs=[HBM, VMEM, VMEM, VMEM],
        out_specs=(VMEM, VMEM, VMEM),
        scratch_shapes=[
            pltpu.VMEM((half, cells, width), jnp.bfloat16),
            pltpu.SemaphoreType.DMA((half + 1,)),
        ],
        compiler_params=PARAMS,
        cost_estimate=pl.CostEstimate(flops=400_000_000, bytes_accessed=3_000_000, transcendentals=0),
    )(in_hbm(weighted), snapshots, edges, rotation)


def kept_kernel(snap, weighted, edges, rotation_t, keep):
    half = weighted.shape[0]
    kept = lax.axis_index("core") * half
    for place in range(half):
        mode = modes_of(rotation_t[...], snap[kept + place])
        keep[place] = totals_of(mode, weighted.at[place], edges.at[kept + place])


def project_kept(snapshots, weighted, edges, rotation_t):
    half, _, width = weighted.shape
    modes = rotation_t.shape[0]
    return pl.pallas_call(
        kept_kernel,
        out_shape=jax.ShapeDtypeStruct((half, width, modes), jnp.float32),
        in_specs=[VMEM] * 4,
        out_specs=VMEM,
        compiler_params=PARAMS,
        cost_estimate=pl.CostEstimate(flops=400_000_000, bytes_accessed=3_000_000, transcendentals=0),
    )(snapshots, weighted, edges, rotation_t)


def place_own_kernel(mine, out, sem):
    half = mine.shape[0]
    copy = pltpu.make_async_copy(mine, out.at[pl.ds(lax.axis_index("core") * half, half)], sem)
    copy.start()
    copy.wait()


def place_other_kernel(begun, other, out, sem):
    half = other.shape[0]
    copy = pltpu.make_async_copy(other, out.at[pl.ds((1 - lax.axis_index("core")) * half, half)], sem)
    copy.start()
    copy.wait()


def place_own(mine):
    half, width, modes = mine.shape
    return pl.pallas_call(
        place_own_kernel,
        out_shape=jax.ShapeDtypeStruct((2 * half, width, modes), mine.dtype),
        in_specs=[VMEM],
        out_specs=HBM,
        scratch_shapes=[pltpu.SemaphoreType.DMA],
        compiler_params=PARAMS,
        cost_estimate=pl.CostEstimate(flops=0, bytes_accessed=1_000_000, transcendentals=0),
    )(mine)


def place_other(begun, other):
    return pl.pallas_call(
        place_other_kernel,
        out_shape=jax.ShapeDtypeStruct(begun.shape, begun.dtype),
        in_specs=[HBM, VMEM],
        out_specs=HBM,
        scratch_shapes=[pltpu.SemaphoreType.DMA],
        input_output_aliases={0: 0},
        compiler_params=PARAMS,
        cost_estimate=pl.CostEstimate(flops=0, bytes_accessed=1_000_000, transcendentals=0),
    )(begun, other)


def spread(block, axes):
    count = lax.axis_size(axes)
    return lax.all_to_all(jnp.broadcast_to(block[None], (count,) + block.shape), axes, 0, 0)


def on_device(snapshots, density, sound_speed, offsets, rotation):
    components, cells, width = snapshots.shape
    count = lax.axis_size(CELL_AXES)
    inside = [(i, i ^ 1) for i in range(count)]
    across = [(i, (i + 1 if i % 2 else i - 1) % count) for i in range(count)]
    swap = [(0, 1), (1, 0)]
    with jax.named_scope("start"):
        inner, outer, rows = start(in_hbm(snapshots), rotation, lax.axis_size(TILE_AXES))
    with jax.named_scope("halo"):
        outer = lax.ppermute(outer, CELL_AXES, across)
        inner = lax.ppermute(inner, CELL_AXES, inside)
    with jax.named_scope("rotation_rows"):
        full_rotation = lax.all_to_all(rows, SPREAD_AXES, 0, 0)
    with jax.named_scope("weighting"):
        weighted, edge_scale, begin, end = weigh(snapshots, density, sound_speed, offsets)
        edges = weigh_edges(begin, end, edge_scale, outer, inner)
    with jax.named_scope("projections"):
        send, rotation_t, weighted_keep = project_sent(weighted, snapshots, edges, full_rotation)
        received = lax.ppermute(send, "core", swap)
        keep = project_kept(snapshots, weighted_keep, edges, rotation_t)
        mine = keep + received
    modes = mine.shape[2]
    members = lax.axis_size(PLANE_AXES)
    with jax.named_scope("sum_plane"):
        pieces = mine.reshape(members, components * width // (2 * members), modes)
        piece = jnp.sum(lax.all_to_all(pieces, PLANE_AXES, 0, 0), axis=0)
    with jax.named_scope("sum_z"):
        piece = jnp.sum(spread(piece, ("z",)), axis=0)
        piece = piece * (1.0 / math.sqrt(cells * count))
    with jax.named_scope("share_plane"):
        mine = spread(piece, PLANE_AXES).reshape(components // 2, width, modes)
    with jax.named_scope("share_core"):
        other = lax.ppermute(mine, "core", swap)
        return place_other(place_own(mine), other)


def solution(mesh):
    fine = Mesh(mesh.devices.reshape(2, 2, 2, 8, 4), CELL_AXES)
    return jax.shard_map(
        on_device,
        mesh=fine,
        in_specs=(
            P(None, CELL_AXES, None),
            P(CELL_AXES),
            P(CELL_AXES),
            P(CELL_AXES),
            P(TILE_AXES, None),
        ),
        out_specs=P(),
        check_vma=False,
    )
```

```python
import math

import jax
import jax.numpy as jnp
from jax import lax
from jax.experimental import pallas as pl
from jax.experimental.pallas import tpu as pltpu
from jax.sharding import Mesh, PartitionSpec as P

HALO = 32
COMPONENTS = 4
BLOCK = 192
PADDED = 8
WEIGHT_FLOPS = 1_000_000_000
EDGE_FLOPS = 1_000_000_000
START_BYTES = 100_000_000
TILE_AXES = ("x_hi", "z", "y")
SPREAD_AXES = ("z", "y", "x_hi")
PLANE_AXES = ("y", "x_lo", "x_hi")
CELL_AXES = ("x_lo", "core", "x_hi", "z", "y")
VMEM = pl.BlockSpec(memory_space=pltpu.VMEM)
HBM = pl.BlockSpec(memory_space=pltpu.HBM)
PARAMS = pltpu.CompilerParams(vmem_limit_bytes=16 << 20)


def in_hbm(array):
    return pltpu.with_memory_space_constraint(array, pltpu.HBM)


def start_kernel(snap, rot_hbm, inner, outer, spread_hbm, begin, end, rot, spread_rot, sems):
    cells = snap.shape[1]
    odd = lax.axis_index("y") % 2
    inner_at = pl.multiple_of((1 - odd) * (cells - HALO), HALO)
    outer_at = pl.multiple_of(odd * (cells - HALO), HALO)
    copies = [
        pltpu.make_async_copy(rot_hbm, rot, sems.at[0]),
        pltpu.make_async_copy(snap.at[:, pl.ds(outer_at, HALO)], begin, sems.at[1]),
        pltpu.make_async_copy(snap.at[:, pl.ds(inner_at, HALO)], end, sems.at[2]),
    ]
    for copy in copies:
        copy.start()
    copies[0].wait()
    rows = rot.shape[0]
    padding = jnp.zeros((PADDED - rows, rot.shape[1]), jnp.float32)
    block = jnp.concatenate([rot[...].astype(jnp.float32), padding], axis=0).astype(jnp.bfloat16)
    for tile in range(spread_rot.shape[0]):
        spread_rot[tile] = block
    written = pltpu.make_async_copy(spread_rot, spread_hbm, sems.at[0])
    written.start()
    for copy, rim, target in ((copies[1], begin, outer), (copies[2], end, inner)):
        copy.wait()
        speed = [rim[component].astype(jnp.float32) for component in range(1, COMPONENTS)]
        target[0] = rim[0]
        target[1] = ((speed[0] + speed[1]) + speed[2]).astype(jnp.bfloat16)
    written.wait()


def start(snapshots, rotation, tiles):
    components, _, width = snapshots.shape
    rows, modes = rotation.shape
    edge = jax.ShapeDtypeStruct((2, HALO, width), jnp.bfloat16)
    rim = pltpu.VMEM((components, HALO, width), jnp.bfloat16)
    return pl.pallas_call(
        start_kernel,
        out_shape=(edge, edge, jax.ShapeDtypeStruct((tiles, PADDED, modes), jnp.bfloat16)),
        in_specs=[HBM, HBM],
        out_specs=(VMEM, VMEM, HBM),
        scratch_shapes=[
            rim,
            rim,
            pltpu.VMEM((rows, modes), jnp.bfloat16),
            pltpu.VMEM((tiles, PADDED, modes), jnp.bfloat16),
            pltpu.SemaphoreType.DMA((3,)),
        ],
        compiler_params=PARAMS,
        cost_estimate=pl.CostEstimate(flops=0, bytes_accessed=START_BYTES, transcendentals=0),
    )(snapshots, in_hbm(rotation))


def stencil_of(shift, window, offset):
    shape = (shift.shape[0], window)
    row_at = lax.broadcasted_iota(jnp.int32, shape, 0) + offset
    col_at = lax.broadcasted_iota(jnp.int32, shape, 1)
    here = (col_at == row_at).astype(jnp.float32)
    there = (col_at == row_at + shift).astype(jnp.float32)
    return (there - here).astype(jnp.bfloat16)


def weigh_rows(scale, offset, around, block):
    rho, inverse, half = scale[:, 0:1], scale[:, 1:2], scale[:, 2:3]
    stencil = stencil_of(scale[:, 3:4].astype(jnp.int32), around(0).shape[0], offset)

    def difference(component):
        return jnp.dot(stencil, around(component), preferred_element_type=jnp.float32)

    press_part = half * difference(0)
    sum_part = half * ((difference(1) + difference(2)) + difference(3))
    values = []
    for component in range(COMPONENTS):
        wide = block(component).astype(jnp.float32)
        value = wide * inverse + sum_part if component == 0 else rho * wide + press_part
        values.append(value.astype(jnp.bfloat16))
    return values


def weighting_kernel(
    snap, dens, speed, offs, weighted_hbm, edge_scale, begin_rim, end_rim, weighted, rows_ref, sems
):
    cells = snap.shape[1]
    begin_rim[...] = snap[:, 0 : 2 * HALO]
    end_rim[...] = snap[:, cells - 2 * HALO :]
    density = dens[...]
    sound = speed[...]
    rows_ref[...] = jnp.zeros_like(rows_ref)
    rows_ref[0:1, 0:cells] = density
    rows_ref[1:2, 0:cells] = 1.0 / (density * sound * sound)
    rows_ref[2:3, 0:cells] = 0.5 / sound
    rows_ref[3:4, 0:cells] = offs[...].astype(jnp.float32)
    columns = rows_ref[...].T
    edge_scale[0:HALO] = columns[0:HALO]
    edge_scale[HALO:] = columns[cells - HALO : cells]
    copies = []
    for begin in range(0, cells, BLOCK):
        stop = begin + BLOCK
        low, high = max(begin - HALO, 0), min(stop + HALO, cells)
        values = weigh_rows(
            columns[begin:stop],
            begin - low,
            lambda component: snap[component, low:high],
            lambda component: snap[component, begin:stop],
        )
        for component in range(COMPONENTS):
            weighted[component, begin:stop] = values[component]
        rows = pl.ds(begin, BLOCK)
        copies.append(
            pltpu.make_async_copy(weighted.at[:, rows], weighted_hbm.at[:, rows], sems.at[len(copies)])
        )
        copies[-1].start()
    for copy in copies:
        copy.wait()


def weigh(snapshots, density, sound_speed, offsets):
    components, cells, width = snapshots.shape
    rim = jax.ShapeDtypeStruct((components, 2 * HALO, width), jnp.bfloat16)
    return pl.pallas_call(
        weighting_kernel,
        out_shape=(
            pltpu.HBM(snapshots.shape, jnp.bfloat16),
            jax.ShapeDtypeStruct((2 * HALO, 8), jnp.float32),
            rim,
            rim,
        ),
        in_specs=[VMEM] * 4,
        out_specs=(HBM, VMEM, VMEM, VMEM),
        scratch_shapes=[
            pltpu.VMEM(snapshots.shape, jnp.bfloat16),
            pltpu.VMEM((8, 1024), jnp.float32),
            pltpu.SemaphoreType.DMA((cells // BLOCK,)),
        ],
        compiler_params=PARAMS,
        cost_estimate=pl.CostEstimate(flops=WEIGHT_FLOPS, bytes_accessed=6_000_000, transcendentals=0),
    )(
        snapshots,
        density.reshape(1, cells),
        sound_speed.reshape(1, cells),
        offsets.reshape(1, cells),
    )


def edge_kernel(begin, end, edge_scale, outer, inner, edges):
    odd = lax.axis_index("y") % 2
    blank = jnp.zeros(outer.shape[1:], outer.dtype)
    mask = lax.broadcast_in_dim(odd, outer.shape, ()) == 1
    low = jnp.where(mask, inner[...], outer[...])
    high = jnp.where(mask, outer[...], inner[...])

    def beyond(halo, component):
        return halo[component] if component < 2 else blank

    first = weigh_rows(
        edge_scale[0:HALO],
        HALO,
        lambda component: jnp.concatenate([beyond(low, component), begin[component]], axis=0),
        lambda component: begin[component, 0:HALO],
    )
    last = weigh_rows(
        edge_scale[HALO:],
        HALO,
        lambda component: jnp.concatenate([end[component], beyond(high, component)], axis=0),
        lambda component: end[component, HALO:],
    )
    for component in range(COMPONENTS):
        edges[component, 0:HALO] = first[component]
        edges[component, HALO:] = last[component]


def weigh_edges(begin, end, edge_scale, outer, inner):
    return pl.pallas_call(
        edge_kernel,
        out_shape=jax.ShapeDtypeStruct(begin.shape, jnp.bfloat16),
        in_specs=[VMEM] * 5,
        out_specs=VMEM,
        compiler_params=PARAMS,
        cost_estimate=pl.CostEstimate(flops=EDGE_FLOPS, bytes_accessed=600_000, transcendentals=0),
    )(begin, end, edge_scale, outer, inner)


def modes_of(rotation_t, snap):
    return lax.dot_general(
        rotation_t, snap, (((1,), (1,)), ((), ())), preferred_element_type=jnp.float32
    ).astype(jnp.bfloat16)


def totals_of(mode, weighted, edges):
    cells = weighted.shape[0]
    parts = [edges[0:HALO], weighted[HALO : cells - HALO], edges[HALO:]]
    return jnp.dot(mode, jnp.concatenate(parts, axis=0), preferred_element_type=jnp.float32).T


def sent_kernel(weighted_hbm, snap, edges, rot, send, rotation_t, weighted, sems):
    half, _, width = weighted.shape
    kept = lax.axis_index("core") * half
    sent = half - kept
    copies = [
        pltpu.make_async_copy(weighted_hbm.at[sent + place], weighted.at[place], sems.at[place])
        for place in range(half)
    ]
    for copy in copies:
        copy.start()
    tiles, padded, modes = rot.shape
    rows = width // tiles
    shape = (width, tiles * padded)
    target = lax.broadcasted_iota(jnp.int32, shape, 0)
    source = lax.broadcasted_iota(jnp.int32, shape, 1)
    within = source & (padded - 1)
    slot = (source - within) // padded
    tile = (slot & 1) * (tiles // 2) + (slot >> 1)
    chosen = jnp.logical_and(target == tile * rows + within, within < rows)
    compact = jnp.dot(
        chosen.astype(jnp.float32).astype(jnp.bfloat16),
        rot[...].reshape(tiles * padded, modes),
        preferred_element_type=jnp.float32,
    )
    turned = compact.T.astype(jnp.bfloat16)
    rotation_t[...] = turned
    mode = [modes_of(turned, snap[sent + place]) for place in range(half)]
    for place in range(half):
        copies[place].wait()
        send[place] = totals_of(mode[place], weighted.at[place], edges.at[sent + place])


def project_sent(weighted, snapshots, edges, rotation):
    components, cells, width = snapshots.shape
    half = components // 2
    modes = rotation.shape[2]
    return pl.pallas_call(
        sent_kernel,
        out_shape=(
            jax.ShapeDtypeStruct((half, width, modes), jnp.float32),
            jax.ShapeDtypeStruct((modes, width), jnp.bfloat16),
        ),
        in_specs=[HBM, VMEM, VMEM, VMEM],
        out_specs=(VMEM, VMEM),
        scratch_shapes=[
            pltpu.VMEM((half, cells, width), jnp.bfloat16),
            pltpu.SemaphoreType.DMA((half,)),
        ],
        compiler_params=PARAMS,
        cost_estimate=pl.CostEstimate(flops=400_000_000, bytes_accessed=3_000_000, transcendentals=0),
    )(in_hbm(weighted), snapshots, edges, rotation)


def kept_kernel(weighted_hbm, snap, edges, rotation_t, keep, weighted, sems):
    half = weighted.shape[0]
    kept = lax.axis_index("core") * half
    copies = [
        pltpu.make_async_copy(weighted_hbm.at[kept + place], weighted.at[place], sems.at[place])
        for place in range(half)
    ]
    for copy in copies:
        copy.start()
    mode = [modes_of(rotation_t[...], snap[kept + place]) for place in range(half)]
    for place in range(half):
        copies[place].wait()
        keep[place] = totals_of(mode[place], weighted.at[place], edges.at[kept + place])


def project_kept(weighted, snapshots, edges, rotation_t):
    components, cells, width = snapshots.shape
    half = components // 2
    modes = rotation_t.shape[0]
    return pl.pallas_call(
        kept_kernel,
        out_shape=jax.ShapeDtypeStruct((half, width, modes), jnp.float32),
        in_specs=[HBM, VMEM, VMEM, VMEM],
        out_specs=VMEM,
        scratch_shapes=[
            pltpu.VMEM((half, cells, width), jnp.bfloat16),
            pltpu.SemaphoreType.DMA((half,)),
        ],
        compiler_params=PARAMS,
        cost_estimate=pl.CostEstimate(flops=400_000_000, bytes_accessed=3_000_000, transcendentals=0),
    )(in_hbm(weighted), snapshots, edges, rotation_t)


def place_own_kernel(mine, out, sem):
    half = mine.shape[0]
    copy = pltpu.make_async_copy(mine, out.at[pl.ds(lax.axis_index("core") * half, half)], sem)
    copy.start()
    copy.wait()


def place_other_kernel(begun, other, out, sem):
    half = other.shape[0]
    copy = pltpu.make_async_copy(other, out.at[pl.ds((1 - lax.axis_index("core")) * half, half)], sem)
    copy.start()
    copy.wait()


def place_own(mine):
    half, width, modes = mine.shape
    return pl.pallas_call(
        place_own_kernel,
        out_shape=jax.ShapeDtypeStruct((2 * half, width, modes), mine.dtype),
        in_specs=[VMEM],
        out_specs=HBM,
        scratch_shapes=[pltpu.SemaphoreType.DMA],
        compiler_params=PARAMS,
        cost_estimate=pl.CostEstimate(flops=0, bytes_accessed=1_000_000, transcendentals=0),
    )(mine)


def place_other(begun, other):
    return pl.pallas_call(
        place_other_kernel,
        out_shape=jax.ShapeDtypeStruct(begun.shape, begun.dtype),
        in_specs=[HBM, VMEM],
        out_specs=HBM,
        scratch_shapes=[pltpu.SemaphoreType.DMA],
        input_output_aliases={0: 0},
        compiler_params=PARAMS,
        cost_estimate=pl.CostEstimate(flops=0, bytes_accessed=1_000_000, transcendentals=0),
    )(begun, other)


def spread(block, axes):
    count = lax.axis_size(axes)
    return lax.all_to_all(jnp.broadcast_to(block[None], (count,) + block.shape), axes, 0, 0)


def on_device(snapshots, density, sound_speed, offsets, rotation):
    components, cells, width = snapshots.shape
    count = lax.axis_size(CELL_AXES)
    inside = [(i, i ^ 1) for i in range(count)]
    across = [(i, (i + 1 if i % 2 else i - 1) % count) for i in range(count)]
    swap = [(0, 1), (1, 0)]
    with jax.named_scope("start"):
        inner, outer, rows = start(in_hbm(snapshots), rotation, lax.axis_size(TILE_AXES))
    with jax.named_scope("halo"):
        outer = lax.ppermute(outer, CELL_AXES, across)
        inner = lax.ppermute(inner, CELL_AXES, inside)
    with jax.named_scope("rotation_rows"):
        full_rotation = lax.all_to_all(rows, SPREAD_AXES, 0, 0)
    with jax.named_scope("weighting"):
        weighted, edge_scale, begin, end = weigh(snapshots, density, sound_speed, offsets)
        edges = weigh_edges(begin, end, edge_scale, outer, inner)
    with jax.named_scope("projections"):
        send, rotation_t = project_sent(weighted, snapshots, edges, full_rotation)
        received = lax.ppermute(send, "core", swap)
        keep = project_kept(weighted, snapshots, edges, rotation_t)
        mine = keep + received
    modes = mine.shape[2]
    members = lax.axis_size(PLANE_AXES)
    with jax.named_scope("sum_plane"):
        pieces = mine.reshape(members, components * width // (2 * members), modes)
        piece = jnp.sum(lax.all_to_all(pieces, PLANE_AXES, 0, 0), axis=0)
    with jax.named_scope("sum_z"):
        piece = jnp.sum(spread(piece, ("z",)), axis=0)
        piece = piece * (1.0 / math.sqrt(cells * count))
    with jax.named_scope("share_plane"):
        mine = spread(piece, PLANE_AXES).reshape(components // 2, width, modes)
    with jax.named_scope("share_core"):
        other = lax.ppermute(mine, "core", swap)
        return place_other(place_own(mine), other)


def solution(mesh):
    fine = Mesh(mesh.devices.reshape(2, 2, 2, 8, 4), CELL_AXES)
    return jax.shard_map(
        on_device,
        mesh=fine,
        in_specs=(
            P(None, CELL_AXES, None),
            P(CELL_AXES),
            P(CELL_AXES),
            P(CELL_AXES),
            P(TILE_AXES, None),
        ),
        out_specs=P(),
        check_vma=False,
    )
```

```python
import math

import jax
import jax.numpy as jnp
from jax import lax
from jax.experimental import pallas as pl
from jax.experimental.pallas import tpu as pltpu
from jax.sharding import Mesh, PartitionSpec as P

HALO = 32
COMPONENTS = 4
BLOCK = 192
PADDED = 8
ROWS = 6
WEIGHT_FLOPS = 1_000_000_000
EDGE_FLOPS = 1_000_000_000
START_BYTES = 100_000_000
TILE_AXES = ("x_hi", "z", "y")
SPREAD_AXES = ("z", "y")
PLANE_AXES = ("y", "x_lo", "x_hi")
CELL_AXES = ("x_lo", "core", "x_hi", "z", "y")
VMEM = pl.BlockSpec(memory_space=pltpu.VMEM)
HBM = pl.BlockSpec(memory_space=pltpu.HBM)
PARAMS = pltpu.CompilerParams(vmem_limit_bytes=16 << 20)


def in_hbm(array):
    return pltpu.with_memory_space_constraint(array, pltpu.HBM)


def start_kernel(snap, rot_hbm, inner, outer, spread_hbm, begin, end, rot, spread_rot, sems):
    cells = snap.shape[1]
    odd = lax.axis_index("y") % 2
    inner_at = pl.multiple_of((1 - odd) * (cells - HALO), HALO)
    outer_at = pl.multiple_of(odd * (cells - HALO), HALO)
    copies = [
        pltpu.make_async_copy(rot_hbm, rot, sems.at[0]),
        pltpu.make_async_copy(snap.at[:, pl.ds(outer_at, HALO)], begin, sems.at[1]),
        pltpu.make_async_copy(snap.at[:, pl.ds(inner_at, HALO)], end, sems.at[2]),
    ]
    for copy in copies:
        copy.start()
    copies[0].wait()
    rows = rot.shape[0]
    padding = jnp.zeros((PADDED - rows, rot.shape[1]), jnp.float32)
    block = jnp.concatenate([rot[...].astype(jnp.float32), padding], axis=0).astype(jnp.bfloat16)
    for tile in range(spread_rot.shape[0]):
        spread_rot[tile] = block
    written = pltpu.make_async_copy(spread_rot, spread_hbm, sems.at[0])
    written.start()
    for copy, rim, target in ((copies[1], begin, outer), (copies[2], end, inner)):
        copy.wait()
        speed = [rim[component].astype(jnp.float32) for component in range(1, COMPONENTS)]
        target[0] = rim[0]
        target[1] = ((speed[0] + speed[1]) + speed[2]).astype(jnp.bfloat16)
    written.wait()


def start(snapshots, rotation, tiles):
    components, _, width = snapshots.shape
    rows, modes = rotation.shape
    edge = jax.ShapeDtypeStruct((2, HALO, width), jnp.bfloat16)
    rim = pltpu.VMEM((components, HALO, width), jnp.bfloat16)
    return pl.pallas_call(
        start_kernel,
        out_shape=(edge, edge, jax.ShapeDtypeStruct((tiles, PADDED, modes), jnp.bfloat16)),
        in_specs=[HBM, HBM],
        out_specs=(VMEM, VMEM, HBM),
        scratch_shapes=[
            rim,
            rim,
            pltpu.VMEM((rows, modes), jnp.bfloat16),
            pltpu.VMEM((tiles, PADDED, modes), jnp.bfloat16),
            pltpu.SemaphoreType.DMA((3,)),
        ],
        compiler_params=PARAMS,
        cost_estimate=pl.CostEstimate(flops=0, bytes_accessed=START_BYTES, transcendentals=0),
    )(snapshots, in_hbm(rotation))


def stencil_of(shift, window, offset):
    shape = (shift.shape[0], window)
    row_at = lax.broadcasted_iota(jnp.int32, shape, 0) + offset
    col_at = lax.broadcasted_iota(jnp.int32, shape, 1)
    here = (col_at == row_at).astype(jnp.float32)
    there = (col_at == row_at + shift).astype(jnp.float32)
    return (there - here).astype(jnp.bfloat16)


def weigh_rows(scale, offset, around, block):
    rho, inverse, half = scale[:, 0:1], scale[:, 1:2], scale[:, 2:3]
    stencil = stencil_of(scale[:, 3:4].astype(jnp.int32), around(0).shape[0], offset)

    def difference(component):
        return jnp.dot(stencil, around(component), preferred_element_type=jnp.float32)

    press_part = half * difference(0)
    sum_part = half * ((difference(1) + difference(2)) + difference(3))
    values = []
    for component in range(COMPONENTS):
        wide = block(component).astype(jnp.float32)
        value = wide * inverse + sum_part if component == 0 else rho * wide + press_part
        values.append(value.astype(jnp.bfloat16))
    return values


def compact_of(rot):
    pieces, padded, modes = rot.shape
    shape = (pieces * ROWS, pieces * padded)
    target = lax.broadcasted_iota(jnp.int32, shape, 0)
    source = lax.broadcasted_iota(jnp.int32, shape, 1)
    within = source & (padded - 1)
    chosen = jnp.logical_and(target == (source - within) // padded * ROWS + within, within < ROWS)
    return jnp.dot(
        chosen.astype(jnp.float32).astype(jnp.bfloat16),
        rot[...].reshape(pieces * padded, modes),
        preferred_element_type=jnp.float32,
    )


def weighting_kernel(
    snap, dens, speed, offs, rot, weighted, edge_scale, begin_rim, end_rim, own_rows, rows_ref
):
    cells = snap.shape[1]
    own_rows[...] = compact_of(rot)
    begin_rim[...] = snap[:, 0 : 2 * HALO]
    end_rim[...] = snap[:, cells - 2 * HALO :]
    density = dens[...]
    sound = speed[...]
    rows_ref[...] = jnp.zeros_like(rows_ref)
    rows_ref[0:1, 0:cells] = density
    rows_ref[1:2, 0:cells] = 1.0 / (density * sound * sound)
    rows_ref[2:3, 0:cells] = 0.5 / sound
    rows_ref[3:4, 0:cells] = offs[...].astype(jnp.float32)
    columns = rows_ref[...].T
    edge_scale[0:HALO] = columns[0:HALO]
    edge_scale[HALO:] = columns[cells - HALO : cells]
    for begin in range(0, cells, BLOCK):
        stop = begin + BLOCK
        low, high = max(begin - HALO, 0), min(stop + HALO, cells)
        values = weigh_rows(
            columns[begin:stop],
            begin - low,
            lambda component: snap[component, low:high],
            lambda component: snap[component, begin:stop],
        )
        for component in range(COMPONENTS):
            weighted[component, begin:stop] = values[component]


def weigh(snapshots, density, sound_speed, offsets, rotation):
    components, cells, width = snapshots.shape
    rim = jax.ShapeDtypeStruct((components, 2 * HALO, width), jnp.bfloat16)
    return pl.pallas_call(
        weighting_kernel,
        out_shape=(
            jax.ShapeDtypeStruct(snapshots.shape, jnp.bfloat16),
            jax.ShapeDtypeStruct((2 * HALO, 8), jnp.float32),
            rim,
            rim,
            jax.ShapeDtypeStruct((rotation.shape[0] * ROWS, rotation.shape[2]), jnp.float32),
        ),
        in_specs=[VMEM] * 5,
        out_specs=(VMEM,) * 5,
        scratch_shapes=[pltpu.VMEM((8, 1024), jnp.float32)],
        compiler_params=PARAMS,
        cost_estimate=pl.CostEstimate(flops=WEIGHT_FLOPS, bytes_accessed=6_000_000, transcendentals=0),
    )(
        snapshots,
        density.reshape(1, cells),
        sound_speed.reshape(1, cells),
        offsets.reshape(1, cells),
        rotation,
    )


def edge_kernel(begin, end, edge_scale, outer, inner, edges):
    odd = lax.axis_index("y") % 2
    blank = jnp.zeros(outer.shape[1:], outer.dtype)
    mask = lax.broadcast_in_dim(odd, outer.shape, ()) == 1
    low = jnp.where(mask, inner[...], outer[...])
    high = jnp.where(mask, outer[...], inner[...])

    def beyond(halo, component):
        return halo[component] if component < 2 else blank

    first = weigh_rows(
        edge_scale[0:HALO],
        HALO,
        lambda component: jnp.concatenate([beyond(low, component), begin[component]], axis=0),
        lambda component: begin[component, 0:HALO],
    )
    last = weigh_rows(
        edge_scale[HALO:],
        HALO,
        lambda component: jnp.concatenate([end[component], beyond(high, component)], axis=0),
        lambda component: end[component, HALO:],
    )
    for component in range(COMPONENTS):
        edges[component, 0:HALO] = first[component]
        edges[component, HALO:] = last[component]


def weigh_edges(begin, end, edge_scale, outer, inner):
    return pl.pallas_call(
        edge_kernel,
        out_shape=jax.ShapeDtypeStruct(begin.shape, jnp.bfloat16),
        in_specs=[VMEM] * 5,
        out_specs=VMEM,
        compiler_params=PARAMS,
        cost_estimate=pl.CostEstimate(flops=EDGE_FLOPS, bytes_accessed=600_000, transcendentals=0),
    )(begin, end, edge_scale, outer, inner)


def modes_of(rotation_t, snap):
    return lax.dot_general(
        rotation_t, snap, (((1,), (1,)), ((), ())), preferred_element_type=jnp.float32
    ).astype(jnp.bfloat16)


def totals_of(mode, weighted, edges):
    cells = weighted.shape[0]
    parts = [edges[0:HALO], weighted[HALO : cells - HALO], edges[HALO:]]
    return jnp.dot(mode, jnp.concatenate(parts, axis=0), preferred_element_type=jnp.float32).T


def sent_kernel(snap, weighted, edges, own_rows, rot, send, rotation_t):
    half = send.shape[0]
    sent = (1 - lax.axis_index("core")) * half
    own = own_rows[...]
    other = compact_of(rot)
    first = lax.broadcast_in_dim(lax.axis_index("x_hi"), own.shape, ()) == 0
    rows = jnp.concatenate([jnp.where(first, own, other), jnp.where(first, other, own)], axis=0)
    turned = rows.T.astype(jnp.bfloat16)
    rotation_t[...] = turned
    for place in range(half):
        mode = modes_of(turned, snap[sent + place])
        send[place] = totals_of(mode, weighted.at[sent + place], edges.at[sent + place])


def project_sent(snapshots, weighted, edges, own_rows, rotation):
    components, _, width = snapshots.shape
    modes = rotation.shape[2]
    return pl.pallas_call(
        sent_kernel,
        out_shape=(
            jax.ShapeDtypeStruct((components // 2, width, modes), jnp.float32),
            jax.ShapeDtypeStruct((modes, width), jnp.bfloat16),
        ),
        in_specs=[VMEM] * 5,
        out_specs=(VMEM, VMEM),
        compiler_params=PARAMS,
        cost_estimate=pl.CostEstimate(flops=400_000_000, bytes_accessed=3_000_000, transcendentals=0),
    )(snapshots, weighted, edges, own_rows, rotation)


def kept_kernel(snap, weighted, edges, rotation_t, keep):
    half = keep.shape[0]
    kept = lax.axis_index("core") * half
    for place in range(half):
        mode = modes_of(rotation_t[...], snap[kept + place])
        keep[place] = totals_of(mode, weighted.at[kept + place], edges.at[kept + place])


def project_kept(snapshots, weighted, edges, rotation_t):
    components, _, width = snapshots.shape
    modes = rotation_t.shape[0]
    return pl.pallas_call(
        kept_kernel,
        out_shape=jax.ShapeDtypeStruct((components // 2, width, modes), jnp.float32),
        in_specs=[VMEM] * 4,
        out_specs=VMEM,
        compiler_params=PARAMS,
        cost_estimate=pl.CostEstimate(flops=400_000_000, bytes_accessed=3_000_000, transcendentals=0),
    )(snapshots, weighted, edges, rotation_t)


def place_own_kernel(mine, out, sem):
    half = mine.shape[0]
    copy = pltpu.make_async_copy(mine, out.at[pl.ds(lax.axis_index("core") * half, half)], sem)
    copy.start()
    copy.wait()


def place_other_kernel(begun, other, out, sem):
    half = other.shape[0]
    copy = pltpu.make_async_copy(other, out.at[pl.ds((1 - lax.axis_index("core")) * half, half)], sem)
    copy.start()
    copy.wait()


def place_own(mine):
    half, width, modes = mine.shape
    return pl.pallas_call(
        place_own_kernel,
        out_shape=jax.ShapeDtypeStruct((2 * half, width, modes), mine.dtype),
        in_specs=[VMEM],
        out_specs=HBM,
        scratch_shapes=[pltpu.SemaphoreType.DMA],
        compiler_params=PARAMS,
        cost_estimate=pl.CostEstimate(flops=0, bytes_accessed=1_000_000, transcendentals=0),
    )(mine)


def place_other(begun, other):
    return pl.pallas_call(
        place_other_kernel,
        out_shape=jax.ShapeDtypeStruct(begun.shape, begun.dtype),
        in_specs=[HBM, VMEM],
        out_specs=HBM,
        scratch_shapes=[pltpu.SemaphoreType.DMA],
        input_output_aliases={0: 0},
        compiler_params=PARAMS,
        cost_estimate=pl.CostEstimate(flops=0, bytes_accessed=1_000_000, transcendentals=0),
    )(begun, other)


def spread(block, axes):
    count = lax.axis_size(axes)
    return lax.all_to_all(jnp.broadcast_to(block[None], (count,) + block.shape), axes, 0, 0)


def on_device(snapshots, density, sound_speed, offsets, rotation):
    components, cells, width = snapshots.shape
    count = lax.axis_size(CELL_AXES)
    inside = [(i, i ^ 1) for i in range(count)]
    across = [(i, (i + 1 if i % 2 else i - 1) % count) for i in range(count)]
    swap = [(0, 1), (1, 0)]
    with jax.named_scope("start"):
        inner, outer, rows = start(in_hbm(snapshots), rotation, lax.axis_size(SPREAD_AXES))
    with jax.named_scope("halo"):
        outer = lax.ppermute(outer, CELL_AXES, across)
        inner = lax.ppermute(inner, CELL_AXES, inside)
    with jax.named_scope("rotation_rows"):
        own_pieces = lax.all_to_all(rows, SPREAD_AXES, 0, 0)
        other_pieces = lax.ppermute(own_pieces, "x_hi", swap)
    with jax.named_scope("weighting"):
        weighted, edge_scale, begin, end, own_rows = weigh(
            snapshots, density, sound_speed, offsets, own_pieces
        )
        edges = weigh_edges(begin, end, edge_scale, outer, inner)
    with jax.named_scope("projections"):
        send, rotation_t = project_sent(snapshots, weighted, edges, own_rows, other_pieces)
        received = lax.ppermute(send, "core", swap)
        keep = project_kept(snapshots, weighted, edges, rotation_t)
        mine = keep + received
    modes = mine.shape[2]
    members = lax.axis_size(PLANE_AXES)
    with jax.named_scope("sum_plane"):
        pieces = mine.reshape(members, components * width // (2 * members), modes)
        piece = jnp.sum(lax.all_to_all(pieces, PLANE_AXES, 0, 0), axis=0)
    with jax.named_scope("sum_z"):
        piece = jnp.sum(spread(piece, ("z",)), axis=0)
        piece = piece * (1.0 / math.sqrt(cells * count))
    with jax.named_scope("share_plane"):
        mine = spread(piece, PLANE_AXES).reshape(components // 2, width, modes)
    with jax.named_scope("share_core"):
        other = lax.ppermute(mine, "core", swap)
        return place_other(place_own(mine), other)


def solution(mesh):
    fine = Mesh(mesh.devices.reshape(2, 2, 2, 8, 4), CELL_AXES)
    return jax.shard_map(
        on_device,
        mesh=fine,
        in_specs=(
            P(None, CELL_AXES, None),
            P(CELL_AXES),
            P(CELL_AXES),
            P(CELL_AXES),
            P(TILE_AXES, None),
        ),
        out_specs=P(),
        check_vma=False,
    )
```

```python
import math

import jax
import jax.numpy as jnp
from jax import lax
from jax.experimental import pallas as pl
from jax.experimental.pallas import tpu as pltpu
from jax.sharding import Mesh, PartitionSpec as P

HALO = 32
COMPONENTS = 4
BLOCK = 192
PADDED = 8
ROWS = 6
WEIGHT_FLOPS = 1_000_000_000
EDGE_FLOPS = 1_000_000_000
START_BYTES = 100_000_000
TILE_AXES = ("x_hi", "z", "y")
SPREAD_AXES = ("z", "y")
PLANE_AXES = ("y", "x_lo", "x_hi")
CELL_AXES = ("x_lo", "core", "x_hi", "z", "y")
VMEM = pl.BlockSpec(memory_space=pltpu.VMEM)
HBM = pl.BlockSpec(memory_space=pltpu.HBM)
PARAMS = pltpu.CompilerParams(vmem_limit_bytes=16 << 20)


def in_hbm(array):
    return pltpu.with_memory_space_constraint(array, pltpu.HBM)


def start_kernel(snap, rot_hbm, inner, outer, spread_hbm, begin, end, rot, spread_rot, sems):
    cells = snap.shape[1]
    odd = lax.axis_index("y") % 2
    inner_at = pl.multiple_of((1 - odd) * (cells - HALO), HALO)
    outer_at = pl.multiple_of(odd * (cells - HALO), HALO)
    copies = [
        pltpu.make_async_copy(rot_hbm, rot, sems.at[0]),
        pltpu.make_async_copy(snap.at[:, pl.ds(outer_at, HALO)], begin, sems.at[1]),
        pltpu.make_async_copy(snap.at[:, pl.ds(inner_at, HALO)], end, sems.at[2]),
    ]
    for copy in copies:
        copy.start()
    copies[0].wait()
    rows = rot.shape[0]
    padding = jnp.zeros((PADDED - rows, rot.shape[1]), jnp.float32)
    block = jnp.concatenate([rot[...].astype(jnp.float32), padding], axis=0).astype(jnp.bfloat16)
    for tile in range(spread_rot.shape[0]):
        spread_rot[tile] = block
    written = pltpu.make_async_copy(spread_rot, spread_hbm, sems.at[0])
    written.start()
    for copy, rim, target in ((copies[1], begin, outer), (copies[2], end, inner)):
        copy.wait()
        speed = [rim[component].astype(jnp.float32) for component in range(1, COMPONENTS)]
        target[0] = rim[0]
        target[1] = ((speed[0] + speed[1]) + speed[2]).astype(jnp.bfloat16)
    written.wait()


def start(snapshots, rotation, tiles):
    components, _, width = snapshots.shape
    rows, modes = rotation.shape
    edge = jax.ShapeDtypeStruct((2, HALO, width), jnp.bfloat16)
    rim = pltpu.VMEM((components, HALO, width), jnp.bfloat16)
    return pl.pallas_call(
        start_kernel,
        out_shape=(edge, edge, jax.ShapeDtypeStruct((tiles, PADDED, modes), jnp.bfloat16)),
        in_specs=[HBM, HBM],
        out_specs=(VMEM, VMEM, HBM),
        scratch_shapes=[
            rim,
            rim,
            pltpu.VMEM((rows, modes), jnp.bfloat16),
            pltpu.VMEM((tiles, PADDED, modes), jnp.bfloat16),
            pltpu.SemaphoreType.DMA((3,)),
        ],
        compiler_params=PARAMS,
        cost_estimate=pl.CostEstimate(flops=0, bytes_accessed=START_BYTES, transcendentals=0),
    )(snapshots, in_hbm(rotation))


def stencil_of(shift, window, offset):
    shape = (shift.shape[0], window)
    row_at = lax.broadcasted_iota(jnp.int32, shape, 0) + offset
    col_at = lax.broadcasted_iota(jnp.int32, shape, 1)
    here = (col_at == row_at).astype(jnp.float32)
    there = (col_at == row_at + shift).astype(jnp.float32)
    return (there - here).astype(jnp.bfloat16)


def weigh_rows(scale, offset, around, block):
    rho, inverse, half = scale[:, 0:1], scale[:, 1:2], scale[:, 2:3]
    stencil = stencil_of(scale[:, 3:4].astype(jnp.int32), around(0).shape[0], offset)

    def difference(component):
        return jnp.dot(stencil, around(component), preferred_element_type=jnp.float32)

    press_part = half * difference(0)
    sum_part = half * ((difference(1) + difference(2)) + difference(3))
    values = []
    for component in range(COMPONENTS):
        wide = block(component).astype(jnp.float32)
        value = wide * inverse + sum_part if component == 0 else rho * wide + press_part
        values.append(value.astype(jnp.bfloat16))
    return values


def compact_of(rot):
    pieces, padded, modes = rot.shape
    shape = (pieces * ROWS, pieces * padded)
    target = lax.broadcasted_iota(jnp.int32, shape, 0)
    source = lax.broadcasted_iota(jnp.int32, shape, 1)
    within = source & (padded - 1)
    chosen = jnp.logical_and(target == (source - within) // padded * ROWS + within, within < ROWS)
    return jnp.dot(
        chosen.astype(jnp.float32).astype(jnp.bfloat16),
        rot[...].reshape(pieces * padded, modes),
        preferred_element_type=jnp.float32,
    )


def weighting_kernel(
    snap, dens, speed, offs, rot, weighted, edge_scale, begin_rim, end_rim, own_rows, rows_ref
):
    cells = snap.shape[1]
    own_rows[...] = compact_of(rot)
    begin_rim[...] = snap[:, 0 : 2 * HALO]
    end_rim[...] = snap[:, cells - 2 * HALO :]
    density = dens[...]
    sound = speed[...]
    rows_ref[...] = jnp.zeros_like(rows_ref)
    rows_ref[0:1, 0:cells] = density
    rows_ref[1:2, 0:cells] = 1.0 / (density * sound * sound)
    rows_ref[2:3, 0:cells] = 0.5 / sound
    rows_ref[3:4, 0:cells] = offs[...].astype(jnp.float32)
    columns = rows_ref[...].T
    edge_scale[0:HALO] = columns[0:HALO]
    edge_scale[HALO:] = columns[cells - HALO : cells]
    for begin in range(0, cells, BLOCK):
        stop = begin + BLOCK
        low, high = max(begin - HALO, 0), min(stop + HALO, cells)
        values = weigh_rows(
            columns[begin:stop],
            begin - low,
            lambda component: snap[component, low:high],
            lambda component: snap[component, begin:stop],
        )
        for component in range(COMPONENTS):
            weighted[component, begin:stop] = values[component]


def weigh(snapshots, density, sound_speed, offsets, rotation):
    components, cells, width = snapshots.shape
    rim = jax.ShapeDtypeStruct((components, 2 * HALO, width), jnp.bfloat16)
    return pl.pallas_call(
        weighting_kernel,
        out_shape=(
            jax.ShapeDtypeStruct(snapshots.shape, jnp.bfloat16),
            jax.ShapeDtypeStruct((2 * HALO, 8), jnp.float32),
            rim,
            rim,
            jax.ShapeDtypeStruct((rotation.shape[0] * ROWS, rotation.shape[2]), jnp.float32),
        ),
        in_specs=[VMEM] * 5,
        out_specs=(VMEM,) * 5,
        scratch_shapes=[pltpu.VMEM((8, 1024), jnp.float32)],
        compiler_params=PARAMS,
        cost_estimate=pl.CostEstimate(flops=WEIGHT_FLOPS, bytes_accessed=6_000_000, transcendentals=0),
    )(
        snapshots,
        density.reshape(1, cells),
        sound_speed.reshape(1, cells),
        offsets.reshape(1, cells),
        rotation,
    )


def edge_kernel(begin, end, edge_scale, outer, inner, edges):
    odd = lax.axis_index("y") % 2
    blank = jnp.zeros(outer.shape[1:], outer.dtype)
    mask = lax.broadcast_in_dim(odd, outer.shape, ()) == 1
    low = jnp.where(mask, inner[...], outer[...])
    high = jnp.where(mask, outer[...], inner[...])

    def beyond(halo, component):
        return halo[component] if component < 2 else blank

    first = weigh_rows(
        edge_scale[0:HALO],
        HALO,
        lambda component: jnp.concatenate([beyond(low, component), begin[component]], axis=0),
        lambda component: begin[component, 0:HALO],
    )
    last = weigh_rows(
        edge_scale[HALO:],
        HALO,
        lambda component: jnp.concatenate([end[component], beyond(high, component)], axis=0),
        lambda component: end[component, HALO:],
    )
    for component in range(COMPONENTS):
        edges[component, 0:HALO] = first[component]
        edges[component, HALO:] = last[component]


def weigh_edges(begin, end, edge_scale, outer, inner):
    return pl.pallas_call(
        edge_kernel,
        out_shape=jax.ShapeDtypeStruct(begin.shape, jnp.bfloat16),
        in_specs=[VMEM] * 5,
        out_specs=VMEM,
        compiler_params=PARAMS,
        cost_estimate=pl.CostEstimate(flops=EDGE_FLOPS, bytes_accessed=600_000, transcendentals=0),
    )(begin, end, edge_scale, outer, inner)


def modes_of(rotation_t, snap):
    return lax.dot_general(
        rotation_t, snap, (((1,), (1,)), ((), ())), preferred_element_type=jnp.float32
    ).astype(jnp.bfloat16)


def totals_of(mode, weighted, edges):
    cells = weighted.shape[0]
    parts = [edges[0:HALO], weighted[HALO : cells - HALO], edges[HALO:]]
    return jnp.dot(mode, jnp.concatenate(parts, axis=0), preferred_element_type=jnp.float32).T


def sent_kernel(snap, weighted, edges, own_rows, rot, send, rotation_t):
    half = send.shape[0]
    sent = (1 - lax.axis_index("core")) * half
    own = own_rows[...]
    other = compact_of(rot)
    first = lax.broadcast_in_dim(lax.axis_index("x_hi"), own.shape, ()) == 0
    rows = jnp.concatenate([jnp.where(first, own, other), jnp.where(first, other, own)], axis=0)
    turned = rows.T.astype(jnp.bfloat16)
    rotation_t[...] = turned
    for place in range(half):
        mode = modes_of(turned, snap[sent + place])
        send[place] = totals_of(mode, weighted.at[sent + place], edges.at[sent + place])


def project_sent(snapshots, weighted, edges, own_rows, rotation):
    components, _, width = snapshots.shape
    modes = rotation.shape[2]
    return pl.pallas_call(
        sent_kernel,
        out_shape=(
            jax.ShapeDtypeStruct((components // 2, width, modes), jnp.float32),
            jax.ShapeDtypeStruct((modes, width), jnp.bfloat16),
        ),
        in_specs=[VMEM] * 5,
        out_specs=(VMEM, VMEM),
        compiler_params=PARAMS,
        cost_estimate=pl.CostEstimate(flops=400_000_000, bytes_accessed=3_000_000, transcendentals=0),
    )(snapshots, weighted, edges, own_rows, rotation)


def kept_kernel(snap, weighted, edges, rotation_t, keep):
    half = keep.shape[0]
    kept = lax.axis_index("core") * half
    for place in range(half):
        mode = modes_of(rotation_t[...], snap[kept + place])
        keep[place] = totals_of(mode, weighted.at[kept + place], edges.at[kept + place])


def project_kept(snapshots, weighted, edges, rotation_t):
    components, _, width = snapshots.shape
    modes = rotation_t.shape[0]
    return pl.pallas_call(
        kept_kernel,
        out_shape=jax.ShapeDtypeStruct((components // 2, width, modes), jnp.float32),
        in_specs=[VMEM] * 4,
        out_specs=VMEM,
        compiler_params=PARAMS,
        cost_estimate=pl.CostEstimate(flops=400_000_000, bytes_accessed=3_000_000, transcendentals=0),
    )(snapshots, weighted, edges, rotation_t)


def place_own_kernel(mine, out, sem):
    half = mine.shape[0]
    copy = pltpu.make_async_copy(mine, out.at[pl.ds(lax.axis_index("core") * half, half)], sem)
    copy.start()
    copy.wait()


def place_other_kernel(begun, other, out, sem):
    half = other.shape[0]
    copy = pltpu.make_async_copy(other, out.at[pl.ds((1 - lax.axis_index("core")) * half, half)], sem)
    copy.start()
    copy.wait()


def place_own(mine):
    half, width, modes = mine.shape
    return pl.pallas_call(
        place_own_kernel,
        out_shape=jax.ShapeDtypeStruct((2 * half, width, modes), mine.dtype),
        in_specs=[VMEM],
        out_specs=HBM,
        scratch_shapes=[pltpu.SemaphoreType.DMA],
        compiler_params=PARAMS,
        cost_estimate=pl.CostEstimate(flops=0, bytes_accessed=1_000_000, transcendentals=0),
    )(mine)


def place_other(begun, other):
    return pl.pallas_call(
        place_other_kernel,
        out_shape=jax.ShapeDtypeStruct(begun.shape, begun.dtype),
        in_specs=[HBM, VMEM],
        out_specs=HBM,
        scratch_shapes=[pltpu.SemaphoreType.DMA],
        input_output_aliases={0: 0},
        compiler_params=PARAMS,
        cost_estimate=pl.CostEstimate(flops=0, bytes_accessed=1_000_000, transcendentals=0),
    )(begun, other)


def spread(block, axes):
    count = lax.axis_size(axes)
    return lax.all_to_all(jnp.broadcast_to(block[None], (count,) + block.shape), axes, 0, 0)


def on_device(snapshots, density, sound_speed, offsets, rotation):
    components, cells, width = snapshots.shape
    count = lax.axis_size(CELL_AXES)
    inside = [(i, i ^ 1) for i in range(count)]
    across = [(i, (i + 1 if i % 2 else i - 1) % count) for i in range(count)]
    swap = [(0, 1), (1, 0)]
    with jax.named_scope("start"):
        inner, outer, rows = start(in_hbm(snapshots), rotation, lax.axis_size(SPREAD_AXES))
    with jax.named_scope("halo"):
        outer = lax.ppermute(outer, CELL_AXES, across)
        inner = lax.ppermute(inner, CELL_AXES, inside)
    with jax.named_scope("rotation_rows"):
        own_pieces = lax.all_to_all(rows, SPREAD_AXES, 0, 0)
        other_pieces = lax.ppermute(own_pieces, ("x_lo", "x_hi"), [(i, 3 - i) for i in range(4)])
    with jax.named_scope("weighting"):
        weighted, edge_scale, begin, end, own_rows = weigh(
            snapshots, density, sound_speed, offsets, own_pieces
        )
        edges = weigh_edges(begin, end, edge_scale, outer, inner)
    with jax.named_scope("projections"):
        send, rotation_t = project_sent(snapshots, weighted, edges, own_rows, other_pieces)
        received = lax.ppermute(send, "core", swap)
        keep = project_kept(snapshots, weighted, edges, rotation_t)
        mine = keep + received
    modes = mine.shape[2]
    members = lax.axis_size(PLANE_AXES)
    with jax.named_scope("sum_plane"):
        pieces = mine.reshape(members, components * width // (2 * members), modes)
        piece = jnp.sum(lax.all_to_all(pieces, PLANE_AXES, 0, 0), axis=0)
    with jax.named_scope("sum_z"):
        piece = jnp.sum(spread(piece, ("z",)), axis=0)
        piece = piece * (1.0 / math.sqrt(cells * count))
    with jax.named_scope("share_plane"):
        mine = spread(piece, PLANE_AXES).reshape(components // 2, width, modes)
    with jax.named_scope("share_core"):
        other = lax.ppermute(mine, "core", swap)
        return place_other(place_own(mine), other)


def solution(mesh):
    fine = Mesh(mesh.devices.reshape(2, 2, 2, 8, 4), CELL_AXES)
    return jax.shard_map(
        on_device,
        mesh=fine,
        in_specs=(
            P(None, CELL_AXES, None),
            P(CELL_AXES),
            P(CELL_AXES),
            P(CELL_AXES),
            P(TILE_AXES, None),
        ),
        out_specs=P(),
        check_vma=False,
    )
```

```python
import math

import jax
import jax.numpy as jnp
from jax import lax
from jax.experimental import pallas as pl
from jax.experimental.pallas import tpu as pltpu
from jax.sharding import Mesh, PartitionSpec as P

HALO = 32
COMPONENTS = 4
BLOCK = 192
PADDED = 8
ROWS = 6
WEIGHT_FLOPS = 1_000_000_000
EDGE_FLOPS = 1_000_000_000
START_BYTES = 100_000_000
RIM_BYTES = 1_000_000
TILE_AXES = ("x_hi", "z", "y")
SPREAD_AXES = ("z", "y")
PLANE_AXES = ("y", "x_lo", "x_hi")
CELL_AXES = ("x_lo", "core", "x_hi", "z", "y")
VMEM = pl.BlockSpec(memory_space=pltpu.VMEM)
HBM = pl.BlockSpec(memory_space=pltpu.HBM)
PARAMS = pltpu.CompilerParams(vmem_limit_bytes=16 << 20)


def in_hbm(array):
    return pltpu.with_memory_space_constraint(array, pltpu.HBM)


def rows_kernel(rot_hbm, spread_hbm, rot, spread_rot, sem):
    load = pltpu.make_async_copy(rot_hbm, rot, sem)
    load.start()
    load.wait()
    rows = rot.shape[0]
    padding = jnp.zeros((PADDED - rows, rot.shape[1]), jnp.float32)
    block = jnp.concatenate([rot[...].astype(jnp.float32), padding], axis=0).astype(jnp.bfloat16)
    for tile in range(spread_rot.shape[0]):
        spread_rot[tile] = block
    written = pltpu.make_async_copy(spread_rot, spread_hbm, sem)
    written.start()
    written.wait()


def spread_rows(rotation, tiles):
    rows, modes = rotation.shape
    shape = (tiles, PADDED, modes)
    return pl.pallas_call(
        rows_kernel,
        out_shape=jax.ShapeDtypeStruct(shape, jnp.bfloat16),
        in_specs=[HBM],
        out_specs=HBM,
        scratch_shapes=[
            pltpu.VMEM((rows, modes), jnp.bfloat16),
            pltpu.VMEM(shape, jnp.bfloat16),
            pltpu.SemaphoreType.DMA,
        ],
        compiler_params=PARAMS,
        cost_estimate=pl.CostEstimate(flops=0, bytes_accessed=START_BYTES, transcendentals=0),
    )(in_hbm(rotation))


def rims_kernel(snap, inner, outer, begin, end, sems):
    cells = snap.shape[1]
    odd = lax.axis_index("y") % 2
    inner_at = pl.multiple_of((1 - odd) * (cells - HALO), HALO)
    outer_at = pl.multiple_of(odd * (cells - HALO), HALO)
    copies = [
        pltpu.make_async_copy(snap.at[:, pl.ds(outer_at, HALO)], begin, sems.at[0]),
        pltpu.make_async_copy(snap.at[:, pl.ds(inner_at, HALO)], end, sems.at[1]),
    ]
    for copy in copies:
        copy.start()
    for copy, rim, target in ((copies[0], begin, outer), (copies[1], end, inner)):
        copy.wait()
        speed = [rim[component].astype(jnp.float32) for component in range(1, COMPONENTS)]
        target[0] = rim[0]
        target[1] = ((speed[0] + speed[1]) + speed[2]).astype(jnp.bfloat16)


def rims(snapshots):
    components, _, width = snapshots.shape
    edge = jax.ShapeDtypeStruct((2, HALO, width), jnp.bfloat16)
    rim = pltpu.VMEM((components, HALO, width), jnp.bfloat16)
    return pl.pallas_call(
        rims_kernel,
        out_shape=(edge, edge),
        in_specs=[HBM],
        out_specs=(VMEM, VMEM),
        scratch_shapes=[rim, rim, pltpu.SemaphoreType.DMA((2,))],
        compiler_params=PARAMS,
        cost_estimate=pl.CostEstimate(flops=0, bytes_accessed=RIM_BYTES, transcendentals=0),
    )(in_hbm(snapshots))


def stencil_of(shift, window, offset):
    shape = (shift.shape[0], window)
    row_at = lax.broadcasted_iota(jnp.int32, shape, 0) + offset
    col_at = lax.broadcasted_iota(jnp.int32, shape, 1)
    here = (col_at == row_at).astype(jnp.float32)
    there = (col_at == row_at + shift).astype(jnp.float32)
    return (there - here).astype(jnp.bfloat16)


def weigh_rows(scale, offset, around, block):
    rho, inverse, half = scale[:, 0:1], scale[:, 1:2], scale[:, 2:3]
    stencil = stencil_of(scale[:, 3:4].astype(jnp.int32), around(0).shape[0], offset)

    def difference(component):
        return jnp.dot(stencil, around(component), preferred_element_type=jnp.float32)

    press_part = half * difference(0)
    sum_part = half * ((difference(1) + difference(2)) + difference(3))
    values = []
    for component in range(COMPONENTS):
        wide = block(component).astype(jnp.float32)
        value = wide * inverse + sum_part if component == 0 else rho * wide + press_part
        values.append(value.astype(jnp.bfloat16))
    return values


def compact_of(rot):
    pieces, padded, modes = rot.shape
    shape = (pieces * ROWS, pieces * padded)
    target = lax.broadcasted_iota(jnp.int32, shape, 0)
    source = lax.broadcasted_iota(jnp.int32, shape, 1)
    within = source & (padded - 1)
    chosen = jnp.logical_and(target == (source - within) // padded * ROWS + within, within < ROWS)
    return jnp.dot(
        chosen.astype(jnp.float32).astype(jnp.bfloat16),
        rot[...].reshape(pieces * padded, modes),
        preferred_element_type=jnp.float32,
    )


def weighting_kernel(
    snap, dens, speed, offs, rot, weighted, edge_scale, begin_rim, end_rim, own_rows, rows_ref
):
    cells = snap.shape[1]
    own_rows[...] = compact_of(rot)
    begin_rim[...] = snap[:, 0 : 2 * HALO]
    end_rim[...] = snap[:, cells - 2 * HALO :]
    density = dens[...]
    sound = speed[...]
    rows_ref[...] = jnp.zeros_like(rows_ref)
    rows_ref[0:1, 0:cells] = density
    rows_ref[1:2, 0:cells] = 1.0 / (density * sound * sound)
    rows_ref[2:3, 0:cells] = 0.5 / sound
    rows_ref[3:4, 0:cells] = offs[...].astype(jnp.float32)
    columns = rows_ref[...].T
    edge_scale[0:HALO] = columns[0:HALO]
    edge_scale[HALO:] = columns[cells - HALO : cells]
    for begin in range(0, cells, BLOCK):
        stop = begin + BLOCK
        low, high = max(begin - HALO, 0), min(stop + HALO, cells)
        values = weigh_rows(
            columns[begin:stop],
            begin - low,
            lambda component: snap[component, low:high],
            lambda component: snap[component, begin:stop],
        )
        for component in range(COMPONENTS):
            weighted[component, begin:stop] = values[component]


def weigh(snapshots, density, sound_speed, offsets, rotation):
    components, cells, width = snapshots.shape
    rim = jax.ShapeDtypeStruct((components, 2 * HALO, width), jnp.bfloat16)
    return pl.pallas_call(
        weighting_kernel,
        out_shape=(
            jax.ShapeDtypeStruct(snapshots.shape, jnp.bfloat16),
            jax.ShapeDtypeStruct((2 * HALO, 8), jnp.float32),
            rim,
            rim,
            jax.ShapeDtypeStruct((rotation.shape[0] * ROWS, rotation.shape[2]), jnp.float32),
        ),
        in_specs=[VMEM] * 5,
        out_specs=(VMEM,) * 5,
        scratch_shapes=[pltpu.VMEM((8, 1024), jnp.float32)],
        compiler_params=PARAMS,
        cost_estimate=pl.CostEstimate(flops=WEIGHT_FLOPS, bytes_accessed=6_000_000, transcendentals=0),
    )(
        snapshots,
        density.reshape(1, cells),
        sound_speed.reshape(1, cells),
        offsets.reshape(1, cells),
        rotation,
    )


def edge_kernel(begin, end, edge_scale, outer, inner, edges):
    odd = lax.axis_index("y") % 2
    blank = jnp.zeros(outer.shape[1:], outer.dtype)
    mask = lax.broadcast_in_dim(odd, outer.shape, ()) == 1
    low = jnp.where(mask, inner[...], outer[...])
    high = jnp.where(mask, outer[...], inner[...])

    def beyond(halo, component):
        return halo[component] if component < 2 else blank

    first = weigh_rows(
        edge_scale[0:HALO],
        HALO,
        lambda component: jnp.concatenate([beyond(low, component), begin[component]], axis=0),
        lambda component: begin[component, 0:HALO],
    )
    last = weigh_rows(
        edge_scale[HALO:],
        HALO,
        lambda component: jnp.concatenate([end[component], beyond(high, component)], axis=0),
        lambda component: end[component, HALO:],
    )
    for component in range(COMPONENTS):
        edges[component, 0:HALO] = first[component]
        edges[component, HALO:] = last[component]


def weigh_edges(begin, end, edge_scale, outer, inner):
    return pl.pallas_call(
        edge_kernel,
        out_shape=jax.ShapeDtypeStruct(begin.shape, jnp.bfloat16),
        in_specs=[VMEM] * 5,
        out_specs=VMEM,
        compiler_params=PARAMS,
        cost_estimate=pl.CostEstimate(flops=EDGE_FLOPS, bytes_accessed=600_000, transcendentals=0),
    )(begin, end, edge_scale, outer, inner)


def modes_of(rotation_t, snap):
    return lax.dot_general(
        rotation_t, snap, (((1,), (1,)), ((), ())), preferred_element_type=jnp.float32
    ).astype(jnp.bfloat16)


def totals_of(mode, weighted, edges):
    cells = weighted.shape[0]
    parts = [edges[0:HALO], weighted[HALO : cells - HALO], edges[HALO:]]
    return jnp.dot(mode, jnp.concatenate(parts, axis=0), preferred_element_type=jnp.float32).T


def sent_kernel(snap, weighted, edges, own_rows, rot, send, rotation_t):
    half = send.shape[0]
    sent = (1 - lax.axis_index("core")) * half
    own = own_rows[...]
    other = compact_of(rot)
    first = lax.broadcast_in_dim(lax.axis_index("x_hi"), own.shape, ()) == 0
    rows = jnp.concatenate([jnp.where(first, own, other), jnp.where(first, other, own)], axis=0)
    turned = rows.T.astype(jnp.bfloat16)
    rotation_t[...] = turned
    for place in range(half):
        mode = modes_of(turned, snap[sent + place])
        send[place] = totals_of(mode, weighted.at[sent + place], edges.at[sent + place])


def project_sent(snapshots, weighted, edges, own_rows, rotation):
    components, _, width = snapshots.shape
    modes = rotation.shape[2]
    return pl.pallas_call(
        sent_kernel,
        out_shape=(
            jax.ShapeDtypeStruct((components // 2, width, modes), jnp.float32),
            jax.ShapeDtypeStruct((modes, width), jnp.bfloat16),
        ),
        in_specs=[VMEM] * 5,
        out_specs=(VMEM, VMEM),
        compiler_params=PARAMS,
        cost_estimate=pl.CostEstimate(flops=400_000_000, bytes_accessed=3_000_000, transcendentals=0),
    )(snapshots, weighted, edges, own_rows, rotation)


def kept_kernel(snap, weighted, edges, rotation_t, keep):
    half = keep.shape[0]
    kept = lax.axis_index("core") * half
    for place in range(half):
        mode = modes_of(rotation_t[...], snap[kept + place])
        keep[place] = totals_of(mode, weighted.at[kept + place], edges.at[kept + place])


def project_kept(snapshots, weighted, edges, rotation_t):
    components, _, width = snapshots.shape
    modes = rotation_t.shape[0]
    return pl.pallas_call(
        kept_kernel,
        out_shape=jax.ShapeDtypeStruct((components // 2, width, modes), jnp.float32),
        in_specs=[VMEM] * 4,
        out_specs=VMEM,
        compiler_params=PARAMS,
        cost_estimate=pl.CostEstimate(flops=400_000_000, bytes_accessed=3_000_000, transcendentals=0),
    )(snapshots, weighted, edges, rotation_t)


def place_own_kernel(mine, out, sem):
    half = mine.shape[0]
    copy = pltpu.make_async_copy(mine, out.at[pl.ds(lax.axis_index("core") * half, half)], sem)
    copy.start()
    copy.wait()


def place_other_kernel(begun, other, out, sem):
    half = other.shape[0]
    copy = pltpu.make_async_copy(other, out.at[pl.ds((1 - lax.axis_index("core")) * half, half)], sem)
    copy.start()
    copy.wait()


def place_own(mine):
    half, width, modes = mine.shape
    return pl.pallas_call(
        place_own_kernel,
        out_shape=jax.ShapeDtypeStruct((2 * half, width, modes), mine.dtype),
        in_specs=[VMEM],
        out_specs=HBM,
        scratch_shapes=[pltpu.SemaphoreType.DMA],
        compiler_params=PARAMS,
        cost_estimate=pl.CostEstimate(flops=0, bytes_accessed=1_000_000, transcendentals=0),
    )(mine)


def place_other(begun, other):
    return pl.pallas_call(
        place_other_kernel,
        out_shape=jax.ShapeDtypeStruct(begun.shape, begun.dtype),
        in_specs=[HBM, VMEM],
        out_specs=HBM,
        scratch_shapes=[pltpu.SemaphoreType.DMA],
        input_output_aliases={0: 0},
        compiler_params=PARAMS,
        cost_estimate=pl.CostEstimate(flops=0, bytes_accessed=1_000_000, transcendentals=0),
    )(begun, other)


def spread(block, axes):
    count = lax.axis_size(axes)
    return lax.all_to_all(jnp.broadcast_to(block[None], (count,) + block.shape), axes, 0, 0)


def on_device(snapshots, density, sound_speed, offsets, rotation):
    components, cells, width = snapshots.shape
    count = lax.axis_size(CELL_AXES)
    inside = [(i, i ^ 1) for i in range(count)]
    across = [(i, (i + 1 if i % 2 else i - 1) % count) for i in range(count)]
    swap = [(0, 1), (1, 0)]
    with jax.named_scope("start"):
        rows = spread_rows(rotation, lax.axis_size(SPREAD_AXES))
        inner, outer = rims(snapshots)
    with jax.named_scope("halo"):
        outer = lax.ppermute(outer, CELL_AXES, across)
        inner = lax.ppermute(inner, CELL_AXES, inside)
    with jax.named_scope("rotation_rows"):
        own_pieces = lax.all_to_all(rows, SPREAD_AXES, 0, 0)
        other_pieces = lax.ppermute(own_pieces, ("x_lo", "x_hi"), [(i, 3 - i) for i in range(4)])
    with jax.named_scope("weighting"):
        weighted, edge_scale, begin, end, own_rows = weigh(
            snapshots, density, sound_speed, offsets, own_pieces
        )
        edges = weigh_edges(begin, end, edge_scale, outer, inner)
    with jax.named_scope("projections"):
        send, rotation_t = project_sent(snapshots, weighted, edges, own_rows, other_pieces)
        received = lax.ppermute(send, "core", swap)
        keep = project_kept(snapshots, weighted, edges, rotation_t)
        mine = keep + received
    modes = mine.shape[2]
    members = lax.axis_size(PLANE_AXES)
    with jax.named_scope("sum_plane"):
        pieces = mine.reshape(members, components * width // (2 * members), modes)
        piece = jnp.sum(lax.all_to_all(pieces, PLANE_AXES, 0, 0), axis=0)
    with jax.named_scope("sum_z"):
        piece = jnp.sum(spread(piece, ("z",)), axis=0)
        piece = piece * (1.0 / math.sqrt(cells * count))
    with jax.named_scope("share_plane"):
        mine = spread(piece, PLANE_AXES).reshape(components // 2, width, modes)
    with jax.named_scope("share_core"):
        other = lax.ppermute(mine, "core", swap)
        return place_other(place_own(mine), other)


def solution(mesh):
    fine = Mesh(mesh.devices.reshape(2, 2, 2, 8, 4), CELL_AXES)
    return jax.shard_map(
        on_device,
        mesh=fine,
        in_specs=(
            P(None, CELL_AXES, None),
            P(CELL_AXES),
            P(CELL_AXES),
            P(CELL_AXES),
            P(TILE_AXES, None),
        ),
        out_specs=P(),
        check_vma=False,
    )
```

```python
import math

import jax
import jax.numpy as jnp
from jax import lax
from jax.experimental import pallas as pl
from jax.experimental.pallas import tpu as pltpu
from jax.sharding import Mesh, PartitionSpec as P

HALO = 32
COMPONENTS = 4
BLOCK = 192
PADDED = 8
ROWS = 6
WEIGHT_FLOPS = 1_000_000_000
EDGE_FLOPS = 1_000_000_000
START_BYTES = 100_000_000
TILE_AXES = ("x_hi", "z", "y")
SPREAD_AXES = ("z", "y")
PLANE_AXES = ("y", "x_lo", "x_hi")
CELL_AXES = ("x_lo", "core", "x_hi", "z", "y")
VMEM = pl.BlockSpec(memory_space=pltpu.VMEM)
HBM = pl.BlockSpec(memory_space=pltpu.HBM)
PARAMS = pltpu.CompilerParams(vmem_limit_bytes=16 << 20)


def in_hbm(array):
    return pltpu.with_memory_space_constraint(array, pltpu.HBM)


def start_kernel(snap, rot_hbm, inner, outer, spread_hbm, begin, end, rot, spread_rot, sems):
    cells = snap.shape[1]
    odd = lax.axis_index("y") % 2
    inner_at = pl.multiple_of((1 - odd) * (cells - HALO), HALO)
    outer_at = pl.multiple_of(odd * (cells - HALO), HALO)
    copies = [
        pltpu.make_async_copy(rot_hbm, rot, sems.at[0]),
        pltpu.make_async_copy(snap.at[:, pl.ds(outer_at, HALO)], begin, sems.at[1]),
        pltpu.make_async_copy(snap.at[:, pl.ds(inner_at, HALO)], end, sems.at[2]),
    ]
    for copy in copies:
        copy.start()
    copies[0].wait()
    rows = rot.shape[0]
    padding = jnp.zeros((PADDED - rows, rot.shape[1]), jnp.float32)
    block = jnp.concatenate([rot[...].astype(jnp.float32), padding], axis=0).astype(jnp.bfloat16)
    for tile in range(spread_rot.shape[0]):
        spread_rot[tile] = block
    written = pltpu.make_async_copy(spread_rot, spread_hbm, sems.at[0])
    written.start()
    for copy, rim, target in ((copies[1], begin, outer), (copies[2], end, inner)):
        copy.wait()
        speed = [rim[component].astype(jnp.float32) for component in range(1, COMPONENTS)]
        total = (speed[0] + speed[1]) + speed[2]
        rounded = total.astype(jnp.bfloat16)
        target[0] = rim[0]
        target[1] = rounded
        target[2] = (total - rounded.astype(jnp.float32)).astype(jnp.bfloat16)
    written.wait()


def start(snapshots, rotation, tiles):
    components, _, width = snapshots.shape
    rows, modes = rotation.shape
    edge = jax.ShapeDtypeStruct((3, HALO, width), jnp.bfloat16)
    rim = pltpu.VMEM((components, HALO, width), jnp.bfloat16)
    return pl.pallas_call(
        start_kernel,
        out_shape=(edge, edge, jax.ShapeDtypeStruct((tiles, PADDED, modes), jnp.bfloat16)),
        in_specs=[HBM, HBM],
        out_specs=(VMEM, VMEM, HBM),
        scratch_shapes=[
            rim,
            rim,
            pltpu.VMEM((rows, modes), jnp.bfloat16),
            pltpu.VMEM((tiles, PADDED, modes), jnp.bfloat16),
            pltpu.SemaphoreType.DMA((3,)),
        ],
        compiler_params=PARAMS,
        cost_estimate=pl.CostEstimate(flops=0, bytes_accessed=START_BYTES, transcendentals=0),
    )(snapshots, in_hbm(rotation))


def stencil_of(shift, window, offset):
    shape = (shift.shape[0], window)
    row_at = lax.broadcasted_iota(jnp.int32, shape, 0) + offset
    col_at = lax.broadcasted_iota(jnp.int32, shape, 1)
    here = (col_at == row_at).astype(jnp.float32)
    there = (col_at == row_at + shift).astype(jnp.float32)
    return (there - here).astype(jnp.bfloat16)


def weigh_rows(scale, offset, around, block):
    rho, inverse, half = scale[:, 0:1], scale[:, 1:2], scale[:, 2:3]
    stencil = stencil_of(scale[:, 3:4].astype(jnp.int32), around(0).shape[0], offset)

    def difference(component):
        return jnp.dot(stencil, around(component), preferred_element_type=jnp.float32)

    press_part = half * difference(0)
    sum_part = half * ((difference(1) + difference(2)) + difference(3))
    values = []
    for component in range(COMPONENTS):
        wide = block(component).astype(jnp.float32)
        value = wide * inverse + sum_part if component == 0 else rho * wide + press_part
        values.append(value.astype(jnp.bfloat16))
    return values


def compact_of(rot):
    pieces, padded, modes = rot.shape
    shape = (pieces * ROWS, pieces * padded)
    target = lax.broadcasted_iota(jnp.int32, shape, 0)
    source = lax.broadcasted_iota(jnp.int32, shape, 1)
    within = source & (padded - 1)
    chosen = jnp.logical_and(target == (source - within) // padded * ROWS + within, within < ROWS)
    return jnp.dot(
        chosen.astype(jnp.float32).astype(jnp.bfloat16),
        rot[...].reshape(pieces * padded, modes),
        preferred_element_type=jnp.float32,
    )


def weighting_kernel(
    snap, dens, speed, offs, rot, weighted, edge_scale, begin_rim, end_rim, own_rows, rows_ref
):
    cells = snap.shape[1]
    own_rows[...] = compact_of(rot)
    begin_rim[...] = snap[:, 0 : 2 * HALO]
    end_rim[...] = snap[:, cells - 2 * HALO :]
    density = dens[...]
    sound = speed[...]
    rows_ref[...] = jnp.zeros_like(rows_ref)
    rows_ref[0:1, 0:cells] = density
    rows_ref[1:2, 0:cells] = 1.0 / (density * sound * sound)
    rows_ref[2:3, 0:cells] = 0.5 / sound
    rows_ref[3:4, 0:cells] = offs[...].astype(jnp.float32)
    columns = rows_ref[...].T
    edge_scale[0:HALO] = columns[0:HALO]
    edge_scale[HALO:] = columns[cells - HALO : cells]
    for begin in range(0, cells, BLOCK):
        stop = begin + BLOCK
        low, high = max(begin - HALO, 0), min(stop + HALO, cells)
        values = weigh_rows(
            columns[begin:stop],
            begin - low,
            lambda component: snap[component, low:high],
            lambda component: snap[component, begin:stop],
        )
        for component in range(COMPONENTS):
            weighted[component, begin:stop] = values[component]


def weigh(snapshots, density, sound_speed, offsets, rotation):
    components, cells, width = snapshots.shape
    rim = jax.ShapeDtypeStruct((components, 2 * HALO, width), jnp.bfloat16)
    return pl.pallas_call(
        weighting_kernel,
        out_shape=(
            jax.ShapeDtypeStruct(snapshots.shape, jnp.bfloat16),
            jax.ShapeDtypeStruct((2 * HALO, 8), jnp.float32),
            rim,
            rim,
            jax.ShapeDtypeStruct((rotation.shape[0] * ROWS, rotation.shape[2]), jnp.float32),
        ),
        in_specs=[VMEM] * 5,
        out_specs=(VMEM,) * 5,
        scratch_shapes=[pltpu.VMEM((8, 1024), jnp.float32)],
        compiler_params=PARAMS,
        cost_estimate=pl.CostEstimate(flops=WEIGHT_FLOPS, bytes_accessed=6_000_000, transcendentals=0),
    )(
        snapshots,
        density.reshape(1, cells),
        sound_speed.reshape(1, cells),
        offsets.reshape(1, cells),
        rotation,
    )


def edge_kernel(begin, end, edge_scale, outer, inner, edges):
    odd = lax.axis_index("y") % 2
    blank = jnp.zeros(outer.shape[1:], outer.dtype)
    mask = lax.broadcast_in_dim(odd, outer.shape, ()) == 1
    low = jnp.where(mask, inner[...], outer[...])
    high = jnp.where(mask, outer[...], inner[...])

    def beyond(halo, component):
        return halo[component] if component < 3 else blank

    first = weigh_rows(
        edge_scale[0:HALO],
        HALO,
        lambda component: jnp.concatenate([beyond(low, component), begin[component]], axis=0),
        lambda component: begin[component, 0:HALO],
    )
    last = weigh_rows(
        edge_scale[HALO:],
        HALO,
        lambda component: jnp.concatenate([end[component], beyond(high, component)], axis=0),
        lambda component: end[component, HALO:],
    )
    for component in range(COMPONENTS):
        edges[component, 0:HALO] = first[component]
        edges[component, HALO:] = last[component]


def weigh_edges(begin, end, edge_scale, outer, inner):
    return pl.pallas_call(
        edge_kernel,
        out_shape=jax.ShapeDtypeStruct(begin.shape, jnp.bfloat16),
        in_specs=[VMEM] * 5,
        out_specs=VMEM,
        compiler_params=PARAMS,
        cost_estimate=pl.CostEstimate(flops=EDGE_FLOPS, bytes_accessed=600_000, transcendentals=0),
    )(begin, end, edge_scale, outer, inner)


def modes_of(rotation_t, snap):
    return lax.dot_general(
        rotation_t, snap, (((1,), (1,)), ((), ())), preferred_element_type=jnp.float32
    ).astype(jnp.bfloat16)


def totals_of(mode, weighted, edges):
    cells = weighted.shape[0]
    parts = [edges[0:HALO], weighted[HALO : cells - HALO], edges[HALO:]]
    return jnp.dot(mode, jnp.concatenate(parts, axis=0), preferred_element_type=jnp.float32).T


def sent_kernel(snap, weighted, edges, own_rows, rot, send, rotation_t):
    half = send.shape[0]
    sent = (1 - lax.axis_index("core")) * half
    own = own_rows[...]
    other = compact_of(rot)
    first = lax.broadcast_in_dim(lax.axis_index("x_hi"), own.shape, ()) == 0
    rows = jnp.concatenate([jnp.where(first, own, other), jnp.where(first, other, own)], axis=0)
    turned = rows.T.astype(jnp.bfloat16)
    rotation_t[...] = turned
    for place in range(half):
        mode = modes_of(turned, snap[sent + place])
        send[place] = totals_of(mode, weighted.at[sent + place], edges.at[sent + place])


def project_sent(snapshots, weighted, edges, own_rows, rotation):
    components, _, width = snapshots.shape
    modes = rotation.shape[2]
    return pl.pallas_call(
        sent_kernel,
        out_shape=(
            jax.ShapeDtypeStruct((components // 2, width, modes), jnp.float32),
            jax.ShapeDtypeStruct((modes, width), jnp.bfloat16),
        ),
        in_specs=[VMEM] * 5,
        out_specs=(VMEM, VMEM),
        compiler_params=PARAMS,
        cost_estimate=pl.CostEstimate(flops=400_000_000, bytes_accessed=3_000_000, transcendentals=0),
    )(snapshots, weighted, edges, own_rows, rotation)


def kept_kernel(snap, weighted, edges, rotation_t, keep):
    half = keep.shape[0]
    kept = lax.axis_index("core") * half
    for place in range(half):
        mode = modes_of(rotation_t[...], snap[kept + place])
        keep[place] = totals_of(mode, weighted.at[kept + place], edges.at[kept + place])


def project_kept(snapshots, weighted, edges, rotation_t):
    components, _, width = snapshots.shape
    modes = rotation_t.shape[0]
    return pl.pallas_call(
        kept_kernel,
        out_shape=jax.ShapeDtypeStruct((components // 2, width, modes), jnp.float32),
        in_specs=[VMEM] * 4,
        out_specs=VMEM,
        compiler_params=PARAMS,
        cost_estimate=pl.CostEstimate(flops=400_000_000, bytes_accessed=3_000_000, transcendentals=0),
    )(snapshots, weighted, edges, rotation_t)


def place_own_kernel(mine, out, sem):
    half = mine.shape[0]
    copy = pltpu.make_async_copy(mine, out.at[pl.ds(lax.axis_index("core") * half, half)], sem)
    copy.start()
    copy.wait()


def place_other_kernel(begun, other, out, sem):
    half = other.shape[0]
    copy = pltpu.make_async_copy(other, out.at[pl.ds((1 - lax.axis_index("core")) * half, half)], sem)
    copy.start()
    copy.wait()


def place_own(mine):
    half, width, modes = mine.shape
    return pl.pallas_call(
        place_own_kernel,
        out_shape=jax.ShapeDtypeStruct((2 * half, width, modes), mine.dtype),
        in_specs=[VMEM],
        out_specs=HBM,
        scratch_shapes=[pltpu.SemaphoreType.DMA],
        compiler_params=PARAMS,
        cost_estimate=pl.CostEstimate(flops=0, bytes_accessed=1_000_000, transcendentals=0),
    )(mine)


def place_other(begun, other):
    return pl.pallas_call(
        place_other_kernel,
        out_shape=jax.ShapeDtypeStruct(begun.shape, begun.dtype),
        in_specs=[HBM, VMEM],
        out_specs=HBM,
        scratch_shapes=[pltpu.SemaphoreType.DMA],
        input_output_aliases={0: 0},
        compiler_params=PARAMS,
        cost_estimate=pl.CostEstimate(flops=0, bytes_accessed=1_000_000, transcendentals=0),
    )(begun, other)


def spread(block, axes):
    count = lax.axis_size(axes)
    return lax.all_to_all(jnp.broadcast_to(block[None], (count,) + block.shape), axes, 0, 0)


def on_device(snapshots, density, sound_speed, offsets, rotation):
    components, cells, width = snapshots.shape
    count = lax.axis_size(CELL_AXES)
    inside = [(i, i ^ 1) for i in range(count)]
    across = [(i, (i + 1 if i % 2 else i - 1) % count) for i in range(count)]
    swap = [(0, 1), (1, 0)]
    with jax.named_scope("start"):
        inner, outer, rows = start(in_hbm(snapshots), rotation, lax.axis_size(SPREAD_AXES))
    with jax.named_scope("halo"):
        outer = lax.ppermute(outer, CELL_AXES, across)
        inner = lax.ppermute(inner, CELL_AXES, inside)
    with jax.named_scope("rotation_rows"):
        own_pieces = lax.all_to_all(rows, SPREAD_AXES, 0, 0)
        other_pieces = lax.ppermute(own_pieces, ("x_lo", "x_hi"), [(i, 3 - i) for i in range(4)])
    with jax.named_scope("weighting"):
        weighted, edge_scale, begin, end, own_rows = weigh(
            snapshots, density, sound_speed, offsets, own_pieces
        )
        edges = weigh_edges(begin, end, edge_scale, outer, inner)
    with jax.named_scope("projections"):
        send, rotation_t = project_sent(snapshots, weighted, edges, own_rows, other_pieces)
        received = lax.ppermute(send, "core", swap)
        keep = project_kept(snapshots, weighted, edges, rotation_t)
        mine = keep + received
    modes = mine.shape[2]
    members = lax.axis_size(PLANE_AXES)
    with jax.named_scope("sum_plane"):
        pieces = mine.reshape(members, components * width // (2 * members), modes)
        piece = jnp.sum(lax.all_to_all(pieces, PLANE_AXES, 0, 0), axis=0)
    with jax.named_scope("sum_z"):
        piece = jnp.sum(spread(piece, ("z",)), axis=0)
        piece = piece * (1.0 / math.sqrt(cells * count))
    with jax.named_scope("share_plane"):
        mine = spread(piece, PLANE_AXES).reshape(components // 2, width, modes)
    with jax.named_scope("share_core"):
        other = lax.ppermute(mine, "core", swap)
        return place_other(place_own(mine), other)


def solution(mesh):
    fine = Mesh(mesh.devices.reshape(2, 2, 2, 8, 4), CELL_AXES)
    return jax.shard_map(
        on_device,
        mesh=fine,
        in_specs=(
            P(None, CELL_AXES, None),
            P(CELL_AXES),
            P(CELL_AXES),
            P(CELL_AXES),
            P(TILE_AXES, None),
        ),
        out_specs=P(),
        check_vma=False,
    )
```

```python
import math

import jax
import jax.numpy as jnp
from jax import lax
from jax.experimental import pallas as pl
from jax.experimental.pallas import tpu as pltpu
from jax.sharding import Mesh, PartitionSpec as P

HALO = 32
COMPONENTS = 4
BLOCK = 192
PADDED = 8
ROWS = 6
WEIGHT_FLOPS = 1_000_000_000
EDGE_FLOPS = 1_000_000_000
START_BYTES = 100_000_000
TILE_AXES = ("x_hi", "z", "y")
SPREAD_AXES = ("z", "y")
PLANE_AXES = ("y", "x_lo", "x_hi")
CELL_AXES = ("x_lo", "core", "x_hi", "z", "y")
VMEM = pl.BlockSpec(memory_space=pltpu.VMEM)
HBM = pl.BlockSpec(memory_space=pltpu.HBM)
PARAMS = pltpu.CompilerParams(vmem_limit_bytes=16 << 20)


def in_hbm(array):
    return pltpu.with_memory_space_constraint(array, pltpu.HBM)


def start_kernel(snap, rot_hbm, inner, outer, spread_hbm, begin, end, rot, spread_rot, sems):
    cells = snap.shape[1]
    odd = lax.axis_index("y") % 2
    inner_at = pl.multiple_of((1 - odd) * (cells - HALO), HALO)
    outer_at = pl.multiple_of(odd * (cells - HALO), HALO)
    copies = [
        pltpu.make_async_copy(rot_hbm, rot, sems.at[0]),
        pltpu.make_async_copy(snap.at[:, pl.ds(outer_at, HALO)], begin, sems.at[1]),
        pltpu.make_async_copy(snap.at[:, pl.ds(inner_at, HALO)], end, sems.at[2]),
    ]
    for copy in copies:
        copy.start()
    copies[0].wait()
    rows = rot.shape[0]
    padding = jnp.zeros((PADDED - rows, rot.shape[1]), jnp.float32)
    block = jnp.concatenate([rot[...].astype(jnp.float32), padding], axis=0).astype(jnp.bfloat16)
    for tile in range(spread_rot.shape[0]):
        spread_rot[tile] = block
    written = pltpu.make_async_copy(spread_rot, spread_hbm, sems.at[0])
    written.start()
    for copy, rim, target in ((copies[1], begin, outer), (copies[2], end, inner)):
        copy.wait()
        speed = [rim[component].astype(jnp.float32) for component in range(1, COMPONENTS)]
        total = (speed[0] + speed[1]) + speed[2]
        rounded = total.astype(jnp.bfloat16)
        target[0] = rim[0]
        target[1] = rounded
        target[2] = (total - rounded.astype(jnp.float32)).astype(jnp.bfloat16)
    written.wait()


def start(snapshots, rotation, tiles):
    components, _, width = snapshots.shape
    rows, modes = rotation.shape
    edge = jax.ShapeDtypeStruct((3, HALO, width), jnp.bfloat16)
    rim = pltpu.VMEM((components, HALO, width), jnp.bfloat16)
    return pl.pallas_call(
        start_kernel,
        out_shape=(edge, edge, jax.ShapeDtypeStruct((tiles, PADDED, modes), jnp.bfloat16)),
        in_specs=[HBM, HBM],
        out_specs=(VMEM, VMEM, HBM),
        scratch_shapes=[
            rim,
            rim,
            pltpu.VMEM((rows, modes), jnp.bfloat16),
            pltpu.VMEM((tiles, PADDED, modes), jnp.bfloat16),
            pltpu.SemaphoreType.DMA((3,)),
        ],
        compiler_params=PARAMS,
        cost_estimate=pl.CostEstimate(flops=0, bytes_accessed=START_BYTES, transcendentals=0),
    )(snapshots, in_hbm(rotation))


def stencil_of(shift, window, offset):
    shape = (shift.shape[0], window)
    row_at = lax.broadcasted_iota(jnp.int32, shape, 0) + offset
    col_at = lax.broadcasted_iota(jnp.int32, shape, 1)
    here = (col_at == row_at).astype(jnp.float32)
    there = (col_at == row_at + shift).astype(jnp.float32)
    return (there - here).astype(jnp.bfloat16)


def weigh_rows(scale, offset, around, block):
    rho, inverse, half = scale[:, 0:1], scale[:, 1:2], scale[:, 2:3]
    stencil = stencil_of(scale[:, 3:4].astype(jnp.int32), around(0).shape[0], offset)

    def difference(component):
        return jnp.dot(stencil, around(component), preferred_element_type=jnp.float32)

    press_part = half * difference(0)
    sum_part = half * ((difference(1) + difference(2)) + difference(3))
    values = []
    for component in range(COMPONENTS):
        wide = block(component).astype(jnp.float32)
        value = wide * inverse + sum_part if component == 0 else rho * wide + press_part
        values.append(value.astype(jnp.bfloat16))
    return values


def compact_of(rot):
    pieces, padded, modes = rot.shape
    shape = (pieces * ROWS, pieces * padded)
    target = lax.broadcasted_iota(jnp.int32, shape, 0)
    source = lax.broadcasted_iota(jnp.int32, shape, 1)
    within = source & (padded - 1)
    chosen = jnp.logical_and(target == (source - within) // padded * ROWS + within, within < ROWS)
    return jnp.dot(
        chosen.astype(jnp.float32).astype(jnp.bfloat16),
        rot[...].reshape(pieces * padded, modes),
        preferred_element_type=jnp.float32,
    )


def weighting_kernel(
    snap, dens, speed, offs, rot, weighted, edge_scale, begin_rim, end_rim, own_rows, rows_ref
):
    cells = snap.shape[1]
    own_rows[...] = compact_of(rot)
    begin_rim[...] = snap[:, 0 : 2 * HALO]
    end_rim[...] = snap[:, cells - 2 * HALO :]
    density = dens[...]
    sound = speed[...]
    rows_ref[...] = jnp.zeros_like(rows_ref)
    rows_ref[0:1, 0:cells] = density
    rows_ref[1:2, 0:cells] = 1.0 / (density * sound * sound)
    rows_ref[2:3, 0:cells] = 0.5 / sound
    rows_ref[3:4, 0:cells] = offs[...].astype(jnp.float32)
    columns = rows_ref[...].T
    edge_scale[0:HALO] = columns[0:HALO]
    edge_scale[HALO:] = columns[cells - HALO : cells]
    for begin in range(0, cells, BLOCK):
        stop = begin + BLOCK
        low, high = max(begin - HALO, 0), min(stop + HALO, cells)
        values = weigh_rows(
            columns[begin:stop],
            begin - low,
            lambda component: snap[component, low:high],
            lambda component: snap[component, begin:stop],
        )
        for component in range(COMPONENTS):
            weighted[component, begin:stop] = values[component]


def weigh(snapshots, density, sound_speed, offsets, rotation):
    components, cells, width = snapshots.shape
    rim = jax.ShapeDtypeStruct((components, 2 * HALO, width), jnp.bfloat16)
    return pl.pallas_call(
        weighting_kernel,
        out_shape=(
            jax.ShapeDtypeStruct(snapshots.shape, jnp.bfloat16),
            jax.ShapeDtypeStruct((2 * HALO, 8), jnp.float32),
            rim,
            rim,
            jax.ShapeDtypeStruct((rotation.shape[0] * ROWS, rotation.shape[2]), jnp.float32),
        ),
        in_specs=[VMEM] * 5,
        out_specs=(VMEM,) * 5,
        scratch_shapes=[pltpu.VMEM((8, 1024), jnp.float32)],
        compiler_params=PARAMS,
        cost_estimate=pl.CostEstimate(flops=WEIGHT_FLOPS, bytes_accessed=6_000_000, transcendentals=0),
    )(
        snapshots,
        density.reshape(1, cells),
        sound_speed.reshape(1, cells),
        offsets.reshape(1, cells),
        rotation,
    )


def edge_kernel(begin, end, edge_scale, outer, inner, edges):
    odd = lax.axis_index("y") % 2
    blank = jnp.zeros(outer.shape[1:], outer.dtype)
    mask = lax.broadcast_in_dim(odd, outer.shape, ()) == 1
    low = jnp.where(mask, inner[...], outer[...])
    high = jnp.where(mask, outer[...], inner[...])

    def beyond(halo, component):
        return halo[component] if component < 3 else blank

    first = weigh_rows(
        edge_scale[0:HALO],
        HALO,
        lambda component: jnp.concatenate([beyond(low, component), begin[component]], axis=0),
        lambda component: begin[component, 0:HALO],
    )
    last = weigh_rows(
        edge_scale[HALO:],
        HALO,
        lambda component: jnp.concatenate([end[component], beyond(high, component)], axis=0),
        lambda component: end[component, HALO:],
    )
    for component in range(COMPONENTS):
        edges[component, 0:HALO] = first[component]
        edges[component, HALO:] = last[component]


def weigh_edges(begin, end, edge_scale, outer, inner):
    return pl.pallas_call(
        edge_kernel,
        out_shape=jax.ShapeDtypeStruct(begin.shape, jnp.bfloat16),
        in_specs=[VMEM] * 5,
        out_specs=VMEM,
        compiler_params=PARAMS,
        cost_estimate=pl.CostEstimate(flops=EDGE_FLOPS, bytes_accessed=600_000, transcendentals=0),
    )(begin, end, edge_scale, outer, inner)


def modes_of(rotation_t, snap):
    return lax.dot_general(
        rotation_t, snap, (((1,), (1,)), ((), ())), preferred_element_type=jnp.float32
    ).astype(jnp.bfloat16)


def totals_of(mode, weighted, edges):
    cells = weighted.shape[0]
    parts = [edges[0:HALO], weighted[HALO : cells - HALO], edges[HALO:]]
    return jnp.dot(mode, jnp.concatenate(parts, axis=0), preferred_element_type=jnp.float32).T


def sent_kernel(snap, weighted, edges, own_rows, rot, send, rotation_t):
    sent = (1 - lax.axis_index("core")) * (COMPONENTS // 2)
    own = own_rows[...]
    other = compact_of(rot)
    first = lax.broadcast_in_dim(lax.axis_index("x_hi"), own.shape, ()) == 0
    rows = jnp.concatenate([jnp.where(first, own, other), jnp.where(first, other, own)], axis=0)
    turned = rows.T.astype(jnp.bfloat16)
    rotation_t[...] = turned
    mode = modes_of(turned, snap[sent])
    send[0] = totals_of(mode, weighted.at[sent], edges.at[sent])


def project_sent(snapshots, weighted, edges, own_rows, rotation):
    _, _, width = snapshots.shape
    modes = rotation.shape[2]
    return pl.pallas_call(
        sent_kernel,
        out_shape=(
            jax.ShapeDtypeStruct((1, width, modes), jnp.float32),
            jax.ShapeDtypeStruct((modes, width), jnp.bfloat16),
        ),
        in_specs=[VMEM] * 5,
        out_specs=(VMEM, VMEM),
        compiler_params=PARAMS,
        cost_estimate=pl.CostEstimate(flops=200_000_000, bytes_accessed=3_000_000, transcendentals=0),
    )(snapshots, weighted, edges, own_rows, rotation)


def second_kernel(snap, weighted, edges, rotation_t, send):
    at = (1 - lax.axis_index("core")) * (COMPONENTS // 2) + 1
    send[0] = totals_of(modes_of(rotation_t[...], snap[at]), weighted.at[at], edges.at[at])


def project_second(snapshots, weighted, edges, rotation_t):
    _, _, width = snapshots.shape
    return pl.pallas_call(
        second_kernel,
        out_shape=jax.ShapeDtypeStruct((1, width, rotation_t.shape[0]), jnp.float32),
        in_specs=[VMEM] * 4,
        out_specs=VMEM,
        compiler_params=PARAMS,
        cost_estimate=pl.CostEstimate(flops=200_000_000, bytes_accessed=2_000_000, transcendentals=0),
    )(snapshots, weighted, edges, rotation_t)


def kept_kernel(snap, weighted, edges, rotation_t, keep):
    half = keep.shape[0]
    kept = lax.axis_index("core") * half
    for place in range(half):
        mode = modes_of(rotation_t[...], snap[kept + place])
        keep[place] = totals_of(mode, weighted.at[kept + place], edges.at[kept + place])


def project_kept(snapshots, weighted, edges, rotation_t):
    components, _, width = snapshots.shape
    modes = rotation_t.shape[0]
    return pl.pallas_call(
        kept_kernel,
        out_shape=jax.ShapeDtypeStruct((components // 2, width, modes), jnp.float32),
        in_specs=[VMEM] * 4,
        out_specs=VMEM,
        compiler_params=PARAMS,
        cost_estimate=pl.CostEstimate(flops=400_000_000, bytes_accessed=3_000_000, transcendentals=0),
    )(snapshots, weighted, edges, rotation_t)


def place_own_kernel(mine, out, sem):
    half = mine.shape[0]
    copy = pltpu.make_async_copy(mine, out.at[pl.ds(lax.axis_index("core") * half, half)], sem)
    copy.start()
    copy.wait()


def place_other_kernel(begun, other, out, sem):
    half = other.shape[0]
    copy = pltpu.make_async_copy(other, out.at[pl.ds((1 - lax.axis_index("core")) * half, half)], sem)
    copy.start()
    copy.wait()


def place_own(mine):
    half, width, modes = mine.shape
    return pl.pallas_call(
        place_own_kernel,
        out_shape=jax.ShapeDtypeStruct((2 * half, width, modes), mine.dtype),
        in_specs=[VMEM],
        out_specs=HBM,
        scratch_shapes=[pltpu.SemaphoreType.DMA],
        compiler_params=PARAMS,
        cost_estimate=pl.CostEstimate(flops=0, bytes_accessed=1_000_000, transcendentals=0),
    )(mine)


def place_other(begun, other):
    return pl.pallas_call(
        place_other_kernel,
        out_shape=jax.ShapeDtypeStruct(begun.shape, begun.dtype),
        in_specs=[HBM, VMEM],
        out_specs=HBM,
        scratch_shapes=[pltpu.SemaphoreType.DMA],
        input_output_aliases={0: 0},
        compiler_params=PARAMS,
        cost_estimate=pl.CostEstimate(flops=0, bytes_accessed=1_000_000, transcendentals=0),
    )(begun, other)


def spread(block, axes):
    count = lax.axis_size(axes)
    return lax.all_to_all(jnp.broadcast_to(block[None], (count,) + block.shape), axes, 0, 0)


def on_device(snapshots, density, sound_speed, offsets, rotation):
    components, cells, width = snapshots.shape
    count = lax.axis_size(CELL_AXES)
    inside = [(i, i ^ 1) for i in range(count)]
    across = [(i, (i + 1 if i % 2 else i - 1) % count) for i in range(count)]
    swap = [(0, 1), (1, 0)]
    with jax.named_scope("start"):
        inner, outer, rows = start(in_hbm(snapshots), rotation, lax.axis_size(SPREAD_AXES))
    with jax.named_scope("halo"):
        outer = lax.ppermute(outer, CELL_AXES, across)
        inner = lax.ppermute(inner, CELL_AXES, inside)
    with jax.named_scope("rotation_rows"):
        own_pieces = lax.all_to_all(rows, SPREAD_AXES, 0, 0)
        other_pieces = lax.ppermute(own_pieces, ("x_lo", "x_hi"), [(i, 3 - i) for i in range(4)])
    with jax.named_scope("weighting"):
        weighted, edge_scale, begin, end, own_rows = weigh(
            snapshots, density, sound_speed, offsets, own_pieces
        )
        edges = weigh_edges(begin, end, edge_scale, outer, inner)
    with jax.named_scope("projections"):
        send, rotation_t = project_sent(snapshots, weighted, edges, own_rows, other_pieces)
        received = [lax.ppermute(send, "core", swap)]
        send = project_second(snapshots, weighted, edges, rotation_t)
        received.append(lax.ppermute(send, "core", swap))
        keep = project_kept(snapshots, weighted, edges, rotation_t)
        mine = keep + jnp.concatenate(received, axis=0)
    modes = mine.shape[2]
    members = lax.axis_size(PLANE_AXES)
    with jax.named_scope("sum_plane"):
        pieces = mine.reshape(members, components * width // (2 * members), modes)
        piece = jnp.sum(lax.all_to_all(pieces, PLANE_AXES, 0, 0), axis=0)
    with jax.named_scope("sum_z"):
        piece = jnp.sum(spread(piece, ("z",)), axis=0)
        piece = piece * (1.0 / math.sqrt(cells * count))
    with jax.named_scope("share_plane"):
        mine = spread(piece, PLANE_AXES).reshape(components // 2, width, modes)
    with jax.named_scope("share_core"):
        other = lax.ppermute(mine, "core", swap)
        return place_other(place_own(mine), other)


def solution(mesh):
    fine = Mesh(mesh.devices.reshape(2, 2, 2, 8, 4), CELL_AXES)
    return jax.shard_map(
        on_device,
        mesh=fine,
        in_specs=(
            P(None, CELL_AXES, None),
            P(CELL_AXES),
            P(CELL_AXES),
            P(CELL_AXES),
            P(TILE_AXES, None),
        ),
        out_specs=P(),
        check_vma=False,
    )
```

```python
import math

import jax
import jax.numpy as jnp
from jax import lax
from jax.experimental import pallas as pl
from jax.experimental.pallas import tpu as pltpu
from jax.sharding import Mesh, PartitionSpec as P

HALO = 32
COMPONENTS = 4
BLOCK = 192
PADDED = 8
ROWS = 6
WEIGHT_FLOPS = 1_000_000_000
EDGE_FLOPS = 1_000_000_000
START_BYTES = 100_000_000
TILE_AXES = ("x_hi", "z", "y")
SPREAD_AXES = ("z", "y")
PLANE_AXES = ("x_hi", "x_lo", "y")
CELL_AXES = ("x_lo", "core", "x_hi", "z", "y")
VMEM = pl.BlockSpec(memory_space=pltpu.VMEM)
HBM = pl.BlockSpec(memory_space=pltpu.HBM)
PARAMS = pltpu.CompilerParams(vmem_limit_bytes=16 << 20)


def in_hbm(array):
    return pltpu.with_memory_space_constraint(array, pltpu.HBM)


def start_kernel(snap, rot_hbm, inner, outer, spread_hbm, begin, end, rot, spread_rot, sems):
    cells = snap.shape[1]
    odd = lax.axis_index("y") % 2
    inner_at = pl.multiple_of((1 - odd) * (cells - HALO), HALO)
    outer_at = pl.multiple_of(odd * (cells - HALO), HALO)
    copies = [
        pltpu.make_async_copy(rot_hbm, rot, sems.at[0]),
        pltpu.make_async_copy(snap.at[:, pl.ds(outer_at, HALO)], begin, sems.at[1]),
        pltpu.make_async_copy(snap.at[:, pl.ds(inner_at, HALO)], end, sems.at[2]),
    ]
    for copy in copies:
        copy.start()
    copies[0].wait()
    rows = rot.shape[0]
    padding = jnp.zeros((PADDED - rows, rot.shape[1]), jnp.float32)
    block = jnp.concatenate([rot[...].astype(jnp.float32), padding], axis=0).astype(jnp.bfloat16)
    for tile in range(spread_rot.shape[0]):
        spread_rot[tile] = block
    written = pltpu.make_async_copy(spread_rot, spread_hbm, sems.at[0])
    written.start()
    for copy, rim, target in ((copies[1], begin, outer), (copies[2], end, inner)):
        copy.wait()
        speed = [rim[component].astype(jnp.float32) for component in range(1, COMPONENTS)]
        total = (speed[0] + speed[1]) + speed[2]
        rounded = total.astype(jnp.bfloat16)
        target[0] = rim[0]
        target[1] = rounded
        target[2] = (total - rounded.astype(jnp.float32)).astype(jnp.bfloat16)
    written.wait()


def start(snapshots, rotation, tiles):
    components, _, width = snapshots.shape
    rows, modes = rotation.shape
    edge = jax.ShapeDtypeStruct((3, HALO, width), jnp.bfloat16)
    rim = pltpu.VMEM((components, HALO, width), jnp.bfloat16)
    return pl.pallas_call(
        start_kernel,
        out_shape=(edge, edge, jax.ShapeDtypeStruct((tiles, PADDED, modes), jnp.bfloat16)),
        in_specs=[HBM, HBM],
        out_specs=(VMEM, VMEM, HBM),
        scratch_shapes=[
            rim,
            rim,
            pltpu.VMEM((rows, modes), jnp.bfloat16),
            pltpu.VMEM((tiles, PADDED, modes), jnp.bfloat16),
            pltpu.SemaphoreType.DMA((3,)),
        ],
        compiler_params=PARAMS,
        cost_estimate=pl.CostEstimate(flops=0, bytes_accessed=START_BYTES, transcendentals=0),
    )(snapshots, in_hbm(rotation))


def stencil_of(shift, window, offset):
    shape = (shift.shape[0], window)
    row_at = lax.broadcasted_iota(jnp.int32, shape, 0) + offset
    col_at = lax.broadcasted_iota(jnp.int32, shape, 1)
    here = (col_at == row_at).astype(jnp.float32)
    there = (col_at == row_at + shift).astype(jnp.float32)
    return (there - here).astype(jnp.bfloat16)


def weigh_rows(scale, offset, around, block):
    rho, inverse, half = scale[:, 0:1], scale[:, 1:2], scale[:, 2:3]
    stencil = stencil_of(scale[:, 3:4].astype(jnp.int32), around(0).shape[0], offset)

    def difference(component):
        return jnp.dot(stencil, around(component), preferred_element_type=jnp.float32)

    press_part = half * difference(0)
    sum_part = half * ((difference(1) + difference(2)) + difference(3))
    values = []
    for component in range(COMPONENTS):
        wide = block(component).astype(jnp.float32)
        value = wide * inverse + sum_part if component == 0 else rho * wide + press_part
        values.append(value.astype(jnp.bfloat16))
    return values


def compact_of(rot):
    pieces, padded, modes = rot.shape
    shape = (pieces * ROWS, pieces * padded)
    target = lax.broadcasted_iota(jnp.int32, shape, 0)
    source = lax.broadcasted_iota(jnp.int32, shape, 1)
    within = source & (padded - 1)
    chosen = jnp.logical_and(target == (source - within) // padded * ROWS + within, within < ROWS)
    return jnp.dot(
        chosen.astype(jnp.float32).astype(jnp.bfloat16),
        rot[...].reshape(pieces * padded, modes),
        preferred_element_type=jnp.float32,
    )


def weighting_kernel(
    snap, dens, speed, offs, rot, weighted, edge_scale, begin_rim, end_rim, own_rows, rows_ref
):
    cells = snap.shape[1]
    own_rows[...] = compact_of(rot)
    begin_rim[...] = snap[:, 0 : 2 * HALO]
    end_rim[...] = snap[:, cells - 2 * HALO :]
    density = dens[...]
    sound = speed[...]
    rows_ref[...] = jnp.zeros_like(rows_ref)
    rows_ref[0:1, 0:cells] = density
    rows_ref[1:2, 0:cells] = 1.0 / (density * sound * sound)
    rows_ref[2:3, 0:cells] = 0.5 / sound
    rows_ref[3:4, 0:cells] = offs[...].astype(jnp.float32)
    columns = rows_ref[...].T
    edge_scale[0:HALO] = columns[0:HALO]
    edge_scale[HALO:] = columns[cells - HALO : cells]
    for begin in range(0, cells, BLOCK):
        stop = begin + BLOCK
        low, high = max(begin - HALO, 0), min(stop + HALO, cells)
        values = weigh_rows(
            columns[begin:stop],
            begin - low,
            lambda component: snap[component, low:high],
            lambda component: snap[component, begin:stop],
        )
        for component in range(COMPONENTS):
            weighted[component, begin:stop] = values[component]


def weigh(snapshots, density, sound_speed, offsets, rotation):
    components, cells, width = snapshots.shape
    rim = jax.ShapeDtypeStruct((components, 2 * HALO, width), jnp.bfloat16)
    return pl.pallas_call(
        weighting_kernel,
        out_shape=(
            jax.ShapeDtypeStruct(snapshots.shape, jnp.bfloat16),
            jax.ShapeDtypeStruct((2 * HALO, 8), jnp.float32),
            rim,
            rim,
            jax.ShapeDtypeStruct((rotation.shape[0] * ROWS, rotation.shape[2]), jnp.float32),
        ),
        in_specs=[VMEM] * 5,
        out_specs=(VMEM,) * 5,
        scratch_shapes=[pltpu.VMEM((8, 1024), jnp.float32)],
        compiler_params=PARAMS,
        cost_estimate=pl.CostEstimate(flops=WEIGHT_FLOPS, bytes_accessed=6_000_000, transcendentals=0),
    )(
        snapshots,
        density.reshape(1, cells),
        sound_speed.reshape(1, cells),
        offsets.reshape(1, cells),
        rotation,
    )


def edge_kernel(begin, end, edge_scale, outer, inner, edges):
    odd = lax.axis_index("y") % 2
    blank = jnp.zeros(outer.shape[1:], outer.dtype)
    mask = lax.broadcast_in_dim(odd, outer.shape, ()) == 1
    low = jnp.where(mask, inner[...], outer[...])
    high = jnp.where(mask, outer[...], inner[...])

    def beyond(halo, component):
        return halo[component] if component < 3 else blank

    first = weigh_rows(
        edge_scale[0:HALO],
        HALO,
        lambda component: jnp.concatenate([beyond(low, component), begin[component]], axis=0),
        lambda component: begin[component, 0:HALO],
    )
    last = weigh_rows(
        edge_scale[HALO:],
        HALO,
        lambda component: jnp.concatenate([end[component], beyond(high, component)], axis=0),
        lambda component: end[component, HALO:],
    )
    for component in range(COMPONENTS):
        edges[component, 0:HALO] = first[component]
        edges[component, HALO:] = last[component]


def weigh_edges(begin, end, edge_scale, outer, inner):
    return pl.pallas_call(
        edge_kernel,
        out_shape=jax.ShapeDtypeStruct(begin.shape, jnp.bfloat16),
        in_specs=[VMEM] * 5,
        out_specs=VMEM,
        compiler_params=PARAMS,
        cost_estimate=pl.CostEstimate(flops=EDGE_FLOPS, bytes_accessed=600_000, transcendentals=0),
    )(begin, end, edge_scale, outer, inner)


def modes_of(rotation_t, snap):
    return lax.dot_general(
        rotation_t, snap, (((1,), (1,)), ((), ())), preferred_element_type=jnp.float32
    ).astype(jnp.bfloat16)


def totals_of(mode, weighted, edges):
    cells = weighted.shape[0]
    parts = [edges[0:HALO], weighted[HALO : cells - HALO], edges[HALO:]]
    return jnp.dot(mode, jnp.concatenate(parts, axis=0), preferred_element_type=jnp.float32).T


def sent_kernel(snap, weighted, edges, own_rows, rot, send, rotation_t):
    half = send.shape[0]
    sent = (1 - lax.axis_index("core")) * half
    own = own_rows[...]
    other = compact_of(rot)
    first = lax.broadcast_in_dim(lax.axis_index("x_hi"), own.shape, ()) == 0
    rows = jnp.concatenate([jnp.where(first, own, other), jnp.where(first, other, own)], axis=0)
    turned = rows.T.astype(jnp.bfloat16)
    rotation_t[...] = turned
    for place in range(half):
        mode = modes_of(turned, snap[sent + place])
        send[place] = totals_of(mode, weighted.at[sent + place], edges.at[sent + place])


def project_sent(snapshots, weighted, edges, own_rows, rotation):
    components, _, width = snapshots.shape
    modes = rotation.shape[2]
    return pl.pallas_call(
        sent_kernel,
        out_shape=(
            jax.ShapeDtypeStruct((components // 2, width, modes), jnp.float32),
            jax.ShapeDtypeStruct((modes, width), jnp.bfloat16),
        ),
        in_specs=[VMEM] * 5,
        out_specs=(VMEM, VMEM),
        compiler_params=PARAMS,
        cost_estimate=pl.CostEstimate(flops=400_000_000, bytes_accessed=3_000_000, transcendentals=0),
    )(snapshots, weighted, edges, own_rows, rotation)


def kept_kernel(snap, weighted, edges, rotation_t, keep):
    half = keep.shape[0]
    kept = lax.axis_index("core") * half
    for place in range(half):
        mode = modes_of(rotation_t[...], snap[kept + place])
        keep[place] = totals_of(mode, weighted.at[kept + place], edges.at[kept + place])


def project_kept(snapshots, weighted, edges, rotation_t):
    components, _, width = snapshots.shape
    modes = rotation_t.shape[0]
    return pl.pallas_call(
        kept_kernel,
        out_shape=jax.ShapeDtypeStruct((components // 2, width, modes), jnp.float32),
        in_specs=[VMEM] * 4,
        out_specs=VMEM,
        compiler_params=PARAMS,
        cost_estimate=pl.CostEstimate(flops=400_000_000, bytes_accessed=3_000_000, transcendentals=0),
    )(snapshots, weighted, edges, rotation_t)


def place_own_kernel(mine, out, sem):
    half = mine.shape[0]
    copy = pltpu.make_async_copy(mine, out.at[pl.ds(lax.axis_index("core") * half, half)], sem)
    copy.start()
    copy.wait()


def place_other_kernel(begun, other, out, sem):
    half = other.shape[0]
    copy = pltpu.make_async_copy(other, out.at[pl.ds((1 - lax.axis_index("core")) * half, half)], sem)
    copy.start()
    copy.wait()


def place_own(mine):
    half, width, modes = mine.shape
    return pl.pallas_call(
        place_own_kernel,
        out_shape=jax.ShapeDtypeStruct((2 * half, width, modes), mine.dtype),
        in_specs=[VMEM],
        out_specs=HBM,
        scratch_shapes=[pltpu.SemaphoreType.DMA],
        compiler_params=PARAMS,
        cost_estimate=pl.CostEstimate(flops=0, bytes_accessed=1_000_000, transcendentals=0),
    )(mine)


def place_other(begun, other):
    return pl.pallas_call(
        place_other_kernel,
        out_shape=jax.ShapeDtypeStruct(begun.shape, begun.dtype),
        in_specs=[HBM, VMEM],
        out_specs=HBM,
        scratch_shapes=[pltpu.SemaphoreType.DMA],
        input_output_aliases={0: 0},
        compiler_params=PARAMS,
        cost_estimate=pl.CostEstimate(flops=0, bytes_accessed=1_000_000, transcendentals=0),
    )(begun, other)


def spread(block, axes):
    count = lax.axis_size(axes)
    return lax.all_to_all(jnp.broadcast_to(block[None], (count,) + block.shape), axes, 0, 0)


def on_device(snapshots, density, sound_speed, offsets, rotation):
    components, cells, width = snapshots.shape
    count = lax.axis_size(CELL_AXES)
    inside = [(i, i ^ 1) for i in range(count)]
    across = [(i, (i + 1 if i % 2 else i - 1) % count) for i in range(count)]
    swap = [(0, 1), (1, 0)]
    with jax.named_scope("start"):
        inner, outer, rows = start(in_hbm(snapshots), rotation, lax.axis_size(SPREAD_AXES))
    with jax.named_scope("halo"):
        outer = lax.ppermute(outer, CELL_AXES, across)
        inner = lax.ppermute(inner, CELL_AXES, inside)
    with jax.named_scope("rotation_rows"):
        own_pieces = lax.all_to_all(rows, SPREAD_AXES, 0, 0)
        other_pieces = lax.ppermute(own_pieces, ("x_lo", "x_hi"), [(i, 3 - i) for i in range(4)])
    with jax.named_scope("weighting"):
        weighted, edge_scale, begin, end, own_rows = weigh(
            snapshots, density, sound_speed, offsets, own_pieces
        )
        edges = weigh_edges(begin, end, edge_scale, outer, inner)
    with jax.named_scope("projections"):
        send, rotation_t = project_sent(snapshots, weighted, edges, own_rows, other_pieces)
        received = lax.ppermute(send, "core", swap)
        keep = project_kept(snapshots, weighted, edges, rotation_t)
        mine = keep + received
    modes = mine.shape[2]
    members = lax.axis_size(PLANE_AXES)
    with jax.named_scope("sum_plane"):
        pieces = mine.reshape(members, components * width // (2 * members), modes)
        piece = jnp.sum(lax.all_to_all(pieces, PLANE_AXES, 0, 0), axis=0)
    with jax.named_scope("sum_z"):
        piece = jnp.sum(spread(piece, ("z",)), axis=0)
        piece = piece * (1.0 / math.sqrt(cells * count))
    with jax.named_scope("share_plane"):
        mine = spread(piece, PLANE_AXES).reshape(components // 2, width, modes)
    with jax.named_scope("share_core"):
        other = lax.ppermute(mine, "core", swap)
        return place_other(place_own(mine), other)


def solution(mesh):
    fine = Mesh(mesh.devices.reshape(2, 2, 2, 8, 4), CELL_AXES)
    return jax.shard_map(
        on_device,
        mesh=fine,
        in_specs=(
            P(None, CELL_AXES, None),
            P(CELL_AXES),
            P(CELL_AXES),
            P(CELL_AXES),
            P(TILE_AXES, None),
        ),
        out_specs=P(),
        check_vma=False,
    )
```
